128 devices in a mesh: gx: 4 (over y_lo, core), gy: 4 (over x), gz: 8 (over y_hi, z).
Axes of the slice: x: 4, y: 4 (y_hi: 2, y_lo: 2; y = y_hi * 2 + y_lo), z: 4, core: 2. Of those that a mesh axis runs over, the one named last changes fastest.
Arguments:
- positions: float32 [3, 8, 12, 16, 128], P(None, 'gx', 'gy', 'gz'), may hold values from 0 to 10
- atom_kinds: int32 [8, 12, 16, 128], P('gx', 'gy', 'gz'), may hold values from 0 to 2, as said below
- bond_partners: int32 [4, 8, 12, 16, 128], P(None, 'gx', 'gy', 'gz'), may hold values from -1 to 3455, as said below
- torsion_bonds: int32 [2, 4, 8, 12, 16, 128], P(None, None, 'gx', 'gy', 'gz'), may hold values from 0 to 3, as said below
- torsion_far: int32 [4, 8, 12, 16, 128], P(None, 'gx', 'gy', 'gz'), may hold values from -1 to 3455, as said below
Outputs:
- charges: float32 [8, 12, 16, 128], P('gx', 'gy', 'gz')
- orders: float32 [4, 8, 12, 16, 128], P(None, 'gx', 'gy', 'gz')
- bond_forces: float32 [3, 4, 8, 12, 16, 128], P(None, None, 'gx', 'gy', 'gz')
- far_forces: float32 [3, 4, 8, 12, 16, 128], P(None, None, 'gx', 'gy', 'gz')
The draws below stay inside these ranges and needn't reach their ends.
Inputs may be any that keep to these rules, and one draw needn't show every extreme that they name: `atom_kinds`: atoms of a cell are stored in groups of eight headed by a silicon atom: atom a is silicon exactly when a % 8 == 0, every other atom is oxygen or hydrogen. `bond_partners`: -1 marks an empty slot; the neighbourhood index is o * 128 + atom with the step code o of the steps. `torsion_bonds`: the two slots of a torsion differ. `torsion_far`: -1 marks an empty torsion slot; otherwise a neighbourhood index as for bond_partners.
All inputs are finite; a program needn't handle non-finite values.
Results may differ from the reference program's by a relative error of at most 0.0003.
Values sent between devices are 32-bit elements; how exact they have to be, the bound alone decides.
A program may use at most 64 MiB of HBM per device.

```python
import jax
import jax.numpy as jnp
from jax import lax

ATOMS = 128
NBOND = 4
NTOR = 4
ITERS = 3
CX = 2
CY = 3
CZ = 2
NX = 8
NY = 12
NZ = 16


def draw_atom_kinds(key, part):
    full_shape = (NX, NY, NZ, ATOMS)
    other_kind = jax.random.randint(jax.random.fold_in(key, 5), full_shape, 1, 3)
    atom_index = jnp.arange(ATOMS, dtype=jnp.int32)
    return jnp.where(atom_index % 8 == 0, 0, other_kind).astype(jnp.int32)


def draw_bond_partners(key, part):
    first_key, second_key = jax.random.split(jax.random.fold_in(key, 11))
    full_shape = (NBOND, NX, NY, NZ, ATOMS)
    partner_index = jax.random.randint(first_key, full_shape, 0, 27 * ATOMS)
    empty_slot = jax.random.randint(second_key, full_shape, 0, 4) == 0
    return jnp.where(empty_slot, -1, partner_index).astype(jnp.int32)


def draw_torsion_bonds(key, part):
    first_key, second_key = jax.random.split(jax.random.fold_in(key, 23))
    full_shape = (NTOR, NX, NY, NZ, ATOMS)
    first_slot = jax.random.randint(first_key, full_shape, 0, NBOND)
    slot_gap = jax.random.randint(second_key, full_shape, 1, NBOND)
    second_slot = (first_slot + slot_gap) % NBOND
    return jnp.stack([first_slot, second_slot]).astype(jnp.int32)


def draw_torsion_far(key, part):
    first_key, second_key = jax.random.split(jax.random.fold_in(key, 37))
    full_shape = (NTOR, NX, NY, NZ, ATOMS)
    far_index = jax.random.randint(first_key, full_shape, 0, 27 * ATOMS)
    empty_slot = jax.random.randint(second_key, full_shape, 0, 4) == 0
    return jnp.where(empty_slot, -1, far_index).astype(jnp.int32)


def block_scale(stream_key, extent, cuts, smallest, high):
    factor_of = 1.0
    for axis_at, parts in cuts:
        draws = jax.random.uniform(jax.random.fold_in(jax.random.fold_in(stream_key, 6), axis_at), (parts,), jnp.float32, smallest / len(cuts), high / len(cuts))
        factor_of = factor_of * jnp.repeat(jnp.exp(draws), extent[axis_at] // parts).reshape((-1,) + (1,) * (len(extent) - 1 - axis_at))
    return factor_of


def setup_inputs(seed: int = 0) -> dict:
    keys = jax.random.split(jax.random.key(seed), 6)
    positions = jnp.clip(10.0 * jax.random.uniform(keys[0], (3, NX, NY, NZ, ATOMS), jnp.float32) ** block_scale(keys[0], (3, NX, NY, NZ, ATOMS), ((1, 4), (2, 4), (3, 8)), -0.2, 0.2), 0.0, 10.0)
    atom_kinds = draw_atom_kinds(jax.random.fold_in(keys[5], 71), 0)
    bond_partners = draw_bond_partners(jax.random.fold_in(keys[5], 71), 0)
    torsion_bonds = draw_torsion_bonds(jax.random.fold_in(keys[5], 71), 0)
    torsion_far = draw_torsion_far(jax.random.fold_in(keys[5], 71), 0)
    return dict(positions=positions, atom_kinds=atom_kinds, bond_partners=bond_partners, torsion_bonds=torsion_bonds, torsion_far=torsion_far)


cell_length = 10.0
cutoff = 10.0
coulomb = 14.4
order_rate = -0.3
excess_rate = 1.0
charge_unit = 100.0
shield_table = (0.82, 1.08, 0.75)
negativity_table = (4.7, 8.5, 5.3)
hardness_table = (6.0, 7.2, 7.4)
radius_table = (5.0, 4.0, 3.0)
valence_table = (4.0, 2.0, 1.0)
bend_table = (40.0, 30.0, 10.0)
cosine_table = (-0.3333, -0.25, -0.5)
twist_table = (20.0, 12.0, 6.0)

def lookup(labels, table):
    result = jnp.zeros(labels.shape, jnp.float32)
    for number, amount in enumerate(table):
        result = result + jnp.where(labels == number, amount, 0.0)
    return result

def neighbour_steps():
    return [(shift_x, shift_y, shift_z) for shift_x in (-1, 0, 1) for shift_y in (-1, 0, 1) for shift_z in (-1, 0, 1)]

def cell_step(shift_x, shift_y, shift_z):
    return jnp.array([shift_x, shift_y, shift_z], jnp.float32).reshape(3, 1, 1, 1, 1) * cell_length

def surround(field):
    pieces = [jnp.roll(field, (-shift_x, -shift_y, -shift_z), axis=(1, 2, 3)) for shift_x, shift_y, shift_z in neighbour_steps()]
    return jnp.concatenate(pieces, axis=-1)

def surround_positions(positions):
    pieces = []
    for shift_x, shift_y, shift_z in neighbour_steps():
        rolled = jnp.roll(positions, (-shift_x, -shift_y, -shift_z), axis=(1, 2, 3))
        pieces.append(rolled + cell_step(shift_x, shift_y, shift_z))
    return jnp.concatenate(pieces, axis=-1)

def coupling(own_pos, own_gamma, near_pos, near_gamma, keep_mask):
    distance_sq = jnp.zeros(own_gamma.shape + near_gamma.shape[-1:], jnp.float32)
    for axis_number in range(3):
        difference = near_pos[axis_number][:, None, :] - own_pos[axis_number][:, :, None]
        distance_sq = distance_sq + difference * difference
    distance = jnp.sqrt(distance_sq)
    scaled = jnp.minimum(distance / cutoff, 1.0)
    taper_val = 1.0 + scaled ** 4 * (-35.0 + scaled * (84.0 + scaled * (-70.0 + 20.0 * scaled)))
    shield = (own_gamma[:, :, None] * near_gamma[:, None, :]) ** (-1.5)
    return keep_mask * (coulomb * taper_val / jnp.cbrt(distance_sq * distance + shield))

def pick(near, index):
    picked = []
    for column in range(index.shape[0]):
        spread_index = jnp.broadcast_to(index[column][None], near.shape[:-1] + index.shape[-1:])
        picked.append(jnp.take_along_axis(near, spread_index, axis=-1))
    return jnp.stack(picked, axis=1)

def select(values, slots):
    result = jnp.zeros((values.shape[0],) + slots.shape, values.dtype)
    for column in range(values.shape[1]):
        result = result + jnp.where((slots == column)[None], values[:, column][:, None], 0.0)
    return result

def damping(excess):
    return 2.0 / (1.0 + jnp.exp(excess_rate * excess))

def raw_orders(positions, radius, near_pos, near_radius, partners):
    bond_live = partners >= 0
    safe_index = jnp.maximum(partners, 0)
    bond_vec = pick(near_pos, safe_index) - positions[:, None]
    partner_radius = pick(near_radius[None], safe_index)[0]
    length_sq = lax.optimization_barrier(jnp.sum(bond_vec * bond_vec, axis=0))
    raw_order = jnp.where(bond_live, jnp.exp(order_rate * length_sq / (radius + partner_radius) ** 2), 0.0)
    return (bond_vec, partner_radius, raw_order)

def corrected(raw_order, excess, near_excess, partners):
    partner_excess = pick(near_excess[None], jnp.maximum(partners, 0))[0]
    return raw_order * damping(excess)[None] * damping(partner_excess)

def energy(bond_vec, far_vec, angle_weight, twist_weight, bend, rest, twist, first_slot, second_slot):
    energy_sum = jnp.zeros((), jnp.float32)
    number = 0
    for slot_a in range(bond_vec.shape[1]):
        for slot_b in range(slot_a + 1, bond_vec.shape[1]):
            left_vec = bond_vec[:, slot_a]
            right_vec = bond_vec[:, slot_b]
            cosine = lax.optimization_barrier(jnp.sum(left_vec * right_vec, axis=0)) / jnp.sqrt((lax.optimization_barrier(jnp.sum(left_vec * left_vec, axis=0)) + 1.0) * (lax.optimization_barrier(jnp.sum(right_vec * right_vec, axis=0)) + 1.0))
            energy_sum = energy_sum + jnp.sum(bend * angle_weight[number] * (cosine - rest) ** 2)
            number = number + 1
    outer_vec = select(bond_vec, first_slot)
    inner_vec = select(bond_vec, second_slot)
    across = far_vec - inner_vec
    first_normal = jnp.cross(outer_vec, inner_vec, axis=0)
    second_normal = jnp.cross(inner_vec, across, axis=0)
    cosine = lax.optimization_barrier(jnp.sum(first_normal * second_normal, axis=0)) / jnp.sqrt((lax.optimization_barrier(jnp.sum(first_normal * first_normal, axis=0)) + 1.0) * (lax.optimization_barrier(jnp.sum(second_normal * second_normal, axis=0)) + 1.0))
    return energy_sum + jnp.sum(twist * twist_weight * (1.0 - cosine * cosine))

def angle_forces(bond_vec, partner_radius, orders, near_pos, near_radius, positions, labels, torsion_bonds, torsion_far):
    far_live = torsion_far >= 0
    far_safe = jnp.maximum(torsion_far, 0)
    far_vec = pick(near_pos, far_safe) - positions[:, None]
    far_radius = pick(near_radius[None], far_safe)[0]
    first_slot = torsion_bonds[0]
    second_slot = torsion_bonds[1]
    inner_vec = select(bond_vec, second_slot)
    inner_radius = select(partner_radius[None], second_slot)[0]
    across = far_vec - inner_vec
    far_order = jnp.exp(order_rate * lax.optimization_barrier(jnp.sum(across * across, axis=0)) / (inner_radius + far_radius) ** 2)
    twist_weight = jnp.where(far_live, select(orders[None], first_slot)[0] * select(orders[None], second_slot)[0] * far_order, 0.0)
    weights = []
    for slot_a in range(orders.shape[0]):
        for slot_b in range(slot_a + 1, orders.shape[0]):
            weights.append(orders[slot_a] * orders[slot_b])
    angle_weight = jnp.stack(weights)
    gradients = jax.grad(energy, argnums=(0, 1))(bond_vec, far_vec, angle_weight, twist_weight, lookup(labels, bend_table), lookup(labels, cosine_table), lookup(labels, twist_table), first_slot, second_slot)
    return (-gradients[0], -gradients[1])

def broaden(values):
    return values[:, None, None, None, None]

def reference(positions, atom_kinds, bond_partners, torsion_bonds, torsion_far):
    atom_count = positions.shape[-1]
    cell_count = NX * NY * NZ
    span_cols = 27 * atom_count
    block_cells = CX * CY * CZ
    groups = cell_count // block_cells
    shielding = lookup(atom_kinds, shield_table)
    negativity = lookup(atom_kinds, negativity_table)
    hardness = lookup(atom_kinds, hardness_table)
    radius = lookup(atom_kinds, radius_table)
    valence = lookup(atom_kinds, valence_table)
    near_full = surround_positions(positions)
    near_radius = surround(radius[None])[0]
    own_pos = positions.reshape(3, groups, block_cells, atom_count).transpose(1, 0, 2, 3)
    own_gamma = shielding.reshape(groups, block_cells, atom_count)
    near_pos = near_full.reshape(3, groups, block_cells, span_cols).transpose(1, 0, 2, 3)
    near_gamma = surround(shielding[None]).reshape(groups, block_cells, span_cols)
    column = jnp.arange(span_cols)[None, :]
    row_index = jnp.arange(atom_count)[:, None]
    keep_mask = jnp.where(column == 13 * atom_count + row_index, 0.0, 1.0)

    def couple(vectors):
        near_vec = surround(vectors).reshape(2, groups, block_cells, span_cols).transpose(1, 0, 2, 3)

        def one_block(pieces):
            block_pos, block_gamma, block_near, block_near_gamma, block_vec = pieces
            coupling_tiles = coupling(block_pos, block_gamma, block_near, block_near_gamma, keep_mask)
            return jnp.einsum('nam,knm->kna', coupling_tiles, block_vec, precision=lax.Precision.HIGHEST)
        result = lax.map(one_block, (own_pos, own_gamma, near_pos, near_gamma, near_vec))
        return result.transpose(1, 0, 2, 3).reshape(2, NX, NY, NZ, atom_count)
    target = jnp.stack([-negativity, -jnp.ones_like(negativity)])
    first_pass = couple(jnp.stack([-negativity, jnp.ones_like(negativity)]))
    diagonal = hardness + first_pass[1]
    applied = diagonal * target + jnp.stack([first_pass[0], -first_pass[1]])
    solution = jnp.zeros_like(target)
    residual = target
    direction = target
    norm_now = lax.optimization_barrier(jnp.sum(residual * residual, axis=(1, 2, 3, 4)))
    for number in range(ITERS):
        if number > 0:
            applied = diagonal * direction + couple(direction)
        curvature = lax.optimization_barrier(jnp.sum(direction * applied, axis=(1, 2, 3, 4)))
        step_size = broaden(norm_now / curvature)
        solution = solution + step_size * direction
        residual = residual - step_size * applied
        norm_next = lax.optimization_barrier(jnp.sum(residual * residual, axis=(1, 2, 3, 4)))
        direction = residual + broaden(norm_next / norm_now) * direction
        norm_now = norm_next
    charge_sums = lax.optimization_barrier(jnp.sum(solution, axis=(1, 2, 3, 4)))
    charges = charge_unit * (solution[0] - charge_sums[0] / charge_sums[1] * solution[1])
    bond_vec, partner_radius, raw_order = raw_orders(positions, radius, near_full, near_radius, bond_partners)
    excess = lax.optimization_barrier(jnp.sum(raw_order, axis=0)) - valence
    near_excess = surround(excess[None])[0]
    orders = corrected(raw_order, excess, near_excess, bond_partners)
    bond_forces, far_forces = angle_forces(bond_vec, partner_radius, orders, near_full, near_radius, positions, atom_kinds, torsion_bonds, torsion_far)
    return (charges, orders, bond_forces, far_forces)
```

```python
import jax
import jax.numpy as jnp
from jax import lax
from jax.experimental import pallas as pl
from jax.experimental.pallas import tpu as pltpu
from jax.sharding import PartitionSpec as P

MESH = pl.DeviceIdType.MESH

ATOMS = 128
NBOND = 4
NTOR = 4
cutoff = 10.0
coulomb = 14.4
order_rate = -0.3
charge_unit = 100.0
shield_table = (0.82, 1.08, 0.75)
negativity_table = (4.7, 8.5, 5.3)
hardness_table = (6.0, 7.2, 7.4)
radius_table = (5.0, 4.0, 3.0)
valence_table = (4.0, 2.0, 1.0)
bend_table = (40.0, 30.0, 10.0)
cosine_table = (-0.3333, -0.25, -0.5)
twist_table = (20.0, 12.0, 6.0)

STEPS = [(a, b, c) for a in (-1, 0, 1) for b in (-1, 0, 1) for c in (-1, 0, 1)]
SIDES = [s for s in STEPS if s != (0, 0, 0)]
KROWS = 16
VROWS = 32


def lookup(kind, table):
    return jnp.where(kind == 0, table[0], jnp.where(kind == 1, table[1], table[2])).astype(jnp.float32)


def send_range(step, size):
    if step > 0:
        return (size, 1)
    if step < 0:
        return (1, 1)
    return (1, size)


def land_range(step, size):
    if step > 0:
        return (0, 1)
    if step < 0:
        return (size + 1, 1)
    return (1, size)


def add3(a, b):
    return [p + q for p, q in zip(a, b)]


def dot3(a, b):
    return a[0] * b[0] + a[1] * b[1] + a[2] * b[2]


def cross3(a, b):
    return [
        a[1] * b[2] - a[2] * b[1],
        a[2] * b[0] - a[0] * b[2],
        a[0] * b[1] - a[1] * b[0],
    ]


def make_kernel(sizes, block, total_atoms):
    nx, ny, nz = sizes
    cx, cy, cz = block
    cells = cx * cy * cz
    cell_list = [(x, y, z) for x in range(cx) for y in range(cy) for z in range(cz)]
    plane = [(i, j) for i in range(nx) for j in range(ny) if (i, j) != (0, 0)]
    line = list(range(1, nz))
    partners = {(a % nx, b % ny, c % nz) for a, b, c in SIDES}
    partners |= {(i, j, 0) for i, j in plane}
    partners |= {(0, 0, k) for k in line}
    partners = sorted(partners)

    def kernel(
        pos, kinds, bp, tb, tf,
        charges, orders_out, bforce, fforce,
        ext, dext, colb, kbuf, ycol, vext, gext, idxb, bv, gb, ownc, kindc, torc, raws,
        ar_send, ar_plane, ar_mid, ar_line,
        pos_send, pos_recv, vec_send, vec_recv, g_send, g_recv,
        plane_send, plane_recv, line_send, line_recv,
    ):
        ix = lax.axis_index("gx")
        iy = lax.axis_index("gy")
        iz = lax.axis_index("gz")

        def device(a, b, c):
            return (lax.rem(ix + a + nx, nx), lax.rem(iy + b + ny, ny), lax.rem(iz + c + nz, nz))

        barrier = pltpu.get_barrier_semaphore()
        for a, b, c in partners:
            pl.semaphore_signal(barrier, inc=1, device_id=device(a, b, c), device_id_type=MESH)

        def halo(ref, send, recv):
            copies = []
            for number, (a, b, c) in enumerate(SIDES):
                sx, sy, sz = send_range(a, cx), send_range(b, cy), send_range(c, cz)
                lx, ly, lz = land_range(a, cx), land_range(b, cy), land_range(c, cz)
                copies.append(
                    pltpu.make_async_remote_copy(
                        src_ref=ref.at[pl.ds(*sx), pl.ds(*sy), pl.ds(*sz)],
                        dst_ref=ref.at[pl.ds(*lx), pl.ds(*ly), pl.ds(*lz)],
                        send_sem=send.at[number],
                        recv_sem=recv.at[number],
                        device_id=device(a, b, c),
                        device_id_type=MESH,
                    )
                )
            for copy in copies:
                copy.start()
            return copies

        def landed(copies):
            for copy in copies:
                copy.wait_recv()

        def finish(copies):
            for copy in copies:
                copy.wait_send()

        for x, y, z in cell_list:
            for f in range(3):
                ext[x + 1, y + 1, z + 1, f : f + 1, :] = pos[f, x, y, z : z + 1, :]
            ext[x + 1, y + 1, z + 1, 3:4, :] = kinds[x, y, z : z + 1, :].astype(jnp.float32)
        for x in range(cx):
            for y in range(cy):
                at = (x * cy + y) * cz
                for f in range(3):
                    ownc[f, at : at + cz, :] = pos[f, x, y]
                kindc[at : at + cz, :] = kinds[x, y]
                for s in range(NTOR):
                    torc[0, s, at : at + cz, :] = tb[0, s, x, y]
                    torc[1, s, at : at + cz, :] = tb[1, s, x, y]
        for number, (x, y, z) in enumerate(cell_list):
            for s in range(NBOND):
                idxb[number, s : s + 1, :] = bp[s, x, y, z : z + 1, :]
                idxb[number, NBOND + s : NBOND + s + 1, :] = tf[s, x, y, z : z + 1, :]

        pl.semaphore_wait(barrier, len(partners))
        pos_copies = halo(ext, pos_send, pos_recv)

        shield_root = [float((cutoff * g) ** -1.5) for g in shield_table]
        kind_own = kindc[0:cells, :]
        g_own = lookup(kind_own, shield_root)
        ycol[...] = jnp.zeros((ATOMS, ATOMS), jnp.float32)
        for f in range(3):
            ycol[16 * f : 16 * f + cells, :] = ownc[f, 0:cells, :] * (1.0 / cutoff)
        ycol[48 : 48 + cells, :] = g_own
        flipped = jnp.transpose(ycol[...])
        for number in range(cells):
            for f in range(4):
                at = 16 * f + number
                colb[number, f] = jnp.broadcast_to(flipped[:, at : at + 1], (ATOMS, ATOMS))

        landed(pos_copies)

        def cell_of(c):
            return (c // (cy * cz), lax.rem(c // cz, cy), lax.rem(c, cz))

        def derive(n, carry):
            x = n // ((cy + 2) * (cz + 2))
            y = lax.rem(n // (cz + 2), cy + 2)
            z = lax.rem(n, cz + 2)
            tile = ext[x, y, z]
            kind = tile[3:4, :]
            dext[x, y, z, 0:3, :] = tile[0:3, :] * (1.0 / cutoff)
            dext[x, y, z, 3:4, :] = lookup(kind, shield_root)
            dext[x, y, z, 4:5, :] = lookup(kind, negativity_table)
            return carry

        lax.fori_loop(0, (cx + 2) * (cy + 2) * (cz + 2), derive, 0)

        def gather_cell(c, carry):
            x, y, z = cell_of(c)
            index = jnp.maximum(idxb[c], 0)
            offset = lax.shift_right_logical(index, 7)
            atom = jnp.bitwise_and(index, 127)
            picked = [jnp.zeros((8, ATOMS), jnp.float32) for _ in range(4)]
            for k, (a, b, d) in enumerate(STEPS):
                here = offset == k
                for f in range(4):
                    row = jnp.broadcast_to(
                        ext[x + 1 + a, y + 1 + b, z + 1 + d, f : f + 1, :], (8, ATOMS)
                    )
                    got = jnp.take_along_axis(row, atom, axis=1, mode="promise_in_bounds")
                    picked[f] = jnp.where(here, got, picked[f])
            sx = (offset >= 9).astype(jnp.int32) + (offset >= 18).astype(jnp.int32)
            rest = offset - 9 * sx
            sy = (rest >= 3).astype(jnp.int32) + (rest >= 6).astype(jnp.int32)
            sz = rest - 3 * sy
            for f, step in enumerate((sx, sy, sz)):
                shift = (step - 1).astype(jnp.float32) * cutoff
                own = ext[x + 1, y + 1, z + 1, f : f + 1, :]
                vec = picked[f] + shift - own
                for s in range(8):
                    bv[f, s, pl.ds(c, 1), :] = vec[s : s + 1, :]
            radius = lookup(picked[3], radius_table)
            for s in range(8):
                bv[3, s, pl.ds(c, 1), :] = radius[s : s + 1, :]
                gb[s, pl.ds(c, 1), :] = jnp.where(idxb[c, s : s + 1, :] >= 0, 1.0, 0.0)
            return carry

        lax.fori_loop(0, cells, gather_cell, 0)

        radius_own = lookup(kind_own, radius_table)
        excess = -lookup(kind_own, valence_table)
        for s in range(NBOND):
            vec = [bv[f, s, 0:cells, :] for f in range(3)]
            span = radius_own + bv[3, s, 0:cells, :]
            raw = gb[s, 0:cells, :] * jnp.exp(order_rate * dot3(vec, vec) / (span * span))
            raws[s, 0:cells, :] = raw
            excess = excess + raw
        g_here = 2.0 / (1.0 + jnp.exp(excess))
        for number, (x, y, z) in enumerate(cell_list):
            gext[x + 1, y + 1, z + 1, 0:1, :] = g_here[number : number + 1, :]
        g_copies = halo(gext, g_send, g_recv)

        lane_of = lax.broadcasted_iota(jnp.int32, (KROWS, ATOMS), 1)
        row_of = lax.broadcasted_iota(jnp.int32, (KROWS, ATOMS), 0)
        lane_v = lax.broadcasted_iota(jnp.int32, (VROWS, ATOMS), 1)

        def coupling_cell(c, carry):
            x, y, z = cell_of(c)

            def rows(r, inner):
                at = pl.multiple_of(r * KROWS, KROWS)
                own = [colb[c, f, pl.ds(at, KROWS), :] for f in range(4)]
                moved = [[own[f] - float(s) for s in (-1, 0, 1)] for f in range(3)]
                sum_one = jnp.zeros((KROWS, ATOMS), jnp.float32)
                sum_chi = jnp.zeros((KROWS, ATOMS), jnp.float32)
                for k, step in enumerate(STEPS):
                    a, b, d = step
                    near = [
                        dext[x + 1 + a, y + 1 + b, z + 1 + d, f : f + 1, :] for f in range(5)
                    ]
                    dist = [near[f] - moved[f][step[f] + 1] for f in range(3)]
                    q = jnp.minimum(dot3(dist, dist), 1.0)
                    u = q * lax.rsqrt(jnp.maximum(q, 1e-30))
                    inner_sum = u * q + own[3] * near[3]
                    inv = jnp.exp2(jnp.log(inner_sum) * (-1.0 / (3.0 * 0.6931471805599453)))
                    even = q * -70.0 - 35.0
                    odd = (q * 20.0 + 84.0) * u
                    value = ((even + odd) * (q * q) + 1.0) * inv
                    if k == 13:
                        value = jnp.where(row_of + at == lane_of, 0.0, value)
                    kbuf[c, k, pl.ds(at, KROWS), :] = value
                    sum_one = sum_one + value
                    sum_chi = sum_chi + value * near[4]
                one = jnp.sum(sum_one, axis=1, keepdims=True)
                chi = jnp.sum(sum_chi, axis=1, keepdims=True)
                old = ycol[pl.ds(at, KROWS), :]
                ycol[pl.ds(at, KROWS), :] = jnp.where(
                    lane_of == c, chi, jnp.where(lane_of == c + 16, one, old)
                )
                return inner

            return lax.fori_loop(0, ATOMS // KROWS, rows, carry)

        lax.fori_loop(0, cells, coupling_cell, 0)

        scale = coulomb / cutoff

        def products():
            turned = jnp.transpose(ycol[...])
            return (scale * turned[0:cells, :], scale * turned[16 : 16 + cells, :])

        def apply(number):
            def cell(c, carry):
                x, y, z = cell_of(c)

                def rows(r, inner):
                    at = pl.multiple_of(r * VROWS, VROWS)
                    first = jnp.zeros((VROWS, ATOMS), jnp.float32)
                    second = jnp.zeros((VROWS, ATOMS), jnp.float32)
                    for k, (a, b, d) in enumerate(STEPS):
                        value = kbuf[c, k, pl.ds(at, VROWS), :]
                        first = first + value * vext[number, x + 1 + a, y + 1 + b, z + 1 + d, 0:1, :]
                        second = second + value * vext[number, x + 1 + a, y + 1 + b, z + 1 + d, 1:2, :]
                    one = jnp.sum(first, axis=1, keepdims=True)
                    two = jnp.sum(second, axis=1, keepdims=True)
                    old = ycol[pl.ds(at, VROWS), :]
                    ycol[pl.ds(at, VROWS), :] = jnp.where(
                        lane_v == c, one, jnp.where(lane_v == c + 16, two, old)
                    )
                    return inner

                return lax.fori_loop(0, ATOMS // VROWS, rows, carry)

            lax.fori_loop(0, cells, cell, 0)
            return products()

        def place(number, first, second):
            for at, (x, y, z) in enumerate(cell_list):
                vext[number, x + 1, y + 1, z + 1, 0:1, :] = first[at : at + 1, :]
                vext[number, x + 1, y + 1, z + 1, 1:2, :] = second[at : at + 1, :]
            return halo(vext.at[number], vec_send.at[number], vec_recv.at[number])

        def reduce_start(number, values):
            for at in range(8):
                if at < len(values):
                    row = jnp.sum(values[at], axis=0, keepdims=True)
                else:
                    row = jnp.zeros((1, ATOMS), jnp.float32)
                ar_send[number, at : at + 1, :] = row
            copies = []
            for slot, (i, j) in enumerate(plane):
                copies.append(
                    pltpu.make_async_remote_copy(
                        src_ref=ar_send.at[number],
                        dst_ref=ar_plane.at[number, slot],
                        send_sem=plane_send.at[number, slot],
                        recv_sem=plane_recv.at[number, slot],
                        device_id=device(i, j, 0),
                        device_id_type=MESH,
                    )
                )
            for copy in copies:
                copy.start()
            return copies

        def reduce_next(number, copies):
            landed(copies)
            total = ar_send[number]
            for slot in range(len(plane)):
                total = total + ar_plane[number, slot]
            ar_mid[number] = total
            after = []
            for slot, k in enumerate(line):
                after.append(
                    pltpu.make_async_remote_copy(
                        src_ref=ar_mid.at[number],
                        dst_ref=ar_line.at[number, slot],
                        send_sem=line_send.at[number, slot],
                        recv_sem=line_recv.at[number, slot],
                        device_id=device(0, 0, k),
                        device_id_type=MESH,
                    )
                )
            for copy in after:
                copy.start()
            return after

        def reduce_end(number, copies):
            landed(copies)
            total = ar_mid[number]
            for slot in range(len(line)):
                total = total + ar_line[number, slot]
            summed = jnp.broadcast_to(jnp.sum(total, axis=1, keepdims=True), (8, ATOMS))
            return [summed[at : at + 1, :] for at in range(8)]

        chi = lookup(kind_own, negativity_table)
        kchi, ksum = products()
        diagonal = lookup(kind_own, hardness_table) + ksum
        ws = -(diagonal * chi + kchi)
        wt = -(diagonal + ksum)
        vec0 = place(0, ws, wt)
        red0 = reduce_start(0, [chi * chi, -chi * ws, ws * ws, -wt, wt * wt, chi])
        red0b = reduce_next(0, red0)
        landed(vec0)
        k2s, k2t = apply(0)
        hws = diagonal * ws + k2s
        hwt = diagonal * wt + k2t
        rr0s, pq0s, qq0s, pq0t, qq0t, chi_sum, _, _ = reduce_end(0, red0b)
        rr0t = jnp.full((1, ATOMS), float(total_atoms), jnp.float32)
        a0s, a0t = rr0s / pq0s, rr0t / pq0t
        b0s = a0s * a0s * qq0s / rr0s - 1.0
        b0t = a0t * a0t * qq0t / rr0t - 1.0
        r1s, r1t = -chi - a0s * ws, -1.0 - a0t * wt
        d1s, d1t = r1s - b0s * chi, r1t - b0t
        hr1s, hr1t = ws - a0s * hws, wt - a0t * hwt
        q1s, q1t = hr1s + b0s * ws, hr1t + b0t * wt
        vec1 = place(1, q1s, q1t)
        red1 = reduce_start(
            1, [r1s * r1s, d1s * q1s, q1s * q1s, d1s, r1t * r1t, d1t * q1t, q1t * q1t, d1t]
        )
        red1b = reduce_next(1, red1)
        landed(vec1)
        k3s, k3t = apply(1)
        hq1s = diagonal * q1s + k3s
        hq1t = diagonal * q1t + k3t
        rr1s, pq1s, qq1s, d1s_sum, rr1t, pq1t, qq1t, d1t_sum = reduce_end(1, red1b)
        a1s, a1t = rr1s / pq1s, rr1t / pq1t
        b1s = a1s * a1s * qq1s / rr1s - 1.0
        b1t = a1t * a1t * qq1t / rr1t - 1.0
        r2s, r2t = r1s - a1s * q1s, r1t - a1t * q1t
        d2s, d2t = r2s + b1s * d1s, r2t + b1t * d1t
        q2s = hr1s - a1s * hq1s + b1s * q1s
        q2t = hr1t - a1t * hq1t + b1t * q1t
        red2 = reduce_start(2, [r2s * r2s, d2s * q2s, d2s, r2t * r2t, d2t * q2t, d2t])

        landed(g_copies)

        def gather_damping(c, carry):
            x, y, z = cell_of(c)
            index = jnp.maximum(idxb[c], 0)
            offset = lax.shift_right_logical(index, 7)
            atom = jnp.bitwise_and(index, 127)
            picked = jnp.zeros((8, ATOMS), jnp.float32)
            for k, (a, b, d) in enumerate(STEPS):
                row = jnp.broadcast_to(gext[x + 1 + a, y + 1 + b, z + 1 + d, 0:1, :], (8, ATOMS))
                got = jnp.take_along_axis(row, atom, axis=1, mode="promise_in_bounds")
                picked = jnp.where(offset == k, got, picked)
            for s in range(NBOND):
                raws[s, pl.ds(c, 1), :] = raws[s, pl.ds(c, 1), :] * picked[s : s + 1, :]
            return carry

        lax.fori_loop(0, cells, gather_damping, 0)
        red2b = reduce_next(2, red2)

        def spread_out(ref, lead, value):
            for x in range(cx):
                for y in range(cy):
                    at = (x * cy + y) * cz
                    ref[(*lead, x, y)] = value[at : at + cz, :]

        order = []
        for s in range(NBOND):
            order.append(raws[s, 0:cells, :] * g_here)
            spread_out(orders_out, (s,), order[s])
        bend = lookup(kind_own, bend_table)
        rest = lookup(kind_own, cosine_table)
        twist = lookup(kind_own, twist_table)
        vecs = [[bv[f, s, 0:cells, :] for f in range(3)] for s in range(NBOND)]
        radii = [bv[3, s, 0:cells, :] for s in range(NBOND)]
        inv = [lax.rsqrt(dot3(vecs[s], vecs[s]) + 1.0) for s in range(NBOND)]
        force = [[jnp.zeros((cells, ATOMS), jnp.float32) for _ in range(3)] for _ in range(NBOND)]
        for a in range(NBOND):
            for b in range(a + 1, NBOND):
                both = inv[a] * inv[b]
                cosine = dot3(vecs[a], vecs[b]) * both
                pull = -2.0 * bend * (order[a] * order[b]) * (cosine - rest)
                cross_part = pull * both
                own_part = pull * cosine
                pa = own_part * (inv[a] * inv[a])
                pb = own_part * (inv[b] * inv[b])
                for f in range(3):
                    force[a][f] = force[a][f] + (cross_part * vecs[b][f] - pa * vecs[a][f])
                    force[b][f] = force[b][f] + (cross_part * vecs[a][f] - pb * vecs[b][f])

        def choose(options, slot):
            out = options[0]
            for s in range(1, NBOND):
                out = jnp.where(slot == s, options[s], out)
            return out

        for t in range(NTOR):
            first = torc[0, t, 0:cells, :]
            second = torc[1, t, 0:cells, :]
            vj = [choose([vecs[s][f] for s in range(NBOND)], first) for f in range(3)]
            vk = [choose([vecs[s][f] for s in range(NBOND)], second) for f in range(3)]
            weight = choose(order, first) * choose(order, second)
            span = choose(radii, second) + bv[3, NBOND + t, 0:cells, :]
            far = [bv[f, NBOND + t, 0:cells, :] for f in range(3)]
            u = [far[f] - vk[f] for f in range(3)]
            weight = weight * jnp.exp(order_rate * dot3(u, u) / (span * span))
            weight = weight * gb[NBOND + t, 0:cells, :]
            n1 = cross3(vj, vk)
            n2 = cross3(vk, u)
            i1 = lax.rsqrt(dot3(n1, n1) + 1.0)
            i2 = lax.rsqrt(dot3(n2, n2) + 1.0)
            both = i1 * i2
            cosine = dot3(n1, n2) * both
            pull = 2.0 * twist * weight * cosine
            cross_part = pull * both
            own1 = pull * cosine * (i1 * i1)
            own2 = pull * cosine * (i2 * i2)
            p1 = [cross_part * n2[f] - own1 * n1[f] for f in range(3)]
            p2 = [cross_part * n1[f] - own2 * n2[f] for f in range(3)]
            fj = cross3(vk, p1)
            fw = cross3(p2, vk)
            part1 = cross3(p1, vj)
            part2 = cross3(u, p2)
            fk = [part1[f] + part2[f] - fw[f] for f in range(3)]
            for s in range(NBOND):
                for f in range(3):
                    force[s][f] = (
                        force[s][f]
                        + jnp.where(first == s, fj[f], 0.0)
                        + jnp.where(second == s, fk[f], 0.0)
                    )
            for f in range(3):
                spread_out(fforce, (f, t), fw[f])
        for s in range(NBOND):
            for f in range(3):
                spread_out(bforce, (f, s), force[s][f])

        rr2s, pq2s, d2s_sum, rr2t, pq2t, d2t_sum, _, _ = reduce_end(2, red2b)
        a2s, a2t = rr2s / pq2s, rr2t / pq2t
        solve_s = -a0s * chi + a1s * d1s + a2s * d2s
        solve_t = -a0t + a1t * d1t + a2t * d2t
        sum_s = -a0s * chi_sum + a1s * d1s_sum + a2s * d2s_sum
        sum_t = -a0t * rr0t + a1t * d1t_sum + a2t * d2t_sum
        result = charge_unit * (solve_s - (sum_s / sum_t) * solve_t)
        spread_out(charges, (), result)

        for copies in (pos_copies, g_copies, vec0, vec1, red0, red0b, red1, red1b, red2, red2b):
            finish(copies)

    def scratch():
        big = (cx + 2, cy + 2, cz + 2)
        sides = len(SIDES)
        dma = pltpu.SemaphoreType.DMA
        f32 = jnp.float32
        return [
            pltpu.VMEM((*big, 4, ATOMS), f32),
            pltpu.VMEM((*big, 8, ATOMS), f32),
            pltpu.VMEM((cells, 4, ATOMS, ATOMS), f32),
            pltpu.VMEM((cells, 27, ATOMS, ATOMS), f32),
            pltpu.VMEM((ATOMS, ATOMS), f32),
            pltpu.VMEM((2, *big, 2, ATOMS), f32),
            pltpu.VMEM((*big, 1, ATOMS), f32),
            pltpu.VMEM((cells, 8, ATOMS), jnp.int32),
            pltpu.VMEM((4, 8, 16, ATOMS), f32),
            pltpu.VMEM((8, 16, ATOMS), f32),
            pltpu.VMEM((3, 16, ATOMS), f32),
            pltpu.VMEM((16, ATOMS), jnp.int32),
            pltpu.VMEM((2, NTOR, 16, ATOMS), jnp.int32),
            pltpu.VMEM((NBOND, 16, ATOMS), f32),
            pltpu.VMEM((3, 8, ATOMS), f32),
            pltpu.VMEM((3, len(plane), 8, ATOMS), f32),
            pltpu.VMEM((3, 8, ATOMS), f32),
            pltpu.VMEM((3, len(line), 8, ATOMS), f32),
            dma((sides,)), dma((sides,)),
            dma((2, sides)), dma((2, sides)),
            dma((sides,)), dma((sides,)),
            dma((3, len(plane))), dma((3, len(plane))),
            dma((3, len(line))), dma((3, len(line))),
        ]

    return kernel, scratch()


def solution(mesh):
    sizes = (mesh.shape["gx"], mesh.shape["gy"], mesh.shape["gz"])

    def on_device(positions, atom_kinds, bond_partners, torsion_bonds, torsion_far):
        block = positions.shape[1:4]
        total = ATOMS
        for count, size in zip(block, sizes):
            total *= count * size
        kernel, scratch = make_kernel(sizes, block, total)
        f32 = jnp.float32
        whole = pl.BlockSpec(memory_space=pltpu.VMEM)
        return pl.pallas_call(
            kernel,
            out_shape=(
                jax.ShapeDtypeStruct((*block, ATOMS), f32),
                jax.ShapeDtypeStruct((NBOND, *block, ATOMS), f32),
                jax.ShapeDtypeStruct((3, NBOND, *block, ATOMS), f32),
                jax.ShapeDtypeStruct((3, NTOR, *block, ATOMS), f32),
            ),
            in_specs=[whole] * 5,
            out_specs=(whole,) * 4,
            scratch_shapes=scratch,
            compiler_params=pltpu.CompilerParams(
                collective_id=0, has_side_effects=True, vmem_limit_bytes=48 * 1024 * 1024
            ),
            name="reax_step",
        )(positions, atom_kinds, bond_partners, torsion_bonds, torsion_far)

    placed = (
        P(None, "gx", "gy", "gz", None),
        P("gx", "gy", "gz", None),
        P(None, "gx", "gy", "gz", None),
        P(None, None, "gx", "gy", "gz", None),
        P(None, "gx", "gy", "gz", None),
    )
    return jax.shard_map(
        on_device,
        mesh=mesh,
        in_specs=placed,
        out_specs=(
            P("gx", "gy", "gz", None),
            P(None, "gx", "gy", "gz", None),
            P(None, None, "gx", "gy", "gz", None),
            P(None, None, "gx", "gy", "gz", None),
        ),
        check_vma=False,
    )
```

```python
import jax
import jax.numpy as jnp
from jax import lax
from jax.experimental import pallas as pl
from jax.experimental.pallas import tpu as pltpu
from jax.sharding import PartitionSpec as P

MESH = pl.DeviceIdType.MESH

ATOMS = 128
NBOND = 4
NTOR = 4
cutoff = 10.0
coulomb = 14.4
order_rate = -0.3
charge_unit = 100.0
shield_table = (0.82, 1.08, 0.75)
negativity_table = (4.7, 8.5, 5.3)
hardness_table = (6.0, 7.2, 7.4)
radius_table = (5.0, 4.0, 3.0)
valence_table = (4.0, 2.0, 1.0)
bend_table = (40.0, 30.0, 10.0)
cosine_table = (-0.3333, -0.25, -0.5)
twist_table = (20.0, 12.0, 6.0)

STEPS = [(a, b, c) for a in (-1, 0, 1) for b in (-1, 0, 1) for c in (-1, 0, 1)]
SIDES = [s for s in STEPS if s != (0, 0, 0)]
ROWS = 128
DEPTH = 64


def lookup(kind, table):
    return jnp.where(kind == 0, table[0], jnp.where(kind == 1, table[1], table[2])).astype(jnp.float32)


def send_range(step, size):
    if step > 0:
        return (size, 1)
    if step < 0:
        return (1, 1)
    return (1, size)


def land_range(step, size):
    if step > 0:
        return (0, 1)
    if step < 0:
        return (size + 1, 1)
    return (1, size)


def add3(a, b):
    return [p + q for p, q in zip(a, b)]


def dot3(a, b):
    return a[0] * b[0] + a[1] * b[1] + a[2] * b[2]


def cross3(a, b):
    return [
        a[1] * b[2] - a[2] * b[1],
        a[2] * b[0] - a[0] * b[2],
        a[0] * b[1] - a[1] * b[0],
    ]


def make_kernel(sizes, block, total_atoms):
    nx, ny, nz = sizes
    cx, cy, cz = block
    cells = cx * cy * cz
    cell_list = [(x, y, z) for x in range(cx) for y in range(cy) for z in range(cz)]
    plane = [(i, j) for i in range(nx) for j in range(ny) if (i, j) != (0, 0)]
    line = list(range(1, nz))
    partners = {(a % nx, b % ny, c % nz) for a, b, c in SIDES}
    partners |= {(i, j, 0) for i, j in plane}
    partners |= {(0, 0, k) for k in line}
    partners = sorted(partners)

    def kernel(
        pos_in, kinds_in, bp_in, tb_in, tf_in,
        charges, orders_out, bforce, fforce,
        pos, kinds, bp, tb, tf, in_sems,
        ext, dext, brhs, alhs, colg, kbuf, ycol, vext, gext, idxb, bv, gb, kindc, torc, raws,
        ar_send, ar_plane, ar_mid, ar_line,
        pos_send, pos_recv, vec_send, vec_recv, g_send, g_recv,
        plane_send, plane_recv, line_send, line_recv,
    ):
        ix = lax.axis_index("gx")
        iy = lax.axis_index("gy")
        iz = lax.axis_index("gz")

        def device(a, b, c):
            return (lax.rem(ix + a + nx, nx), lax.rem(iy + b + ny, ny), lax.rem(iz + c + nz, nz))

        fetches = [
            pltpu.make_async_copy(source, target, in_sems.at[number])
            for number, (source, target) in enumerate(
                ((pos_in, pos), (kinds_in, kinds), (bp_in, bp), (tf_in, tf), (tb_in, tb))
            )
        ]
        for fetch in fetches:
            fetch.start()
        barrier = pltpu.get_barrier_semaphore()
        for a, b, c in partners:
            pl.semaphore_signal(barrier, inc=1, device_id=device(a, b, c), device_id_type=MESH)

        def halo(ref, send, recv):
            copies = []
            for number, (a, b, c) in enumerate(SIDES):
                sx, sy, sz = send_range(a, cx), send_range(b, cy), send_range(c, cz)
                lx, ly, lz = land_range(a, cx), land_range(b, cy), land_range(c, cz)
                copies.append(
                    pltpu.make_async_remote_copy(
                        src_ref=ref.at[pl.ds(*sx), pl.ds(*sy), pl.ds(*sz)],
                        dst_ref=ref.at[pl.ds(*lx), pl.ds(*ly), pl.ds(*lz)],
                        send_sem=send.at[number],
                        recv_sem=recv.at[number],
                        device_id=device(a, b, c),
                        device_id_type=MESH,
                    )
                )
            for copy in copies:
                copy.start()
            return copies

        def landed(copies):
            for copy in copies:
                copy.wait_recv()

        def finish(copies):
            for copy in copies:
                copy.wait_send()

        fetches[0].wait()
        fetches[1].wait()
        for x, y, z in cell_list:
            for f in range(3):
                ext[x + 1, y + 1, z + 1, f : f + 1, :] = pos[f, x, y, z : z + 1, :]
            ext[x + 1, y + 1, z + 1, 3:4, :] = kinds[x, y, z : z + 1, :].astype(jnp.float32)
        for x in range(cx):
            for y in range(cy):
                at = (x * cy + y) * cz
                kindc[at : at + cz, :] = kinds[x, y]
        kind_own = kindc[0:cells, :]

        def cell_of(c):
            return (c // (cy * cz), lax.rem(c // cz, cy), lax.rem(c, cz))

        shield_root = [float((cutoff * g) ** -1.5) for g in shield_table]
        row8 = lax.broadcasted_iota(jnp.int32, (8, ATOMS), 0)
        ones3 = jnp.where(row8 < 3, 1.0, 0.0)

        def narrow(value):
            return value.astype(jnp.bfloat16).astype(jnp.float32)

        def by_row(values):
            out = jnp.zeros((8, ATOMS), jnp.float32)
            for at, value in enumerate(values):
                if value is not None:
                    out = jnp.where(row8 == at, value, out)
            return out

        def derive(x, y, z, number):
            middle = (x - 0.5 * (cx + 2), y - 0.5 * (cy + 2), z - 0.5 * (cz + 2))
            place_at = by_row(
                [
                    ext[x, y, z, f : f + 1, :] * (1.0 / cutoff) + jnp.float32(middle[f])
                    for f in range(3)
                ]
            )
            grid = jnp.round(place_at * 64.0) * (1.0 / 64.0)
            rest = place_at - grid
            mid = narrow(rest)
            low = rest - mid
            grid_sq = jnp.sum(grid * grid, axis=0, keepdims=True)
            rest_sq = jnp.sum(rest * (2.0 * grid + rest), axis=0, keepdims=True)
            grid_1 = jnp.round(grid_sq * 16.0) * (1.0 / 16.0)
            grid_2 = grid_sq - grid_1
            rest_1 = narrow(rest_sq)
            rest_2 = narrow(rest_sq - rest_1)
            rest_3 = (rest_sq - rest_1) - rest_2
            heads = by_row([grid_1, grid_2, 1.0, 1.0, rest_1, rest_2, rest_3])
            tile = jnp.concatenate([grid, heads, ones3, mid, low, grid, grid, mid], axis=0)
            brhs[x, y, z] = tile.astype(jnp.bfloat16)
            kind = ext[x, y, z, 3:4, :]
            dext[x, y, z, 0:1, :] = lookup(kind, shield_root)
            dext[x, y, z, 1:2, :] = lookup(kind, negativity_table)
            if number is not None:
                heads = by_row([1.0, 1.0, grid_1, grid_2, 1.0, 1.0, 1.0])
                tails = by_row([rest_1, rest_2, rest_3])
                left = jnp.concatenate(
                    [
                        -2.0 * grid, heads, tails, -2.0 * grid,
                        -2.0 * grid, -2.0 * mid, -2.0 * low, -2.0 * mid,
                    ],
                    axis=0,
                )
                alhs[number] = jnp.transpose(left).astype(jnp.bfloat16)

        def derive_own(n, carry):
            x = n // cy
            y = lax.rem(n, cy)
            for z in range(cz):
                derive(x + 1, y + 1, z + 1, (x * cy + y) * cz + z)
            return carry

        lax.fori_loop(0, cx * cy, derive_own, 0)

        ycol[...] = jnp.zeros((ATOMS, ATOMS), jnp.float32)
        ycol[0:cells, :] = lookup(kind_own, shield_root)
        flipped = jnp.transpose(ycol[...])
        for number in range(cells):
            colg[number] = jnp.broadcast_to(flipped[:, number : number + 1], (ATOMS, ATOMS))
        ycol[...] = jnp.zeros((ATOMS, ATOMS), jnp.float32)

        def tiles_of(y):
            every = [
                (i, j, k) for j in (y, y + 1, y + 2) for i in (1, 2, None) for k in (1, 2, None)
            ]
            own = [t for t in every if t[0] and t[2] and 1 <= t[1] <= cy]
            return own, [t for t in every if t not in own]

        row_of = lax.broadcasted_iota(jnp.int32, (ROWS, ATOMS), 0)
        lane_of = lax.broadcasted_iota(jnp.int32, (ROWS, ATOMS), 1)

        def keep_sums(at, c, first, second):
            one = jnp.sum(first, axis=1, keepdims=True)
            two = jnp.sum(second, axis=1, keepdims=True)
            ycol[pl.ds(at, ROWS), :] = ycol[pl.ds(at, ROWS), :] + jnp.where(
                lane_of == c, one, jnp.where(lane_of == c + 16, two, 0.0)
            )

        def coupling_part(y, tiles, base):
            def cell(xz, carry):
                x = xz // cz
                z = lax.rem(xz, cz)
                c = (x * cy + y) * cz + z

                def rows(r, inner):
                    at = pl.multiple_of(r * ROWS, ROWS)
                    left = alhs[c, pl.ds(at, ROWS), :]
                    own_g = colg[c, pl.ds(at, ROWS), :]
                    sum_one = jnp.zeros((ROWS, ATOMS), jnp.float32)
                    sum_chi = jnp.zeros((ROWS, ATOMS), jnp.float32)
                    for slot, (i, j, k) in enumerate(tiles):
                        ex = (cx + 1) * x if i is None else i
                        ez = (cz + 1) * z if k is None else k
                        near_g = dext[ex, j, ez, 0:1, :]
                        near_chi = dext[ex, j, ez, 1:2, :]
                        square = jnp.dot(
                            left, brhs[ex, j, ez], preferred_element_type=jnp.float32
                        )
                        q = jnp.minimum(jnp.maximum(square, 1e-30), 1.0)
                        u = q * lax.rsqrt(q)
                        inv = jnp.exp2(lax.log2(u * q + own_g * near_g) * (-1.0 / 3.0))
                        even = q * -70.0 - 35.0
                        odd = (q * 20.0 + 84.0) * u
                        value = ((even + odd) * (q * q) + 1.0) * inv
                        if i and k and j == y + 1:
                            same = jnp.logical_and(x + 1 == i, z + 1 == k)
                            value = jnp.where(
                                row_of + jnp.where(same, at, -ATOMS) == lane_of, 0.0, value
                            )
                        kbuf[c, r, base + slot] = value
                        sum_one = sum_one + value
                        sum_chi = sum_chi + value * near_chi
                    keep_sums(at, c, sum_chi, sum_one)
                    return inner

                return lax.fori_loop(0, ATOMS // ROWS, rows, carry)

            lax.fori_loop(0, cx * cz, cell, 0)

        tile_sets = [tiles_of(y) for y in range(cy)]
        coupling_part(0, tile_sets[0][0], 0)
        pl.semaphore_wait(barrier, len(partners))
        pos_copies = halo(ext, pos_send, pos_recv)
        for y in range(1, cy):
            coupling_part(y, tile_sets[y][0], 0)

        for fetch in fetches[2:]:
            fetch.wait()
        for x in range(cx):
            for y in range(cy):
                at = (x * cy + y) * cz
                for s in range(NTOR):
                    torc[0, s, at : at + cz, :] = tb[0, s, x, y]
                    torc[1, s, at : at + cz, :] = tb[1, s, x, y]
        for number, (x, y, z) in enumerate(cell_list):
            for s in range(NBOND):
                idxb[number, s : s + 1, :] = bp[s, x, y, z : z + 1, :]
                idxb[number, NBOND + s : NBOND + s + 1, :] = tf[s, x, y, z : z + 1, :]

        landed(pos_copies)

        def derive_x(n, carry):
            x = (cx + 1) * (n // (cy + 2))
            for z in range(cz + 2):
                derive(x, lax.rem(n, cy + 2), z, None)
            return carry

        def derive_y(n, carry):
            for z in range(cz + 2):
                derive(n // 2 + 1, (cy + 1) * lax.rem(n, 2), z, None)
            return carry

        def derive_z(n, carry):
            for z in (0, cz + 1):
                derive(n // cy + 1, lax.rem(n, cy) + 1, z, None)
            return carry

        lax.fori_loop(0, 2 * (cy + 2), derive_x, 0)
        lax.fori_loop(0, 2 * cx, derive_y, 0)
        lax.fori_loop(0, cx * cy, derive_z, 0)
        for y in range(cy):
            coupling_part(y, tile_sets[y][1], len(tile_sets[y][0]))

        def gather_cell(c, carry):
            x, y, z = cell_of(c)
            index = jnp.maximum(idxb[c], 0)
            offset = lax.shift_right_logical(index, 7)
            atom = jnp.bitwise_and(index, 127)
            picked = [jnp.zeros((8, ATOMS), jnp.float32) for _ in range(4)]
            for k, (a, b, d) in enumerate(STEPS):
                here = offset == k
                for f in range(4):
                    row = jnp.broadcast_to(
                        ext[x + 1 + a, y + 1 + b, z + 1 + d, f : f + 1, :], (8, ATOMS)
                    )
                    got = jnp.take_along_axis(row, atom, axis=1, mode="promise_in_bounds")
                    picked[f] = jnp.where(here, got, picked[f])
            sx = (offset >= 9).astype(jnp.int32) + (offset >= 18).astype(jnp.int32)
            rest = offset - 9 * sx
            sy = (rest >= 3).astype(jnp.int32) + (rest >= 6).astype(jnp.int32)
            sz = rest - 3 * sy
            for f, step in enumerate((sx, sy, sz)):
                shift = (step - 1).astype(jnp.float32) * cutoff
                own = ext[x + 1, y + 1, z + 1, f : f + 1, :]
                vec = picked[f] + shift - own
                for s in range(8):
                    bv[f, s, pl.ds(c, 1), :] = vec[s : s + 1, :]
            radius = lookup(picked[3], radius_table)
            for s in range(8):
                bv[3, s, pl.ds(c, 1), :] = radius[s : s + 1, :]
                gb[s, pl.ds(c, 1), :] = jnp.where(idxb[c, s : s + 1, :] >= 0, 1.0, 0.0)
            return carry

        def excess_damping():
            radius_own = lookup(kind_own, radius_table)
            excess = -lookup(kind_own, valence_table)
            for s in range(NBOND):
                vec = [bv[f, s, 0:cells, :] for f in range(3)]
                span = radius_own + bv[3, s, 0:cells, :]
                raw = gb[s, 0:cells, :] * jnp.exp(order_rate * dot3(vec, vec) / (span * span))
                raws[s, 0:cells, :] = raw
                excess = excess + raw
            g_here = 2.0 / (1.0 + jnp.exp(excess))
            for number, (x, y, z) in enumerate(cell_list):
                gext[x + 1, y + 1, z + 1, 0:1, :] = g_here[number : number + 1, :]
            return g_here

        scale = coulomb / cutoff

        def products():
            turned = jnp.transpose(ycol[...])
            return (scale * turned[0:cells, :], scale * turned[16 : 16 + cells, :])

        def apply_part(number, side):
            for y in range(cy):
                tiles = tile_sets[y][side]
                base = side * len(tile_sets[y][0])

                def cell(xz, carry):
                    x = xz // cz
                    z = lax.rem(xz, cz)
                    c = (x * cy + y) * cz + z

                    def rows(r, inner):
                        at = pl.multiple_of(r * ROWS, ROWS)
                        first = jnp.zeros((ROWS, ATOMS), jnp.float32)
                        second = jnp.zeros((ROWS, ATOMS), jnp.float32)
                        for slot, (i, j, k) in enumerate(tiles):
                            ex = (cx + 1) * x if i is None else i
                            ez = (cz + 1) * z if k is None else k
                            value = kbuf[c, r, base + slot]
                            first = first + value * vext[number, ex, j, ez, 0:1, :]
                            second = second + value * vext[number, ex, j, ez, 1:2, :]
                        keep_sums(at, c, first, second)
                        return inner

                    return lax.fori_loop(0, ATOMS // ROWS, rows, carry)

                lax.fori_loop(0, cx * cz, cell, 0)

        def apply_own(number):
            ycol[...] = jnp.zeros((ATOMS, ATOMS), jnp.float32)
            apply_part(number, 0)

        def apply_ghost(number):
            apply_part(number, 1)
            return products()

        def place(number, first, second):
            for at, (x, y, z) in enumerate(cell_list):
                vext[number, x + 1, y + 1, z + 1, 0:1, :] = first[at : at + 1, :]
                vext[number, x + 1, y + 1, z + 1, 1:2, :] = second[at : at + 1, :]
            return halo(vext.at[number], vec_send.at[number], vec_recv.at[number])

        def reduce_start(number, values):
            for at in range(8):
                if at < len(values):
                    row = jnp.sum(values[at], axis=0, keepdims=True)
                else:
                    row = jnp.zeros((1, ATOMS), jnp.float32)
                ar_send[number, at : at + 1, :] = row
            copies = []
            for slot, (i, j) in enumerate(plane):
                copies.append(
                    pltpu.make_async_remote_copy(
                        src_ref=ar_send.at[number],
                        dst_ref=ar_plane.at[number, slot],
                        send_sem=plane_send.at[number, slot],
                        recv_sem=plane_recv.at[number, slot],
                        device_id=device(i, j, 0),
                        device_id_type=MESH,
                    )
                )
            for copy in copies:
                copy.start()
            return copies

        def reduce_next(number, copies):
            landed(copies)
            total = ar_send[number]
            for slot in range(len(plane)):
                total = total + ar_plane[number, slot]
            ar_mid[number] = total
            after = []
            for slot, k in enumerate(line):
                after.append(
                    pltpu.make_async_remote_copy(
                        src_ref=ar_mid.at[number],
                        dst_ref=ar_line.at[number, slot],
                        send_sem=line_send.at[number, slot],
                        recv_sem=line_recv.at[number, slot],
                        device_id=device(0, 0, k),
                        device_id_type=MESH,
                    )
                )
            for copy in after:
                copy.start()
            return after

        def reduce_end(number, copies):
            landed(copies)
            total = ar_mid[number]
            for slot in range(len(line)):
                total = total + ar_line[number, slot]
            summed = jnp.broadcast_to(jnp.sum(total, axis=1, keepdims=True), (8, ATOMS))
            return [summed[at : at + 1, :] for at in range(8)]

        chi = lookup(kind_own, negativity_table)
        kchi, ksum = products()
        diagonal = lookup(kind_own, hardness_table) + ksum
        ws = -(diagonal * chi + kchi)
        wt = -(diagonal + ksum)
        vec0 = place(0, ws, wt)
        red0 = reduce_start(0, [chi * chi, -chi * ws, ws * ws, -wt, wt * wt, chi])
        apply_own(0)
        red0b = reduce_next(0, red0)
        lax.fori_loop(0, cells // 2, gather_cell, 0)
        landed(vec0)
        k2s, k2t = apply_ghost(0)
        hws = diagonal * ws + k2s
        hwt = diagonal * wt + k2t
        rr0s, pq0s, qq0s, pq0t, qq0t, chi_sum, _, _ = reduce_end(0, red0b)
        rr0t = jnp.full((1, ATOMS), float(total_atoms), jnp.float32)
        a0s, a0t = rr0s / pq0s, rr0t / pq0t
        b0s = a0s * a0s * qq0s / rr0s - 1.0
        b0t = a0t * a0t * qq0t / rr0t - 1.0
        r1s, r1t = -chi - a0s * ws, -1.0 - a0t * wt
        d1s, d1t = r1s - b0s * chi, r1t - b0t
        hr1s, hr1t = ws - a0s * hws, wt - a0t * hwt
        q1s, q1t = hr1s + b0s * ws, hr1t + b0t * wt
        vec1 = place(1, q1s, q1t)
        red1 = reduce_start(
            1, [r1s * r1s, d1s * q1s, q1s * q1s, d1s, r1t * r1t, d1t * q1t, q1t * q1t, d1t]
        )
        apply_own(1)
        red1b = reduce_next(1, red1)
        lax.fori_loop(cells // 2, cells, gather_cell, 0)
        g_here = excess_damping()
        g_copies = halo(gext, g_send, g_recv)
        landed(vec1)
        k3s, k3t = apply_ghost(1)
        hq1s = diagonal * q1s + k3s
        hq1t = diagonal * q1t + k3t
        rr1s, pq1s, qq1s, d1s_sum, rr1t, pq1t, qq1t, d1t_sum = reduce_end(1, red1b)
        a1s, a1t = rr1s / pq1s, rr1t / pq1t
        b1s = a1s * a1s * qq1s / rr1s - 1.0
        b1t = a1t * a1t * qq1t / rr1t - 1.0
        r2s, r2t = r1s - a1s * q1s, r1t - a1t * q1t
        d2s, d2t = r2s + b1s * d1s, r2t + b1t * d1t
        q2s = hr1s - a1s * hq1s + b1s * q1s
        q2t = hr1t - a1t * hq1t + b1t * q1t
        red2 = reduce_start(2, [r2s * r2s, d2s * q2s, d2s, r2t * r2t, d2t * q2t, d2t])

        landed(g_copies)

        def gather_damping(c, carry):
            x, y, z = cell_of(c)
            index = jnp.maximum(idxb[c], 0)
            offset = lax.shift_right_logical(index, 7)
            atom = jnp.bitwise_and(index, 127)
            picked = jnp.zeros((8, ATOMS), jnp.float32)
            for k, (a, b, d) in enumerate(STEPS):
                row = jnp.broadcast_to(gext[x + 1 + a, y + 1 + b, z + 1 + d, 0:1, :], (8, ATOMS))
                got = jnp.take_along_axis(row, atom, axis=1, mode="promise_in_bounds")
                picked = jnp.where(offset == k, got, picked)
            for s in range(NBOND):
                raws[s, pl.ds(c, 1), :] = raws[s, pl.ds(c, 1), :] * picked[s : s + 1, :]
            return carry

        lax.fori_loop(0, cells, gather_damping, 0)
        red2b = reduce_next(2, red2)

        def spread_out(ref, lead, value):
            for x in range(cx):
                for y in range(cy):
                    at = (x * cy + y) * cz
                    ref[(*lead, x, y)] = value[at : at + cz, :]

        order = []
        for s in range(NBOND):
            order.append(raws[s, 0:cells, :] * g_here)
            spread_out(orders_out, (s,), order[s])
        bend = lookup(kind_own, bend_table)
        rest = lookup(kind_own, cosine_table)
        twist = lookup(kind_own, twist_table)
        vecs = [[bv[f, s, 0:cells, :] for f in range(3)] for s in range(NBOND)]
        radii = [bv[3, s, 0:cells, :] for s in range(NBOND)]
        inv = [lax.rsqrt(dot3(vecs[s], vecs[s]) + 1.0) for s in range(NBOND)]
        force = [[jnp.zeros((cells, ATOMS), jnp.float32) for _ in range(3)] for _ in range(NBOND)]
        for a in range(NBOND):
            for b in range(a + 1, NBOND):
                both = inv[a] * inv[b]
                cosine = dot3(vecs[a], vecs[b]) * both
                pull = -2.0 * bend * (order[a] * order[b]) * (cosine - rest)
                cross_part = pull * both
                own_part = pull * cosine
                pa = own_part * (inv[a] * inv[a])
                pb = own_part * (inv[b] * inv[b])
                for f in range(3):
                    force[a][f] = force[a][f] + (cross_part * vecs[b][f] - pa * vecs[a][f])
                    force[b][f] = force[b][f] + (cross_part * vecs[a][f] - pb * vecs[b][f])

        def choose(options, slot):
            out = options[0]
            for s in range(1, NBOND):
                out = jnp.where(slot == s, options[s], out)
            return out

        for t in range(NTOR):
            first = torc[0, t, 0:cells, :]
            second = torc[1, t, 0:cells, :]
            vj = [choose([vecs[s][f] for s in range(NBOND)], first) for f in range(3)]
            vk = [choose([vecs[s][f] for s in range(NBOND)], second) for f in range(3)]
            weight = choose(order, first) * choose(order, second)
            span = choose(radii, second) + bv[3, NBOND + t, 0:cells, :]
            far = [bv[f, NBOND + t, 0:cells, :] for f in range(3)]
            u = [far[f] - vk[f] for f in range(3)]
            weight = weight * jnp.exp(order_rate * dot3(u, u) / (span * span))
            weight = weight * gb[NBOND + t, 0:cells, :]
            n1 = cross3(vj, vk)
            n2 = cross3(vk, u)
            i1 = lax.rsqrt(dot3(n1, n1) + 1.0)
            i2 = lax.rsqrt(dot3(n2, n2) + 1.0)
            both = i1 * i2
            cosine = dot3(n1, n2) * both
            pull = 2.0 * twist * weight * cosine
            cross_part = pull * both
            own1 = pull * cosine * (i1 * i1)
            own2 = pull * cosine * (i2 * i2)
            p1 = [cross_part * n2[f] - own1 * n1[f] for f in range(3)]
            p2 = [cross_part * n1[f] - own2 * n2[f] for f in range(3)]
            fj = cross3(vk, p1)
            fw = cross3(p2, vk)
            part1 = cross3(p1, vj)
            part2 = cross3(u, p2)
            fk = [part1[f] + part2[f] - fw[f] for f in range(3)]
            for s in range(NBOND):
                for f in range(3):
                    force[s][f] = (
                        force[s][f]
                        + jnp.where(first == s, fj[f], 0.0)
                        + jnp.where(second == s, fk[f], 0.0)
                    )
            for f in range(3):
                spread_out(fforce, (f, t), fw[f])
        for s in range(NBOND):
            for f in range(3):
                spread_out(bforce, (f, s), force[s][f])

        rr2s, pq2s, d2s_sum, rr2t, pq2t, d2t_sum, _, _ = reduce_end(2, red2b)
        a2s, a2t = rr2s / pq2s, rr2t / pq2t
        solve_s = -a0s * chi + a1s * d1s + a2s * d2s
        solve_t = -a0t + a1t * d1t + a2t * d2t
        sum_s = -a0s * chi_sum + a1s * d1s_sum + a2s * d2s_sum
        sum_t = -a0t * rr0t + a1t * d1t_sum + a2t * d2t_sum
        result = charge_unit * (solve_s - (sum_s / sum_t) * solve_t)
        spread_out(charges, (), result)

        for copies in (pos_copies, g_copies, vec0, vec1, red0, red0b, red1, red1b, red2, red2b):
            finish(copies)

    def scratch():
        big = (cx + 2, cy + 2, cz + 2)
        sides = len(SIDES)
        dma = pltpu.SemaphoreType.DMA
        f32 = jnp.float32
        return [
            pltpu.VMEM((3, *block, ATOMS), f32),
            pltpu.VMEM((*block, ATOMS), jnp.int32),
            pltpu.VMEM((NBOND, *block, ATOMS), jnp.int32),
            pltpu.VMEM((2, NTOR, *block, ATOMS), jnp.int32),
            pltpu.VMEM((NTOR, *block, ATOMS), jnp.int32),
            dma((5,)),
            pltpu.VMEM((*big, 4, ATOMS), f32),
            pltpu.VMEM((*big, 2, ATOMS), f32),
            pltpu.VMEM((*big, DEPTH, ATOMS), jnp.bfloat16),
            pltpu.VMEM((cells, ATOMS, DEPTH), jnp.bfloat16),
            pltpu.VMEM((cells, ATOMS, ATOMS), f32),
            pltpu.VMEM((cells, ATOMS // ROWS, 27, ROWS, ATOMS), f32),
            pltpu.VMEM((ATOMS, ATOMS), f32),
            pltpu.VMEM((2, *big, 2, ATOMS), f32),
            pltpu.VMEM((*big, 1, ATOMS), f32),
            pltpu.VMEM((cells, 8, ATOMS), jnp.int32),
            pltpu.VMEM((4, 8, 16, ATOMS), f32),
            pltpu.VMEM((8, 16, ATOMS), f32),
            pltpu.VMEM((16, ATOMS), jnp.int32),
            pltpu.VMEM((2, NTOR, 16, ATOMS), jnp.int32),
            pltpu.VMEM((NBOND, 16, ATOMS), f32),
            pltpu.VMEM((3, 8, ATOMS), f32),
            pltpu.VMEM((3, len(plane), 8, ATOMS), f32),
            pltpu.VMEM((3, 8, ATOMS), f32),
            pltpu.VMEM((3, len(line), 8, ATOMS), f32),
            dma((sides,)), dma((sides,)),
            dma((2, sides)), dma((2, sides)),
            dma((sides,)), dma((sides,)),
            dma((3, len(plane))), dma((3, len(plane))),
            dma((3, len(line))), dma((3, len(line))),
        ]

    return kernel, scratch()


def solution(mesh):
    sizes = (mesh.shape["gx"], mesh.shape["gy"], mesh.shape["gz"])

    def on_device(positions, atom_kinds, bond_partners, torsion_bonds, torsion_far):
        block = positions.shape[1:4]
        total = ATOMS
        for count, size in zip(block, sizes):
            total *= count * size
        kernel, scratch = make_kernel(sizes, block, total)
        f32 = jnp.float32
        whole = pl.BlockSpec(memory_space=pltpu.VMEM)
        return pl.pallas_call(
            kernel,
            out_shape=(
                jax.ShapeDtypeStruct((*block, ATOMS), f32),
                jax.ShapeDtypeStruct((NBOND, *block, ATOMS), f32),
                jax.ShapeDtypeStruct((3, NBOND, *block, ATOMS), f32),
                jax.ShapeDtypeStruct((3, NTOR, *block, ATOMS), f32),
            ),
            in_specs=[pl.BlockSpec(memory_space=pltpu.MemorySpace.HBM)] * 5,
            out_specs=(whole,) * 4,
            scratch_shapes=scratch,
            compiler_params=pltpu.CompilerParams(
                collective_id=0, has_side_effects=True, vmem_limit_bytes=48 * 1024 * 1024
            ),
            name="reax_step",
        )(positions, atom_kinds, bond_partners, torsion_bonds, torsion_far)

    placed = (
        P(None, "gx", "gy", "gz", None),
        P("gx", "gy", "gz", None),
        P(None, "gx", "gy", "gz", None),
        P(None, None, "gx", "gy", "gz", None),
        P(None, "gx", "gy", "gz", None),
    )
    return jax.shard_map(
        on_device,
        mesh=mesh,
        in_specs=placed,
        out_specs=(
            P("gx", "gy", "gz", None),
            P(None, "gx", "gy", "gz", None),
            P(None, None, "gx", "gy", "gz", None),
            P(None, None, "gx", "gy", "gz", None),
        ),
        check_vma=False,
    )
```

```python
import jax
import jax.numpy as jnp
from jax import lax
from jax.experimental import pallas as pl
from jax.experimental.pallas import tpu as pltpu
from jax.sharding import PartitionSpec as P

MESH = pl.DeviceIdType.MESH

ATOMS = 128
NBOND = 4
NTOR = 4
cutoff = 10.0
coulomb = 14.4
order_rate = -0.3
charge_unit = 100.0
shield_table = (0.82, 1.08, 0.75)
negativity_table = (4.7, 8.5, 5.3)
hardness_table = (6.0, 7.2, 7.4)
radius_table = (5.0, 4.0, 3.0)
valence_table = (4.0, 2.0, 1.0)
bend_table = (40.0, 30.0, 10.0)
cosine_table = (-0.3333, -0.25, -0.5)
twist_table = (20.0, 12.0, 6.0)

STEPS = [(a, b, c) for a in (-1, 0, 1) for b in (-1, 0, 1) for c in (-1, 0, 1)]
SIDES = [s for s in STEPS if s != (0, 0, 0)]
ROWS = 128
TAPER_GRID = 2.0**-22
TAPER_42 = round(4.2 / (2 * TAPER_GRID)) * (2 * TAPER_GRID)
TAPER_05 = round(0.05 / TAPER_GRID) * TAPER_GRID
TAPER = (TAPER_42, TAPER_42 - 2.5 + TAPER_05, TAPER_05)
DEPTH = 64


def lookup(kind, table):
    return jnp.where(kind == 0, table[0], jnp.where(kind == 1, table[1], table[2])).astype(jnp.float32)


def send_range(step, size):
    if step > 0:
        return (size, 1)
    if step < 0:
        return (1, 1)
    return (1, size)


def land_range(step, size):
    if step > 0:
        return (0, 1)
    if step < 0:
        return (size + 1, 1)
    return (1, size)


def add3(a, b):
    return [p + q for p, q in zip(a, b)]


def dot3(a, b):
    return a[0] * b[0] + a[1] * b[1] + a[2] * b[2]


def cross3(a, b):
    return [
        a[1] * b[2] - a[2] * b[1],
        a[2] * b[0] - a[0] * b[2],
        a[0] * b[1] - a[1] * b[0],
    ]


def make_kernel(sizes, block, total_atoms):
    nx, ny, nz = sizes
    cx, cy, cz = block
    cells = cx * cy * cz
    cell_list = [(x, y, z) for x in range(cx) for y in range(cy) for z in range(cz)]
    px, pz = 2, nz // 2
    flat = [
        (i, j, k) for i in range(px) for j in range(ny) for k in range(pz) if (i, j, k) != (0, 0, 0)
    ]
    line = [(i, k) for i in range(nx // px) for k in range(nz // pz) if (i, k) != (0, 0)]

    def kernel(
        pos_in, kinds_in, bp_in, tb_in, tf_in,
        charges, orders_out, bforce, fforce,
        pos, kinds, bp, tb, tf, in_sems,
        ext, dext, brhs, alhs, colg, kbuf, ycol, vext, gext, idxb, bv, gb, kindc, torc, raws,
        ar_send, ar_flat, ar_mid, ar_line,
        pos_send, pos_recv, vec_send, vec_recv, g_send, g_recv,
        flat_send, flat_recv, line_send, line_recv,
    ):
        ix = lax.axis_index("gx")
        iy = lax.axis_index("gy")
        iz = lax.axis_index("gz")

        def device(a, b, c):
            return (lax.rem(ix + a + nx, nx), lax.rem(iy + b + ny, ny), lax.rem(iz + c + nz, nz))

        fetches = [
            pltpu.make_async_copy(source, target, in_sems.at[number])
            for number, (source, target) in enumerate(
                ((pos_in, pos), (kinds_in, kinds), (bp_in, bp), (tf_in, tf), (tb_in, tb))
            )
        ]
        for fetch in fetches:
            fetch.start()
        def flat_device(i, j, k):
            return (
                (ix // px) * px + lax.rem(lax.rem(ix, px) + i, px),
                lax.rem(iy + j, ny),
                (iz // pz) * pz + lax.rem(lax.rem(iz, pz) + k, pz),
            )

        def line_device(i, k):
            return (
                lax.rem(ix // px + i, nx // px) * px + lax.rem(ix, px),
                iy,
                lax.rem(iz // pz + k, nz // pz) * pz + lax.rem(iz, pz),
            )

        greeted = [device(*side) for side in SIDES]
        greeted += [flat_device(*peer) for peer in flat] + [line_device(*peer) for peer in line]
        barrier = pltpu.get_barrier_semaphore()
        for peer in greeted:
            pl.semaphore_signal(barrier, inc=1, device_id=peer, device_id_type=MESH)

        def halo(ref, send, recv):
            copies = []
            for number, (a, b, c) in enumerate(SIDES):
                sx, sy, sz = send_range(a, cx), send_range(b, cy), send_range(c, cz)
                lx, ly, lz = land_range(a, cx), land_range(b, cy), land_range(c, cz)
                copies.append(
                    pltpu.make_async_remote_copy(
                        src_ref=ref.at[pl.ds(*sx), pl.ds(*sy), pl.ds(*sz)],
                        dst_ref=ref.at[pl.ds(*lx), pl.ds(*ly), pl.ds(*lz)],
                        send_sem=send.at[number],
                        recv_sem=recv.at[number],
                        device_id=device(a, b, c),
                        device_id_type=MESH,
                    )
                )
            for copy, side in zip(copies, SIDES):
                if side[2] != 0:
                    copy.start()
            for copy, side in zip(copies, SIDES):
                if side[2] == 0:
                    copy.start()
            return copies

        def landed(copies):
            for copy in copies:
                copy.wait_recv()

        def finish(copies):
            for copy in copies:
                copy.wait_send()

        fetches[0].wait()
        fetches[1].wait()
        for x, y, z in cell_list:
            for f in range(3):
                ext[x + 1, y + 1, z + 1, f : f + 1, :] = pos[f, x, y, z : z + 1, :]
            ext[x + 1, y + 1, z + 1, 3:4, :] = kinds[x, y, z : z + 1, :].astype(jnp.float32)
        for x in range(cx):
            for y in range(cy):
                at = (x * cy + y) * cz
                kindc[at : at + cz, :] = kinds[x, y]
        kind_own = kindc[0:cells, :]

        def cell_of(c):
            return (c // (cy * cz), lax.rem(c // cz, cy), lax.rem(c, cz))

        shield_root = [float((cutoff * g) ** -1.5) for g in shield_table]
        row8 = lax.broadcasted_iota(jnp.int32, (8, ATOMS), 0)
        ones3 = jnp.where(row8 < 3, 1.0, 0.0)

        def narrow(value):
            return value.astype(jnp.bfloat16).astype(jnp.float32)

        def by_row(values):
            out = jnp.zeros((8, ATOMS), jnp.float32)
            for at, value in enumerate(values):
                if value is not None:
                    out = jnp.where(row8 == at, value, out)
            return out

        def derive(x, y, z, number):
            middle = (x - 0.5 * (cx + 2), y - 0.5 * (cy + 2), z - 0.5 * (cz + 2))
            place_at = by_row(
                [
                    ext[x, y, z, f : f + 1, :] * (1.0 / cutoff) + jnp.float32(middle[f])
                    for f in range(3)
                ]
            )
            grid = jnp.round(place_at * 64.0) * (1.0 / 64.0)
            rest = place_at - grid
            mid = narrow(rest)
            low = rest - mid
            grid_sq = jnp.sum(grid * grid, axis=0, keepdims=True)
            rest_sq = jnp.sum(rest * (2.0 * grid + rest), axis=0, keepdims=True)
            grid_1 = jnp.round(grid_sq * 16.0) * (1.0 / 16.0)
            grid_2 = grid_sq - grid_1
            rest_1 = narrow(rest_sq)
            rest_2 = narrow(rest_sq - rest_1)
            rest_3 = (rest_sq - rest_1) - rest_2
            heads = by_row([grid_1, grid_2, 1.0, 1.0, rest_1, rest_2, rest_3])
            tile = jnp.concatenate([grid, heads, ones3, mid, low, grid, grid, mid], axis=0)
            brhs[x, y, z] = tile.astype(jnp.bfloat16)
            kind = ext[x, y, z, 3:4, :]
            dext[x, y, z, 0:1, :] = lookup(kind, shield_root)
            dext[x, y, z, 1:2, :] = lookup(kind, negativity_table)
            if number is not None:
                heads = by_row([1.0, 1.0, grid_1, grid_2, 1.0, 1.0, 1.0])
                tails = by_row([rest_1, rest_2, rest_3])
                left = jnp.concatenate(
                    [
                        -2.0 * grid, heads, tails, -2.0 * grid,
                        -2.0 * grid, -2.0 * mid, -2.0 * low, -2.0 * mid,
                    ],
                    axis=0,
                )
                alhs[number] = jnp.transpose(left).astype(jnp.bfloat16)

        def derive_own(n, carry):
            x = n // cy
            y = lax.rem(n, cy)
            for z in range(cz):
                derive(x + 1, y + 1, z + 1, (x * cy + y) * cz + z)
            return carry

        lax.fori_loop(0, cx * cy, derive_own, 0)

        ycol[...] = jnp.zeros((ATOMS, ATOMS), jnp.float32)
        ycol[0:cells, :] = lookup(kind_own, shield_root)
        flipped = jnp.transpose(ycol[...])
        for number in range(cells):
            colg[number] = jnp.broadcast_to(flipped[:, number : number + 1], (ATOMS, ATOMS))
        ycol[...] = jnp.zeros((ATOMS, ATOMS), jnp.float32)

        def tiles_of(y):
            every = [
                (i, j, k) for j in (y, y + 1, y + 2) for i in (1, 2, None) for k in (1, 2, None)
            ]
            own = [t for t in every if t[0] and t[2] and 1 <= t[1] <= cy]
            far = [t for t in every if t[2] is None]
            return own, [t for t in every if t not in own + far], far

        row_of = lax.broadcasted_iota(jnp.int32, (ROWS, ATOMS), 0)
        lane_of = lax.broadcasted_iota(jnp.int32, (ROWS, ATOMS), 1)

        def keep_sums(at, c, first, second):
            one = jnp.sum(first, axis=1, keepdims=True)
            two = jnp.sum(second, axis=1, keepdims=True)
            ycol[pl.ds(at, ROWS), :] = ycol[pl.ds(at, ROWS), :] + jnp.where(
                lane_of == c, one, jnp.where(lane_of == c + 16, two, 0.0)
            )

        def coupling_part(y, tiles, base):
            def cell(xz, carry):
                x = xz // cz
                z = lax.rem(xz, cz)
                c = (x * cy + y) * cz + z

                def rows(r, inner):
                    at = pl.multiple_of(r * ROWS, ROWS)
                    left = alhs[c, pl.ds(at, ROWS), :]
                    own_g = colg[c, pl.ds(at, ROWS), :]
                    sum_one = jnp.zeros((ROWS, ATOMS), jnp.float32)
                    sum_chi = jnp.zeros((ROWS, ATOMS), jnp.float32)
                    for slot, (i, j, k) in enumerate(tiles):
                        ex = (cx + 1) * x if i is None else i
                        ez = (cz + 1) * z if k is None else k
                        near_g = dext[ex, j, ez, 0:1, :]
                        near_chi = dext[ex, j, ez, 1:2, :]
                        square = jnp.dot(
                            left, brhs[ex, j, ez], preferred_element_type=jnp.float32
                        )
                        q = jnp.minimum(jnp.maximum(square, 1e-30), 1.0)
                        u = q * lax.rsqrt(q)
                        inv = jnp.exp2(lax.log2(u * q + own_g * near_g) * (-1.0 / 3.0))
                        inner_part = (u - 3.5) * q + (u * TAPER[0] - TAPER[1])
                        value = (inner_part * (q * q) + TAPER[2]) * inv
                        if i and k and j == y + 1:
                            same = jnp.logical_and(x + 1 == i, z + 1 == k)
                            value = jnp.where(
                                row_of + jnp.where(same, at, -ATOMS) == lane_of, 0.0, value
                            )
                        kbuf[c, r, base + slot] = value
                        sum_one = sum_one + value
                        sum_chi = sum_chi + value * near_chi
                    keep_sums(at, c, sum_chi, sum_one)
                    return inner

                return lax.fori_loop(0, ATOMS // ROWS, rows, carry)

            lax.fori_loop(0, cx * cz, cell, 0)

        tile_sets = [tiles_of(y) for y in range(cy)]
        coupling_part(0, tile_sets[0][0], 0)
        pl.semaphore_wait(barrier, len(greeted))
        pos_copies = halo(ext, pos_send, pos_recv)
        for y in range(1, cy):
            coupling_part(y, tile_sets[y][0], 0)

        for fetch in fetches[2:]:
            fetch.wait()
        for x in range(cx):
            for y in range(cy):
                at = (x * cy + y) * cz
                for s in range(NTOR):
                    torc[0, s, at : at + cz, :] = tb[0, s, x, y]
                    torc[1, s, at : at + cz, :] = tb[1, s, x, y]
        for number, (x, y, z) in enumerate(cell_list):
            for s in range(NBOND):
                idxb[number, s : s + 1, :] = bp[s, x, y, z : z + 1, :]
                idxb[number, NBOND + s : NBOND + s + 1, :] = tf[s, x, y, z : z + 1, :]

        landed(pos_copies)

        def derive_x(n, carry):
            x = (cx + 1) * (n // (cy + 2))
            for z in range(cz + 2):
                derive(x, lax.rem(n, cy + 2), z, None)
            return carry

        def derive_y(n, carry):
            for z in range(cz + 2):
                derive(n // 2 + 1, (cy + 1) * lax.rem(n, 2), z, None)
            return carry

        def derive_z(n, carry):
            for z in (0, cz + 1):
                derive(n // cy + 1, lax.rem(n, cy) + 1, z, None)
            return carry

        lax.fori_loop(0, 2 * (cy + 2), derive_x, 0)
        lax.fori_loop(0, 2 * cx, derive_y, 0)
        lax.fori_loop(0, cx * cy, derive_z, 0)
        for y in range(cy):
            coupling_part(y, tile_sets[y][1] + tile_sets[y][2], len(tile_sets[y][0]))

        def gather_cell(c, carry):
            x, y, z = cell_of(c)
            index = jnp.maximum(idxb[c], 0)
            offset = lax.shift_right_logical(index, 7)
            atom = jnp.bitwise_and(index, 127)
            picked = [jnp.zeros((8, ATOMS), jnp.float32) for _ in range(4)]
            around = ext.at[pl.ds(x, 3), pl.ds(y, 3), pl.ds(z, 3)]
            for k, (a, b, d) in enumerate(STEPS):
                here = offset == k
                for f in range(4):
                    row = jnp.broadcast_to(
                        around[1 + a, 1 + b, 1 + d, f : f + 1, :], (8, ATOMS)
                    )
                    got = jnp.take_along_axis(row, atom, axis=1, mode="promise_in_bounds")
                    picked[f] = jnp.where(here, got, picked[f])
            sx = (offset >= 9).astype(jnp.int32) + (offset >= 18).astype(jnp.int32)
            rest = offset - 9 * sx
            sy = (rest >= 3).astype(jnp.int32) + (rest >= 6).astype(jnp.int32)
            sz = rest - 3 * sy
            for f, step in enumerate((sx, sy, sz)):
                shift = (step - 1).astype(jnp.float32) * cutoff
                own = ext[x + 1, y + 1, z + 1, f : f + 1, :]
                vec = picked[f] + shift - own
                for s in range(8):
                    bv[f, s, pl.ds(c, 1), :] = vec[s : s + 1, :]
            radius = lookup(picked[3], radius_table)
            for s in range(8):
                bv[3, s, pl.ds(c, 1), :] = radius[s : s + 1, :]
                gb[s, pl.ds(c, 1), :] = jnp.where(idxb[c, s : s + 1, :] >= 0, 1.0, 0.0)
            return carry

        def excess_damping():
            radius_own = lookup(kind_own, radius_table)
            excess = -lookup(kind_own, valence_table)
            for s in range(NBOND):
                vec = [bv[f, s, 0:cells, :] for f in range(3)]
                span = radius_own + bv[3, s, 0:cells, :]
                raw = gb[s, 0:cells, :] * jnp.exp(order_rate * dot3(vec, vec) / (span * span))
                raws[s, 0:cells, :] = raw
                excess = excess + raw
            g_here = 2.0 / (1.0 + jnp.exp(excess))
            for number, (x, y, z) in enumerate(cell_list):
                gext[x + 1, y + 1, z + 1, 0:1, :] = g_here[number : number + 1, :]
            return g_here

        scale = 20.0 * coulomb / cutoff

        def products():
            turned = jnp.transpose(ycol[...])
            return (scale * turned[0:cells, :], scale * turned[16 : 16 + cells, :])

        def apply_part(number, side):
            for y in range(cy):
                tiles = tile_sets[y][side]
                base = sum(len(group) for group in tile_sets[y][:side])

                def cell(xz, carry):
                    x = xz // cz
                    z = lax.rem(xz, cz)
                    c = (x * cy + y) * cz + z

                    def rows(r, inner):
                        at = pl.multiple_of(r * ROWS, ROWS)
                        first = jnp.zeros((ROWS, ATOMS), jnp.float32)
                        second = jnp.zeros((ROWS, ATOMS), jnp.float32)
                        for slot, (i, j, k) in enumerate(tiles):
                            ex = (cx + 1) * x if i is None else i
                            ez = (cz + 1) * z if k is None else k
                            value = kbuf[c, r, base + slot]
                            first = first + value * vext[number, ex, j, ez, 0:1, :]
                            second = second + value * vext[number, ex, j, ez, 1:2, :]
                        keep_sums(at, c, first, second)
                        return inner

                    return lax.fori_loop(0, ATOMS // ROWS, rows, carry)

                lax.fori_loop(0, cx * cz, cell, 0)

        def apply_own(number):
            ycol[...] = jnp.zeros((ATOMS, ATOMS), jnp.float32)
            apply_part(number, 0)

        def apply_ghost(number, copies):
            landed([c for c, side in zip(copies, SIDES) if side[2] == 0])
            apply_part(number, 1)
            landed([c for c, side in zip(copies, SIDES) if side[2] != 0])
            apply_part(number, 2)
            return products()

        def place(number, first, second):
            for at, (x, y, z) in enumerate(cell_list):
                vext[number, x + 1, y + 1, z + 1, 0:1, :] = first[at : at + 1, :]
                vext[number, x + 1, y + 1, z + 1, 1:2, :] = second[at : at + 1, :]
            return halo(vext.at[number], vec_send.at[number], vec_recv.at[number])

        row8_lane = row8 == lax.broadcasted_iota(jnp.int32, (8, ATOMS), 1)

        def reduce_start(number, values):
            rows = by_row([jnp.sum(value, axis=0, keepdims=True) for value in values])
            rows = jnp.sum(rows, axis=1, keepdims=True)
            ar_send[number] = jnp.sum(jnp.where(row8_lane, rows, 0.0), axis=0, keepdims=True)
            copies = []
            for slot, peer in enumerate(flat):
                copies.append(
                    pltpu.make_async_remote_copy(
                        src_ref=ar_send.at[number],
                        dst_ref=ar_flat.at[number, slot],
                        send_sem=flat_send.at[number, slot],
                        recv_sem=flat_recv.at[number, slot],
                        device_id=flat_device(*peer),
                        device_id_type=MESH,
                    )
                )
            for copy in copies:
                copy.start()
            return copies

        def reduce_next(number, copies):
            landed(copies)
            parts = [ar_send[number]] + [ar_flat[number, slot] for slot in range(len(flat))]
            while len(parts) > 1:
                parts = [sum(parts[at : at + 2]) for at in range(0, len(parts), 2)]
            ar_mid[number] = parts[0]
            after = []
            for slot, peer in enumerate(line):
                after.append(
                    pltpu.make_async_remote_copy(
                        src_ref=ar_mid.at[number],
                        dst_ref=ar_line.at[number, slot],
                        send_sem=line_send.at[number, slot],
                        recv_sem=line_recv.at[number, slot],
                        device_id=line_device(*peer),
                        device_id_type=MESH,
                    )
                )
            for copy in after:
                copy.start()
            return after

        def reduce_end(number, copies):
            landed(copies)
            total = ar_mid[number]
            for slot in range(len(line)):
                total = total + ar_line[number, slot]
            return [jnp.broadcast_to(total[:, at : at + 1], (1, ATOMS)) for at in range(8)]

        chi = lookup(kind_own, negativity_table)
        kchi, ksum = products()
        diagonal = lookup(kind_own, hardness_table) + ksum
        ws = -(diagonal * chi + kchi)
        wt = -(diagonal + ksum)
        vec0 = place(0, ws, wt)
        red0 = reduce_start(0, [chi * chi, -chi * ws, ws * ws, -wt, wt * wt, chi])
        apply_own(0)
        red0b = reduce_next(0, red0)
        lax.fori_loop(0, cells // 2, gather_cell, 0)
        k2s, k2t = apply_ghost(0, vec0)
        hws = diagonal * ws + k2s
        hwt = diagonal * wt + k2t
        rr0s, pq0s, qq0s, pq0t, qq0t, chi_sum, _, _ = reduce_end(0, red0b)
        rr0t = jnp.full((1, ATOMS), float(total_atoms), jnp.float32)
        a0s, a0t = rr0s / pq0s, rr0t / pq0t
        b0s = a0s * a0s * qq0s / rr0s - 1.0
        b0t = a0t * a0t * qq0t / rr0t - 1.0
        r1s, r1t = -chi - a0s * ws, -1.0 - a0t * wt
        d1s, d1t = r1s - b0s * chi, r1t - b0t
        hr1s, hr1t = ws - a0s * hws, wt - a0t * hwt
        q1s, q1t = hr1s + b0s * ws, hr1t + b0t * wt
        vec1 = place(1, q1s, q1t)
        red1 = reduce_start(
            1, [r1s * r1s, d1s * q1s, q1s * q1s, d1s, r1t * r1t, d1t * q1t, q1t * q1t, d1t]
        )
        apply_own(1)
        red1b = reduce_next(1, red1)
        lax.fori_loop(cells // 2, cells, gather_cell, 0)
        g_here = excess_damping()
        g_copies = halo(gext, g_send, g_recv)
        k3s, k3t = apply_ghost(1, vec1)
        hq1s = diagonal * q1s + k3s
        hq1t = diagonal * q1t + k3t
        rr1s, pq1s, qq1s, d1s_sum, rr1t, pq1t, qq1t, d1t_sum = reduce_end(1, red1b)
        a1s, a1t = rr1s / pq1s, rr1t / pq1t
        b1s = a1s * a1s * qq1s / rr1s - 1.0
        b1t = a1t * a1t * qq1t / rr1t - 1.0
        r2s, r2t = r1s - a1s * q1s, r1t - a1t * q1t
        d2s, d2t = r2s + b1s * d1s, r2t + b1t * d1t
        q2s = hr1s - a1s * hq1s + b1s * q1s
        q2t = hr1t - a1t * hq1t + b1t * q1t
        red2 = reduce_start(2, [r2s * r2s, d2s * q2s, d2s, r2t * r2t, d2t * q2t, d2t])

        landed(g_copies)

        def gather_damping(c, carry):
            x, y, z = cell_of(c)
            index = jnp.maximum(idxb[c], 0)
            offset = lax.shift_right_logical(index, 7)
            atom = jnp.bitwise_and(index, 127)
            picked = jnp.zeros((8, ATOMS), jnp.float32)
            around = gext.at[pl.ds(x, 3), pl.ds(y, 3), pl.ds(z, 3)]
            for k, (a, b, d) in enumerate(STEPS):
                row = jnp.broadcast_to(around[1 + a, 1 + b, 1 + d, 0:1, :], (8, ATOMS))
                got = jnp.take_along_axis(row, atom, axis=1, mode="promise_in_bounds")
                picked = jnp.where(offset == k, got, picked)
            for s in range(NBOND):
                raws[s, pl.ds(c, 1), :] = raws[s, pl.ds(c, 1), :] * picked[s : s + 1, :]
            return carry

        lax.fori_loop(0, cells, gather_damping, 0)
        red2b = reduce_next(2, red2)

        def spread_out(ref, lead, value):
            for x in range(cx):
                for y in range(cy):
                    at = (x * cy + y) * cz
                    ref[(*lead, x, y)] = value[at : at + cz, :]

        order = []
        for s in range(NBOND):
            order.append(raws[s, 0:cells, :] * g_here)
            spread_out(orders_out, (s,), order[s])
        bend = lookup(kind_own, bend_table)
        rest = lookup(kind_own, cosine_table)
        twist = lookup(kind_own, twist_table)
        vecs = [[bv[f, s, 0:cells, :] for f in range(3)] for s in range(NBOND)]
        radii = [bv[3, s, 0:cells, :] for s in range(NBOND)]
        inv = [lax.rsqrt(dot3(vecs[s], vecs[s]) + 1.0) for s in range(NBOND)]
        force = [[jnp.zeros((cells, ATOMS), jnp.float32) for _ in range(3)] for _ in range(NBOND)]
        for a in range(NBOND):
            for b in range(a + 1, NBOND):
                both = inv[a] * inv[b]
                cosine = dot3(vecs[a], vecs[b]) * both
                pull = -2.0 * bend * (order[a] * order[b]) * (cosine - rest)
                cross_part = pull * both
                own_part = pull * cosine
                pa = own_part * (inv[a] * inv[a])
                pb = own_part * (inv[b] * inv[b])
                for f in range(3):
                    force[a][f] = force[a][f] + (cross_part * vecs[b][f] - pa * vecs[a][f])
                    force[b][f] = force[b][f] + (cross_part * vecs[a][f] - pb * vecs[b][f])

        def choose(options, slot):
            out = options[0]
            for s in range(1, NBOND):
                out = jnp.where(slot == s, options[s], out)
            return out

        for t in range(NTOR):
            first = torc[0, t, 0:cells, :]
            second = torc[1, t, 0:cells, :]
            vj = [choose([vecs[s][f] for s in range(NBOND)], first) for f in range(3)]
            vk = [choose([vecs[s][f] for s in range(NBOND)], second) for f in range(3)]
            weight = choose(order, first) * choose(order, second)
            span = choose(radii, second) + bv[3, NBOND + t, 0:cells, :]
            far = [bv[f, NBOND + t, 0:cells, :] for f in range(3)]
            u = [far[f] - vk[f] for f in range(3)]
            weight = weight * jnp.exp(order_rate * dot3(u, u) / (span * span))
            weight = weight * gb[NBOND + t, 0:cells, :]
            n1 = cross3(vj, vk)
            n2 = cross3(vk, u)
            i1 = lax.rsqrt(dot3(n1, n1) + 1.0)
            i2 = lax.rsqrt(dot3(n2, n2) + 1.0)
            both = i1 * i2
            cosine = dot3(n1, n2) * both
            pull = 2.0 * twist * weight * cosine
            cross_part = pull * both
            own1 = pull * cosine * (i1 * i1)
            own2 = pull * cosine * (i2 * i2)
            p1 = [cross_part * n2[f] - own1 * n1[f] for f in range(3)]
            p2 = [cross_part * n1[f] - own2 * n2[f] for f in range(3)]
            fj = cross3(vk, p1)
            fw = cross3(p2, vk)
            part1 = cross3(p1, vj)
            part2 = cross3(u, p2)
            fk = [part1[f] + part2[f] - fw[f] for f in range(3)]
            for s in range(NBOND):
                for f in range(3):
                    force[s][f] = (
                        force[s][f]
                        + jnp.where(first == s, fj[f], 0.0)
                        + jnp.where(second == s, fk[f], 0.0)
                    )
            for f in range(3):
                spread_out(fforce, (f, t), fw[f])
        for s in range(NBOND):
            for f in range(3):
                spread_out(bforce, (f, s), force[s][f])

        rr2s, pq2s, d2s_sum, rr2t, pq2t, d2t_sum, _, _ = reduce_end(2, red2b)
        a2s, a2t = rr2s / pq2s, rr2t / pq2t
        solve_s = -a0s * chi + a1s * d1s + a2s * d2s
        solve_t = -a0t + a1t * d1t + a2t * d2t
        sum_s = -a0s * chi_sum + a1s * d1s_sum + a2s * d2s_sum
        sum_t = -a0t * rr0t + a1t * d1t_sum + a2t * d2t_sum
        result = charge_unit * (solve_s - (sum_s / sum_t) * solve_t)
        spread_out(charges, (), result)

        for copies in (pos_copies, g_copies, vec0, vec1, red0, red0b, red1, red1b, red2, red2b):
            finish(copies)

    def scratch():
        big = (cx + 2, cy + 2, cz + 2)
        sides = len(SIDES)
        dma = pltpu.SemaphoreType.DMA
        f32 = jnp.float32
        return [
            pltpu.VMEM((3, *block, ATOMS), f32),
            pltpu.VMEM((*block, ATOMS), jnp.int32),
            pltpu.VMEM((NBOND, *block, ATOMS), jnp.int32),
            pltpu.VMEM((2, NTOR, *block, ATOMS), jnp.int32),
            pltpu.VMEM((NTOR, *block, ATOMS), jnp.int32),
            dma((5,)),
            pltpu.VMEM((*big, 4, ATOMS), f32),
            pltpu.VMEM((*big, 2, ATOMS), f32),
            pltpu.VMEM((*big, DEPTH, ATOMS), jnp.bfloat16),
            pltpu.VMEM((cells, ATOMS, DEPTH), jnp.bfloat16),
            pltpu.VMEM((cells, ATOMS, ATOMS), f32),
            pltpu.VMEM((cells, ATOMS // ROWS, 27, ROWS, ATOMS), f32),
            pltpu.VMEM((ATOMS, ATOMS), f32),
            pltpu.VMEM((2, *big, 2, ATOMS), f32),
            pltpu.VMEM((*big, 1, ATOMS), f32),
            pltpu.VMEM((cells, 8, ATOMS), jnp.int32),
            pltpu.VMEM((4, 8, 16, ATOMS), f32),
            pltpu.VMEM((8, 16, ATOMS), f32),
            pltpu.VMEM((16, ATOMS), jnp.int32),
            pltpu.VMEM((2, NTOR, 16, ATOMS), jnp.int32),
            pltpu.VMEM((NBOND, 16, ATOMS), f32),
            pltpu.VMEM((3, 1, ATOMS), f32),
            pltpu.VMEM((3, len(flat), 1, ATOMS), f32),
            pltpu.VMEM((3, 1, ATOMS), f32),
            pltpu.VMEM((3, len(line), 1, ATOMS), f32),
            dma((sides,)), dma((sides,)),
            dma((2, sides)), dma((2, sides)),
            dma((sides,)), dma((sides,)),
            dma((3, len(flat))), dma((3, len(flat))),
            dma((3, len(line))), dma((3, len(line))),
        ]

    return kernel, scratch()


def write_out(*refs):
    sources, targets, sems = refs[:4], refs[4:8], refs[8]
    copies = [
        pltpu.make_async_copy(source, target, sems.at[number])
        for number, (source, target) in enumerate(zip(sources, targets))
    ]
    for copy in copies:
        copy.start()
    for copy in copies:
        copy.wait()


def solution(mesh):
    sizes = (mesh.shape["gx"], mesh.shape["gy"], mesh.shape["gz"])

    def on_device(positions, atom_kinds, bond_partners, torsion_bonds, torsion_far):
        block = positions.shape[1:4]
        total = ATOMS
        for count, size in zip(block, sizes):
            total *= count * size
        kernel, scratch = make_kernel(sizes, block, total)
        f32 = jnp.float32
        whole = pl.BlockSpec(memory_space=pltpu.VMEM)
        shapes = (
                jax.ShapeDtypeStruct((*block, ATOMS), f32),
                jax.ShapeDtypeStruct((NBOND, *block, ATOMS), f32),
                jax.ShapeDtypeStruct((3, NBOND, *block, ATOMS), f32),
                jax.ShapeDtypeStruct((3, NTOR, *block, ATOMS), f32),
            )
        arrays = (positions, atom_kinds, bond_partners, torsion_bonds, torsion_far)
        hbm = pl.BlockSpec(memory_space=pltpu.MemorySpace.HBM)
        results = pl.pallas_call(
            kernel,
            out_shape=shapes,
            in_specs=[hbm] * 5,
            out_specs=(whole,) * 4,
            scratch_shapes=scratch,
            compiler_params=pltpu.CompilerParams(
                collective_id=0, has_side_effects=True, vmem_limit_bytes=48 * 1024 * 1024
            ),
            name="reax_step",
        )(*[pltpu.with_memory_space_constraint(a, pltpu.MemorySpace.HBM) for a in arrays])
        return pl.pallas_call(
            write_out,
            out_shape=shapes,
            in_specs=[whole] * 4,
            out_specs=(hbm,) * 4,
            scratch_shapes=[pltpu.SemaphoreType.DMA((4,))],
            name="write_out",
        )(*[pltpu.with_memory_space_constraint(r, pltpu.MemorySpace.VMEM) for r in results])

    placed = (
        P(None, "gx", "gy", "gz", None),
        P("gx", "gy", "gz", None),
        P(None, "gx", "gy", "gz", None),
        P(None, None, "gx", "gy", "gz", None),
        P(None, "gx", "gy", "gz", None),
    )
    return jax.shard_map(
        on_device,
        mesh=mesh,
        in_specs=placed,
        out_specs=(
            P("gx", "gy", "gz", None),
            P(None, "gx", "gy", "gz", None),
            P(None, None, "gx", "gy", "gz", None),
            P(None, None, "gx", "gy", "gz", None),
        ),
        check_vma=False,
    )
```

```python
import jax
import jax.numpy as jnp
from jax import lax
from jax.experimental import pallas as pl
from jax.experimental.pallas import tpu as pltpu
from jax.sharding import PartitionSpec as P

MESH = pl.DeviceIdType.MESH

ATOMS = 128
NBOND = 4
NTOR = 4
cutoff = 10.0
coulomb = 14.4
order_rate = -0.3
charge_unit = 100.0
shield_table = (0.82, 1.08, 0.75)
negativity_table = (4.7, 8.5, 5.3)
hardness_table = (6.0, 7.2, 7.4)
radius_table = (5.0, 4.0, 3.0)
valence_table = (4.0, 2.0, 1.0)
bend_table = (40.0, 30.0, 10.0)
cosine_table = (-0.3333, -0.25, -0.5)
twist_table = (20.0, 12.0, 6.0)

STEPS = [(a, b, c) for a in (-1, 0, 1) for b in (-1, 0, 1) for c in (-1, 0, 1)]
SIDES = [s for s in STEPS if s != (0, 0, 0)]
ROWS = 128
TAPER_GRID = 2.0**-22
TAPER_42 = round(4.2 / (2 * TAPER_GRID)) * (2 * TAPER_GRID)
TAPER_05 = round(0.05 / TAPER_GRID) * TAPER_GRID
TAPER = (TAPER_42, TAPER_42 - 2.5 + TAPER_05, TAPER_05)
DEPTH = 64


def lookup(kind, table):
    return jnp.where(kind == 0, table[0], jnp.where(kind == 1, table[1], table[2])).astype(jnp.float32)


def send_range(step, size):
    if step > 0:
        return (size, 1)
    if step < 0:
        return (1, 1)
    return (1, size)


def land_range(step, size):
    if step > 0:
        return (0, 1)
    if step < 0:
        return (size + 1, 1)
    return (1, size)


def add3(a, b):
    return [p + q for p, q in zip(a, b)]


def dot3(a, b):
    return a[0] * b[0] + a[1] * b[1] + a[2] * b[2]


def cross3(a, b):
    return [
        a[1] * b[2] - a[2] * b[1],
        a[2] * b[0] - a[0] * b[2],
        a[0] * b[1] - a[1] * b[0],
    ]


def make_kernel(sizes, block, total_atoms):
    nx, ny, nz = sizes
    cx, cy, cz = block
    cells = cx * cy * cz
    cell_list = [(x, y, z) for x in range(cx) for y in range(cy) for z in range(cz)]
    px, pz = 2, nz // 2
    flat = [(i, j) for i in range(px) for j in range(ny) if (i, j) != (0, 0)]
    line = [
        (i, j, k)
        for i in range(nx // px)
        for j in range(nz // pz)
        for k in range(pz)
        if (i, j, k) != (0, 0, 0)
    ]

    def kernel(
        pos_in, kinds_in, bp_in, tb_in, tf_in,
        charges, orders_out, bforce, fforce,
        pos, kinds, bp, tb, tf, in_sems,
        ext, dext, brhs, alhs, colg, square_a, square_b, part_sum, kbuf, ycol, vext, gext, idxb, bv, gb, kindc, torc, raws,
        ar_send, ar_flat, ar_mid, ar_line,
        pos_send, pos_recv, vec_send, vec_recv, g_send, g_recv,
        flat_send, flat_recv, line_send, line_recv,
    ):
        ix = lax.axis_index("gx")
        iy = lax.axis_index("gy")
        iz = lax.axis_index("gz")

        def device(a, b, c):
            return (lax.rem(ix + a + nx, nx), lax.rem(iy + b + ny, ny), lax.rem(iz + c + nz, nz))

        fetches = [
            pltpu.make_async_copy(source, target, in_sems.at[number])
            for number, (source, target) in enumerate(
                ((pos_in, pos), (kinds_in, kinds), (bp_in, bp), (tf_in, tf), (tb_in, tb))
            )
        ]
        for fetch in fetches:
            fetch.start()
        def flat_device(i, j):
            return ((ix // px) * px + lax.rem(lax.rem(ix, px) + i, px), lax.rem(iy + j, ny), iz)

        def line_device(i, j, k):
            return (
                lax.rem(ix // px + i, nx // px) * px + lax.rem(ix, px),
                iy,
                lax.rem(iz // pz + j, nz // pz) * pz + lax.rem(lax.rem(iz, pz) + k, pz),
            )

        greeted = [device(*side) for side in SIDES]
        greeted += [flat_device(*peer) for peer in flat] + [line_device(*peer) for peer in line]
        barrier = pltpu.get_barrier_semaphore()
        for peer in greeted:
            pl.semaphore_signal(barrier, inc=1, device_id=peer, device_id_type=MESH)

        def halo(ref, send, recv):
            copies = []
            for number, (a, b, c) in enumerate(SIDES):
                sx, sy, sz = send_range(a, cx), send_range(b, cy), send_range(c, cz)
                lx, ly, lz = land_range(a, cx), land_range(b, cy), land_range(c, cz)
                copies.append(
                    pltpu.make_async_remote_copy(
                        src_ref=ref.at[pl.ds(*sx), pl.ds(*sy), pl.ds(*sz)],
                        dst_ref=ref.at[pl.ds(*lx), pl.ds(*ly), pl.ds(*lz)],
                        send_sem=send.at[number],
                        recv_sem=recv.at[number],
                        device_id=device(a, b, c),
                        device_id_type=MESH,
                    )
                )
            for copy, side in zip(copies, SIDES):
                if side[2] != 0:
                    copy.start()
            for copy, side in zip(copies, SIDES):
                if side[2] == 0:
                    copy.start()
            return copies

        def landed(copies):
            for copy in copies:
                copy.wait_recv()

        def finish(copies):
            for copy in copies:
                copy.wait_send()

        fetches[0].wait()
        fetches[1].wait()
        for x, y, z in cell_list:
            for f in range(3):
                ext[x + 1, y + 1, z + 1, f : f + 1, :] = pos[f, x, y, z : z + 1, :]
            ext[x + 1, y + 1, z + 1, 3:4, :] = kinds[x, y, z : z + 1, :].astype(jnp.float32)
        for x in range(cx):
            for y in range(cy):
                at = (x * cy + y) * cz
                kindc[at : at + cz, :] = kinds[x, y]
        kind_own = kindc[0:cells, :]

        def cell_of(c):
            return (c // (cy * cz), lax.rem(c // cz, cy), lax.rem(c, cz))

        shield_root = [float((cutoff * g) ** -1.5) for g in shield_table]
        row8 = lax.broadcasted_iota(jnp.int32, (8, ATOMS), 0)
        ones3 = jnp.where(row8 < 3, 1.0, 0.0)

        def narrow(value):
            return value.astype(jnp.bfloat16).astype(jnp.float32)

        def by_row(values):
            out = jnp.zeros((8, ATOMS), jnp.float32)
            for at, value in enumerate(values):
                if value is not None:
                    out = jnp.where(row8 == at, value, out)
            return out

        def derive(x, y, z, number):
            middle = (x - 0.5 * (cx + 2), y - 0.5 * (cy + 2), z - 0.5 * (cz + 2))
            place_at = by_row(
                [
                    ext[x, y, z, f : f + 1, :] * (1.0 / cutoff) + jnp.float32(middle[f])
                    for f in range(3)
                ]
            )
            grid = jnp.round(place_at * 64.0) * (1.0 / 64.0)
            rest = place_at - grid
            mid = narrow(rest)
            low = rest - mid
            grid_sq = jnp.sum(grid * grid, axis=0, keepdims=True)
            rest_sq = jnp.sum(rest * (2.0 * grid + rest), axis=0, keepdims=True)
            grid_1 = jnp.round(grid_sq * 16.0) * (1.0 / 16.0)
            grid_2 = grid_sq - grid_1
            rest_1 = narrow(rest_sq)
            rest_2 = narrow(rest_sq - rest_1)
            rest_3 = (rest_sq - rest_1) - rest_2
            heads = by_row([grid_1, grid_2, 1.0, 1.0, rest_1, rest_2, rest_3])
            tile = jnp.concatenate([grid, heads, ones3, mid, low, grid, grid, mid], axis=0)
            brhs[x, y, z] = tile.astype(jnp.bfloat16)
            kind = ext[x, y, z, 3:4, :]
            dext[x, y, z, 0:1, :] = lookup(kind, shield_root)
            dext[x, y, z, 1:2, :] = lookup(kind, negativity_table)
            if number is not None:
                heads = by_row([1.0, 1.0, grid_1, grid_2, 1.0, 1.0, 1.0])
                tails = by_row([rest_1, rest_2, rest_3])
                left = jnp.concatenate(
                    [
                        -2.0 * grid, heads, tails, -2.0 * grid,
                        -2.0 * grid, -2.0 * mid, -2.0 * low, -2.0 * mid,
                    ],
                    axis=0,
                )
                alhs[number] = jnp.transpose(left).astype(jnp.bfloat16)

        def derive_own(n, carry):
            x = n // cy
            y = lax.rem(n, cy)
            for z in range(cz):
                derive(x + 1, y + 1, z + 1, (x * cy + y) * cz + z)
            return carry

        lax.fori_loop(0, cx * cy, derive_own, 0)

        ycol[...] = jnp.zeros((ATOMS, ATOMS), jnp.float32)
        ycol[0:cells, :] = lookup(kind_own, shield_root)
        flipped = jnp.transpose(ycol[...])
        for number in range(cells):
            colg[number] = jnp.broadcast_to(flipped[:, number : number + 1], (ATOMS, ATOMS))
        ycol[...] = jnp.zeros((ATOMS, ATOMS), jnp.float32)

        def tiles_of(y):
            every = [
                (i, j, k) for j in (y, y + 1, y + 2) for i in (1, 2, None) for k in (1, 2, None)
            ]
            own = [t for t in every if t[0] and t[2] and 1 <= t[1] <= cy]
            far = [t for t in every if t[2] is None]
            return own, [t for t in every if t not in own + far], far

        row_of = lax.broadcasted_iota(jnp.int32, (ROWS, ATOMS), 0)
        lane_of = lax.broadcasted_iota(jnp.int32, (ROWS, ATOMS), 1)

        def keep_sums(at, c, first, second):
            one = jnp.sum(first, axis=1, keepdims=True)
            two = jnp.sum(second, axis=1, keepdims=True)
            ycol[pl.ds(at, ROWS), :] = ycol[pl.ds(at, ROWS), :] + jnp.where(
                lane_of == c, one, jnp.where(lane_of == c + 16, two, 0.0)
            )

        def coupling_part(y, tiles, base, last):
            def at_cell(xz):
                x = xz // cz
                z = lax.rem(xz, cz)
                return x, z, (x * cy + y) * cz + z

            def neighbour(x, z, tile):
                i, j, k = tile
                return ((cx + 1) * x if i is None else i, j, (cz + 1) * z if k is None else k)

            def squares(xz, target):
                x, z, c = at_cell(xz)
                for slot, tile in enumerate(tiles):
                    target[slot] = jnp.dot(
                        alhs[c], brhs[neighbour(x, z, tile)], preferred_element_type=jnp.float32
                    )

            def entries(xz, source):
                x, z, c = at_cell(xz)
                own_g = colg[c]
                if last:
                    sum_one, sum_chi = part_sum[0, c], part_sum[1, c]
                else:
                    sum_one = jnp.zeros((ROWS, ATOMS), jnp.float32)
                    sum_chi = jnp.zeros((ROWS, ATOMS), jnp.float32)
                for slot, tile in enumerate(tiles):
                    i, j, k = tile
                    near = neighbour(x, z, tile)
                    near_g = dext[(*near, slice(0, 1), slice(None))]
                    near_chi = dext[(*near, slice(1, 2), slice(None))]
                    q = jnp.minimum(jnp.maximum(source[slot], 1e-30), 1.0)
                    u = q * lax.rsqrt(q)
                    inv = jnp.exp2(lax.log2(u * q + own_g * near_g) * (-1.0 / 3.0))
                    inner_part = (u - 3.5) * q + (u * TAPER[0] - TAPER[1])
                    value = (inner_part * (q * q) + TAPER[2]) * inv
                    if i and k and j == y + 1:
                        same = jnp.logical_and(x + 1 == i, z + 1 == k)
                        value = jnp.where(
                            row_of + jnp.where(same, 0, -ATOMS) == lane_of, 0.0, value
                        )
                    kbuf[c, 0, base + slot] = value
                    sum_one = sum_one + value
                    sum_chi = sum_chi + value * near_chi
                if last:
                    keep_sums(0, c, sum_chi, sum_one)
                else:
                    part_sum[0, c] = sum_one
                    part_sum[1, c] = sum_chi

            squares(0, square_a)

            def pair(m, carry):
                squares(2 * m + 1, square_b)
                entries(2 * m, square_a)
                squares(jnp.minimum(2 * m + 2, cx * cz - 1), square_a)
                entries(2 * m + 1, square_b)
                return carry

            lax.fori_loop(0, cx * cz // 2, pair, 0)

        tile_sets = [tiles_of(y) for y in range(cy)]
        coupling_part(0, tile_sets[0][0], 0, False)
        pl.semaphore_wait(barrier, len(greeted))
        pos_copies = halo(ext, pos_send, pos_recv)
        for y in range(1, cy):
            coupling_part(y, tile_sets[y][0], 0, False)

        for fetch in fetches[2:]:
            fetch.wait()
        for x in range(cx):
            for y in range(cy):
                at = (x * cy + y) * cz
                for s in range(NTOR):
                    torc[0, s, at : at + cz, :] = tb[0, s, x, y]
                    torc[1, s, at : at + cz, :] = tb[1, s, x, y]
        for number, (x, y, z) in enumerate(cell_list):
            for s in range(NBOND):
                idxb[number, s : s + 1, :] = bp[s, x, y, z : z + 1, :]
                idxb[number, NBOND + s : NBOND + s + 1, :] = tf[s, x, y, z : z + 1, :]

        landed(pos_copies)

        def derive_x(n, carry):
            x = (cx + 1) * (n // (cy + 2))
            for z in range(cz + 2):
                derive(x, lax.rem(n, cy + 2), z, None)
            return carry

        def derive_y(n, carry):
            for z in range(cz + 2):
                derive(n // 2 + 1, (cy + 1) * lax.rem(n, 2), z, None)
            return carry

        def derive_z(n, carry):
            for z in (0, cz + 1):
                derive(n // cy + 1, lax.rem(n, cy) + 1, z, None)
            return carry

        lax.fori_loop(0, 2 * (cy + 2), derive_x, 0)
        lax.fori_loop(0, 2 * cx, derive_y, 0)
        lax.fori_loop(0, cx * cy, derive_z, 0)
        for y in range(cy):
            coupling_part(y, tile_sets[y][1] + tile_sets[y][2], len(tile_sets[y][0]), True)

        def gather_cell(c, carry):
            x, y, z = cell_of(c)
            index = jnp.maximum(idxb[c], 0)
            offset = lax.shift_right_logical(index, 7)
            atom = jnp.bitwise_and(index, 127)
            picked = [jnp.zeros((8, ATOMS), jnp.float32) for _ in range(4)]
            around = ext.at[pl.ds(x, 3), pl.ds(y, 3), pl.ds(z, 3)]
            for k, (a, b, d) in enumerate(STEPS):
                here = offset == k
                for f in range(4):
                    row = jnp.broadcast_to(
                        around[1 + a, 1 + b, 1 + d, f : f + 1, :], (8, ATOMS)
                    )
                    got = jnp.take_along_axis(row, atom, axis=1, mode="promise_in_bounds")
                    picked[f] = jnp.where(here, got, picked[f])
            sx = (offset >= 9).astype(jnp.int32) + (offset >= 18).astype(jnp.int32)
            rest = offset - 9 * sx
            sy = (rest >= 3).astype(jnp.int32) + (rest >= 6).astype(jnp.int32)
            sz = rest - 3 * sy
            for f, step in enumerate((sx, sy, sz)):
                shift = (step - 1).astype(jnp.float32) * cutoff
                own = ext[x + 1, y + 1, z + 1, f : f + 1, :]
                vec = picked[f] + shift - own
                for s in range(8):
                    bv[f, s, pl.ds(c, 1), :] = vec[s : s + 1, :]
            radius = lookup(picked[3], radius_table)
            for s in range(8):
                bv[3, s, pl.ds(c, 1), :] = radius[s : s + 1, :]
                gb[s, pl.ds(c, 1), :] = jnp.where(idxb[c, s : s + 1, :] >= 0, 1.0, 0.0)
            return carry

        def excess_damping():
            radius_own = lookup(kind_own, radius_table)
            excess = -lookup(kind_own, valence_table)
            for s in range(NBOND):
                vec = [bv[f, s, 0:cells, :] for f in range(3)]
                span = radius_own + bv[3, s, 0:cells, :]
                raw = gb[s, 0:cells, :] * jnp.exp(order_rate * dot3(vec, vec) / (span * span))
                raws[s, 0:cells, :] = raw
                excess = excess + raw
            g_here = 2.0 / (1.0 + jnp.exp(excess))
            for number, (x, y, z) in enumerate(cell_list):
                gext[x + 1, y + 1, z + 1, 0:1, :] = g_here[number : number + 1, :]
            return g_here

        scale = 20.0 * coulomb / cutoff

        def products():
            turned = jnp.transpose(ycol[...])
            return (scale * turned[0:cells, :], scale * turned[16 : 16 + cells, :])

        def apply_part(number, side):
            for y in range(cy):
                tiles = tile_sets[y][side]
                base = sum(len(group) for group in tile_sets[y][:side])

                def cell(xz, carry):
                    x = xz // cz
                    z = lax.rem(xz, cz)
                    c = (x * cy + y) * cz + z

                    def rows(r, inner):
                        at = pl.multiple_of(r * ROWS, ROWS)
                        first = jnp.zeros((ROWS, ATOMS), jnp.float32)
                        second = jnp.zeros((ROWS, ATOMS), jnp.float32)
                        for slot, (i, j, k) in enumerate(tiles):
                            ex = (cx + 1) * x if i is None else i
                            ez = (cz + 1) * z if k is None else k
                            value = kbuf[c, r, base + slot]
                            first = first + value * vext[number, ex, j, ez, 0:1, :]
                            second = second + value * vext[number, ex, j, ez, 1:2, :]
                        keep_sums(at, c, first, second)
                        return inner

                    return lax.fori_loop(0, ATOMS // ROWS, rows, carry)

                lax.fori_loop(0, cx * cz, cell, 0)

        def apply_own(number):
            ycol[...] = jnp.zeros((ATOMS, ATOMS), jnp.float32)
            apply_part(number, 0)

        def apply_near(number, copies):
            landed([c for c, side in zip(copies, SIDES) if side[2] == 0])
            apply_part(number, 1)

        def apply_far(number, copies):
            landed([c for c, side in zip(copies, SIDES) if side[2] != 0])
            apply_part(number, 2)
            return products()

        def place(number, first, second):
            for at, (x, y, z) in enumerate(cell_list):
                vext[number, x + 1, y + 1, z + 1, 0:1, :] = first[at : at + 1, :]
                vext[number, x + 1, y + 1, z + 1, 1:2, :] = second[at : at + 1, :]
            return halo(vext.at[number], vec_send.at[number], vec_recv.at[number])

        row8_lane = row8 == lax.broadcasted_iota(jnp.int32, (8, ATOMS), 1)

        def reduce_start(number, values):
            rows = by_row([jnp.sum(value, axis=0, keepdims=True) for value in values])
            rows = jnp.sum(rows, axis=1, keepdims=True)
            ar_send[number] = jnp.sum(jnp.where(row8_lane, rows, 0.0), axis=0, keepdims=True)
            copies = []
            for slot, peer in enumerate(flat):
                copies.append(
                    pltpu.make_async_remote_copy(
                        src_ref=ar_send.at[number],
                        dst_ref=ar_flat.at[number, slot],
                        send_sem=flat_send.at[number, slot],
                        recv_sem=flat_recv.at[number, slot],
                        device_id=flat_device(*peer),
                        device_id_type=MESH,
                    )
                )
            for copy in copies:
                copy.start()
            return copies

        def reduce_next(number, copies):
            landed(copies)
            parts = [ar_send[number]] + [ar_flat[number, slot] for slot in range(len(flat))]
            while len(parts) > 1:
                parts = [sum(parts[at : at + 2]) for at in range(0, len(parts), 2)]
            ar_mid[number] = parts[0]
            after = []
            for slot, peer in enumerate(line):
                after.append(
                    pltpu.make_async_remote_copy(
                        src_ref=ar_mid.at[number],
                        dst_ref=ar_line.at[number, slot],
                        send_sem=line_send.at[number, slot],
                        recv_sem=line_recv.at[number, slot],
                        device_id=line_device(*peer),
                        device_id_type=MESH,
                    )
                )
            for copy in after:
                copy.start()
            return after

        def reduce_end(number, copies):
            landed(copies)
            parts = [ar_mid[number]] + [ar_line[number, slot] for slot in range(len(line))]
            while len(parts) > 1:
                parts = [sum(parts[at : at + 2]) for at in range(0, len(parts), 2)]
            total = parts[0]
            return [jnp.broadcast_to(total[:, at : at + 1], (1, ATOMS)) for at in range(8)]

        chi = lookup(kind_own, negativity_table)
        kchi, ksum = products()
        diagonal = lookup(kind_own, hardness_table) + ksum
        ws = -(diagonal * chi + kchi)
        wt = -(diagonal + ksum)
        vec0 = place(0, ws, wt)
        red0 = reduce_start(0, [chi * chi, -chi * ws, ws * ws, -wt, wt * wt, chi])
        apply_own(0)
        lax.fori_loop(0, 2, gather_cell, 0)
        red0b = reduce_next(0, red0)
        apply_near(0, vec0)
        lax.fori_loop(2, cells, gather_cell, 0)
        k2s, k2t = apply_far(0, vec0)
        hws = diagonal * ws + k2s
        hwt = diagonal * wt + k2t
        rr0s, pq0s, qq0s, pq0t, qq0t, chi_sum, _, _ = reduce_end(0, red0b)
        rr0t = jnp.full((1, ATOMS), float(total_atoms), jnp.float32)
        a0s, a0t = rr0s / pq0s, rr0t / pq0t
        b0s = a0s * a0s * qq0s / rr0s - 1.0
        b0t = a0t * a0t * qq0t / rr0t - 1.0
        r1s, r1t = -chi - a0s * ws, -1.0 - a0t * wt
        d1s, d1t = r1s - b0s * chi, r1t - b0t
        hr1s, hr1t = ws - a0s * hws, wt - a0t * hwt
        q1s, q1t = hr1s + b0s * ws, hr1t + b0t * wt
        vec1 = place(1, q1s, q1t)
        red1 = reduce_start(
            1, [r1s * r1s, d1s * q1s, q1s * q1s, d1s, r1t * r1t, d1t * q1t, q1t * q1t, d1t]
        )
        g_here = excess_damping()
        g_copies = halo(gext, g_send, g_recv)
        apply_own(1)
        red1b = reduce_next(1, red1)
        apply_near(1, vec1)
        k3s, k3t = apply_far(1, vec1)
        hq1s = diagonal * q1s + k3s
        hq1t = diagonal * q1t + k3t
        rr1s, pq1s, qq1s, d1s_sum, rr1t, pq1t, qq1t, d1t_sum = reduce_end(1, red1b)
        a1s, a1t = rr1s / pq1s, rr1t / pq1t
        b1s = a1s * a1s * qq1s / rr1s - 1.0
        b1t = a1t * a1t * qq1t / rr1t - 1.0
        r2s, r2t = r1s - a1s * q1s, r1t - a1t * q1t
        d2s, d2t = r2s + b1s * d1s, r2t + b1t * d1t
        q2s = hr1s - a1s * hq1s + b1s * q1s
        q2t = hr1t - a1t * hq1t + b1t * q1t
        red2 = reduce_start(2, [r2s * r2s, d2s * q2s, d2s, r2t * r2t, d2t * q2t, d2t])

        landed(g_copies)

        def gather_damping(c, carry):
            x, y, z = cell_of(c)
            index = jnp.maximum(idxb[c], 0)
            offset = lax.shift_right_logical(index, 7)
            atom = jnp.bitwise_and(index, 127)
            picked = jnp.zeros((8, ATOMS), jnp.float32)
            around = gext.at[pl.ds(x, 3), pl.ds(y, 3), pl.ds(z, 3)]
            for k, (a, b, d) in enumerate(STEPS):
                row = jnp.broadcast_to(around[1 + a, 1 + b, 1 + d, 0:1, :], (8, ATOMS))
                got = jnp.take_along_axis(row, atom, axis=1, mode="promise_in_bounds")
                picked = jnp.where(offset == k, got, picked)
            for s in range(NBOND):
                raws[s, pl.ds(c, 1), :] = raws[s, pl.ds(c, 1), :] * picked[s : s + 1, :]
            return carry

        lax.fori_loop(0, cells, gather_damping, 0)
        red2b = reduce_next(2, red2)

        def spread_out(ref, lead, value):
            for x in range(cx):
                for y in range(cy):
                    at = (x * cy + y) * cz
                    ref[(*lead, x, y)] = value[at : at + cz, :]

        order = []
        for s in range(NBOND):
            order.append(raws[s, 0:cells, :] * g_here)
            spread_out(orders_out, (s,), order[s])
        bend = lookup(kind_own, bend_table)
        rest = lookup(kind_own, cosine_table)
        twist = lookup(kind_own, twist_table)
        vecs = [[bv[f, s, 0:cells, :] for f in range(3)] for s in range(NBOND)]
        radii = [bv[3, s, 0:cells, :] for s in range(NBOND)]
        inv = [lax.rsqrt(dot3(vecs[s], vecs[s]) + 1.0) for s in range(NBOND)]
        force = [[jnp.zeros((cells, ATOMS), jnp.float32) for _ in range(3)] for _ in range(NBOND)]
        for a in range(NBOND):
            for b in range(a + 1, NBOND):
                both = inv[a] * inv[b]
                cosine = dot3(vecs[a], vecs[b]) * both
                pull = -2.0 * bend * (order[a] * order[b]) * (cosine - rest)
                cross_part = pull * both
                own_part = pull * cosine
                pa = own_part * (inv[a] * inv[a])
                pb = own_part * (inv[b] * inv[b])
                for f in range(3):
                    force[a][f] = force[a][f] + (cross_part * vecs[b][f] - pa * vecs[a][f])
                    force[b][f] = force[b][f] + (cross_part * vecs[a][f] - pb * vecs[b][f])

        def choose(options, slot):
            out = options[0]
            for s in range(1, NBOND):
                out = jnp.where(slot == s, options[s], out)
            return out

        for t in range(NTOR):
            first = torc[0, t, 0:cells, :]
            second = torc[1, t, 0:cells, :]
            vj = [choose([vecs[s][f] for s in range(NBOND)], first) for f in range(3)]
            vk = [choose([vecs[s][f] for s in range(NBOND)], second) for f in range(3)]
            weight = choose(order, first) * choose(order, second)
            span = choose(radii, second) + bv[3, NBOND + t, 0:cells, :]
            far = [bv[f, NBOND + t, 0:cells, :] for f in range(3)]
            u = [far[f] - vk[f] for f in range(3)]
            weight = weight * jnp.exp(order_rate * dot3(u, u) / (span * span))
            weight = weight * gb[NBOND + t, 0:cells, :]
            n1 = cross3(vj, vk)
            n2 = cross3(vk, u)
            i1 = lax.rsqrt(dot3(n1, n1) + 1.0)
            i2 = lax.rsqrt(dot3(n2, n2) + 1.0)
            both = i1 * i2
            cosine = dot3(n1, n2) * both
            pull = 2.0 * twist * weight * cosine
            cross_part = pull * both
            own1 = pull * cosine * (i1 * i1)
            own2 = pull * cosine * (i2 * i2)
            p1 = [cross_part * n2[f] - own1 * n1[f] for f in range(3)]
            p2 = [cross_part * n1[f] - own2 * n2[f] for f in range(3)]
            fj = cross3(vk, p1)
            fw = cross3(p2, vk)
            part1 = cross3(p1, vj)
            part2 = cross3(u, p2)
            fk = [part1[f] + part2[f] - fw[f] for f in range(3)]
            for s in range(NBOND):
                for f in range(3):
                    force[s][f] = (
                        force[s][f]
                        + jnp.where(first == s, fj[f], 0.0)
                        + jnp.where(second == s, fk[f], 0.0)
                    )
            for f in range(3):
                spread_out(fforce, (f, t), fw[f])
        for s in range(NBOND):
            for f in range(3):
                spread_out(bforce, (f, s), force[s][f])

        rr2s, pq2s, d2s_sum, rr2t, pq2t, d2t_sum, _, _ = reduce_end(2, red2b)
        a2s, a2t = rr2s / pq2s, rr2t / pq2t
        solve_s = -a0s * chi + a1s * d1s + a2s * d2s
        solve_t = -a0t + a1t * d1t + a2t * d2t
        sum_s = -a0s * chi_sum + a1s * d1s_sum + a2s * d2s_sum
        sum_t = -a0t * rr0t + a1t * d1t_sum + a2t * d2t_sum
        result = charge_unit * (solve_s - (sum_s / sum_t) * solve_t)
        spread_out(charges, (), result)

        for copies in (pos_copies, g_copies, vec0, vec1, red0, red0b, red1, red1b, red2, red2b):
            finish(copies)

    def scratch():
        big = (cx + 2, cy + 2, cz + 2)
        sides = len(SIDES)
        dma = pltpu.SemaphoreType.DMA
        f32 = jnp.float32
        return [
            pltpu.VMEM((3, *block, ATOMS), f32),
            pltpu.VMEM((*block, ATOMS), jnp.int32),
            pltpu.VMEM((NBOND, *block, ATOMS), jnp.int32),
            pltpu.VMEM((2, NTOR, *block, ATOMS), jnp.int32),
            pltpu.VMEM((NTOR, *block, ATOMS), jnp.int32),
            dma((5,)),
            pltpu.VMEM((*big, 4, ATOMS), f32),
            pltpu.VMEM((*big, 2, ATOMS), f32),
            pltpu.VMEM((*big, DEPTH, ATOMS), jnp.bfloat16),
            pltpu.VMEM((cells, ATOMS, DEPTH), jnp.bfloat16),
            pltpu.VMEM((cells, ATOMS, ATOMS), f32),
            pltpu.VMEM((19, ATOMS, ATOMS), f32),
            pltpu.VMEM((19, ATOMS, ATOMS), f32),
            pltpu.VMEM((2, cells, ATOMS, ATOMS), f32),
            pltpu.VMEM((cells, ATOMS // ROWS, 27, ROWS, ATOMS), f32),
            pltpu.VMEM((ATOMS, ATOMS), f32),
            pltpu.VMEM((2, *big, 2, ATOMS), f32),
            pltpu.VMEM((*big, 1, ATOMS), f32),
            pltpu.VMEM((cells, 8, ATOMS), jnp.int32),
            pltpu.VMEM((4, 8, 16, ATOMS), f32),
            pltpu.VMEM((8, 16, ATOMS), f32),
            pltpu.VMEM((16, ATOMS), jnp.int32),
            pltpu.VMEM((2, NTOR, 16, ATOMS), jnp.int32),
            pltpu.VMEM((NBOND, 16, ATOMS), f32),
            pltpu.VMEM((3, 1, ATOMS), f32),
            pltpu.VMEM((3, len(flat), 1, ATOMS), f32),
            pltpu.VMEM((3, 1, ATOMS), f32),
            pltpu.VMEM((3, len(line), 1, ATOMS), f32),
            dma((sides,)), dma((sides,)),
            dma((2, sides)), dma((2, sides)),
            dma((sides,)), dma((sides,)),
            dma((3, len(flat))), dma((3, len(flat))),
            dma((3, len(line))), dma((3, len(line))),
        ]

    return kernel, scratch()


def write_out(*refs):
    sources, targets, sems = refs[:4], refs[4:8], refs[8]
    copies = [
        pltpu.make_async_copy(source, target, sems.at[number])
        for number, (source, target) in enumerate(zip(sources, targets))
    ]
    for copy in copies:
        copy.start()
    for copy in copies:
        copy.wait()


def solution(mesh):
    sizes = (mesh.shape["gx"], mesh.shape["gy"], mesh.shape["gz"])

    def on_device(positions, atom_kinds, bond_partners, torsion_bonds, torsion_far):
        block = positions.shape[1:4]
        total = ATOMS
        for count, size in zip(block, sizes):
            total *= count * size
        kernel, scratch = make_kernel(sizes, block, total)
        f32 = jnp.float32
        whole = pl.BlockSpec(memory_space=pltpu.VMEM)
        shapes = (
                jax.ShapeDtypeStruct((*block, ATOMS), f32),
                jax.ShapeDtypeStruct((NBOND, *block, ATOMS), f32),
                jax.ShapeDtypeStruct((3, NBOND, *block, ATOMS), f32),
                jax.ShapeDtypeStruct((3, NTOR, *block, ATOMS), f32),
            )
        arrays = (positions, atom_kinds, bond_partners, torsion_bonds, torsion_far)
        hbm = pl.BlockSpec(memory_space=pltpu.MemorySpace.HBM)
        results = pl.pallas_call(
            kernel,
            out_shape=shapes,
            in_specs=[hbm] * 5,
            out_specs=(whole,) * 4,
            scratch_shapes=scratch,
            compiler_params=pltpu.CompilerParams(
                collective_id=0, has_side_effects=True, vmem_limit_bytes=48 * 1024 * 1024
            ),
            name="reax_step",
        )(*[pltpu.with_memory_space_constraint(a, pltpu.MemorySpace.HBM) for a in arrays])
        return pl.pallas_call(
            write_out,
            out_shape=shapes,
            in_specs=[whole] * 4,
            out_specs=(hbm,) * 4,
            scratch_shapes=[pltpu.SemaphoreType.DMA((4,))],
            name="write_out",
        )(*[pltpu.with_memory_space_constraint(r, pltpu.MemorySpace.VMEM) for r in results])

    placed = (
        P(None, "gx", "gy", "gz", None),
        P("gx", "gy", "gz", None),
        P(None, "gx", "gy", "gz", None),
        P(None, None, "gx", "gy", "gz", None),
        P(None, "gx", "gy", "gz", None),
    )
    return jax.shard_map(
        on_device,
        mesh=mesh,
        in_specs=placed,
        out_specs=(
            P("gx", "gy", "gz", None),
            P(None, "gx", "gy", "gz", None),
            P(None, None, "gx", "gy", "gz", None),
            P(None, None, "gx", "gy", "gz", None),
        ),
        check_vma=False,
    )
```

```python
import jax
import jax.numpy as jnp
from jax import lax
from jax.experimental import pallas as pl
from jax.experimental.pallas import tpu as pltpu
from jax.sharding import PartitionSpec as P

MESH = pl.DeviceIdType.MESH

ATOMS = 128
NBOND = 4
NTOR = 4
cutoff = 10.0
coulomb = 14.4
order_rate = -0.3
charge_unit = 100.0
shield_table = (0.82, 1.08, 0.75)
negativity_table = (4.7, 8.5, 5.3)
hardness_table = (6.0, 7.2, 7.4)
radius_table = (5.0, 4.0, 3.0)
valence_table = (4.0, 2.0, 1.0)
bend_table = (40.0, 30.0, 10.0)
cosine_table = (-0.3333, -0.25, -0.5)
twist_table = (20.0, 12.0, 6.0)

STEPS = [(a, b, c) for a in (-1, 0, 1) for b in (-1, 0, 1) for c in (-1, 0, 1)]
SIDES = [s for s in STEPS if s != (0, 0, 0)]
ROWS = 128
TAPER_GRID = 2.0**-22
TAPER_42 = round(4.2 / (2 * TAPER_GRID)) * (2 * TAPER_GRID)
TAPER_05 = round(0.05 / TAPER_GRID) * TAPER_GRID
TAPER = (TAPER_42, TAPER_42 - 2.5 + TAPER_05, TAPER_05)
DEPTH = 64


def lookup(kind, table):
    return jnp.where(kind == 0, table[0], jnp.where(kind == 1, table[1], table[2])).astype(jnp.float32)


def send_range(step, size):
    if step > 0:
        return (size, 1)
    if step < 0:
        return (1, 1)
    return (1, size)


def land_range(step, size):
    if step > 0:
        return (0, 1)
    if step < 0:
        return (size + 1, 1)
    return (1, size)


def add3(a, b):
    return [p + q for p, q in zip(a, b)]


def dot3(a, b):
    return a[0] * b[0] + a[1] * b[1] + a[2] * b[2]


def cross3(a, b):
    return [
        a[1] * b[2] - a[2] * b[1],
        a[2] * b[0] - a[0] * b[2],
        a[0] * b[1] - a[1] * b[0],
    ]


def make_kernel(sizes, block, total_atoms):
    nx, ny, nz = sizes
    cx, cy, cz = block
    cells = cx * cy * cz
    cell_list = [(x, y, z) for x in range(cx) for y in range(cy) for z in range(cz)]
    px, pz = 2, nz // 2
    flat = [(i, j) for i in range(px) for j in range(ny) if (i, j) != (0, 0)]
    line = [
        (i, j, k)
        for i in range(nx // px)
        for j in range(nz // pz)
        for k in range(pz)
        if (i, j, k) != (0, 0, 0)
    ]

    def kernel(
        pos_in, kinds_in, bp_in, tb_in, tf_in,
        charges, orders_out, bforce, fforce,
        pos, kinds, bp, tb, tf, in_sems,
        ext, dext, brhs, alhs, colg, square_a, square_b, part_sum, kbuf, ycol, vext, gext, idxb, bv, gb, kindc, torc, raws,
        ar_send, ar_flat, ar_mid, ar_line,
        pos_send, pos_recv, vec_send, vec_recv, g_send, g_recv,
        flat_send, flat_recv, line_send, line_recv,
    ):
        ix = lax.axis_index("gx")
        iy = lax.axis_index("gy")
        iz = lax.axis_index("gz")

        def device(a, b, c):
            return (lax.rem(ix + a + nx, nx), lax.rem(iy + b + ny, ny), lax.rem(iz + c + nz, nz))

        fetches = [
            pltpu.make_async_copy(source, target, in_sems.at[number])
            for number, (source, target) in enumerate(
                ((pos_in, pos), (kinds_in, kinds), (bp_in, bp), (tf_in, tf), (tb_in, tb))
            )
        ]
        for fetch in fetches:
            fetch.start()
        def flat_device(i, j):
            return ((ix // px) * px + lax.rem(lax.rem(ix, px) + i, px), lax.rem(iy + j, ny), iz)

        def line_device(i, j, k):
            return (
                lax.rem(ix // px + i, nx // px) * px + lax.rem(ix, px),
                iy,
                lax.rem(iz // pz + j, nz // pz) * pz + lax.rem(lax.rem(iz, pz) + k, pz),
            )

        greeted = [device(*side) for side in SIDES]
        greeted += [flat_device(*peer) for peer in flat] + [line_device(*peer) for peer in line]
        barrier = pltpu.get_barrier_semaphore()
        for peer in greeted:
            pl.semaphore_signal(barrier, inc=1, device_id=peer, device_id_type=MESH)

        def halo(ref, send, recv):
            copies = []
            for number, (a, b, c) in enumerate(SIDES):
                sx, sy, sz = send_range(a, cx), send_range(b, cy), send_range(c, cz)
                lx, ly, lz = land_range(a, cx), land_range(b, cy), land_range(c, cz)
                copies.append(
                    pltpu.make_async_remote_copy(
                        src_ref=ref.at[pl.ds(*sx), pl.ds(*sy), pl.ds(*sz)],
                        dst_ref=ref.at[pl.ds(*lx), pl.ds(*ly), pl.ds(*lz)],
                        send_sem=send.at[number],
                        recv_sem=recv.at[number],
                        device_id=device(a, b, c),
                        device_id_type=MESH,
                    )
                )
            for copy, side in zip(copies, SIDES):
                if side[2] != 0:
                    copy.start()
            for copy, side in zip(copies, SIDES):
                if side[2] == 0:
                    copy.start()
            return copies

        def landed(copies):
            for copy in copies:
                copy.wait_recv()

        def finish(copies):
            for copy in copies:
                copy.wait_send()

        fetches[0].wait()
        fetches[1].wait()
        for x, y, z in cell_list:
            for f in range(3):
                ext[x + 1, y + 1, z + 1, f : f + 1, :] = pos[f, x, y, z : z + 1, :]
            ext[x + 1, y + 1, z + 1, 3:4, :] = kinds[x, y, z : z + 1, :].astype(jnp.float32)
        for x in range(cx):
            for y in range(cy):
                at = (x * cy + y) * cz
                kindc[at : at + cz, :] = kinds[x, y]
        kind_own = kindc[0:cells, :]

        def cell_of(c):
            return (c // (cy * cz), lax.rem(c // cz, cy), lax.rem(c, cz))

        shield_root = [float((cutoff * g) ** -1.5) for g in shield_table]
        row8 = lax.broadcasted_iota(jnp.int32, (8, ATOMS), 0)
        ones3 = jnp.where(row8 < 3, 1.0, 0.0)

        def narrow(value):
            return value.astype(jnp.bfloat16).astype(jnp.float32)

        def by_row(values):
            out = jnp.zeros((8, ATOMS), jnp.float32)
            for at, value in enumerate(values):
                if value is not None:
                    out = jnp.where(row8 == at, value, out)
            return out

        def derive(x, y, z, number):
            middle = (x - 0.5 * (cx + 2), y - 0.5 * (cy + 2), z - 0.5 * (cz + 2))
            place_at = by_row(
                [
                    ext[x, y, z, f : f + 1, :] * (1.0 / cutoff) + jnp.float32(middle[f])
                    for f in range(3)
                ]
            )
            grid = jnp.round(place_at * 64.0) * (1.0 / 64.0)
            rest = place_at - grid
            mid = narrow(rest)
            low = rest - mid
            grid_sq = jnp.sum(grid * grid, axis=0, keepdims=True)
            rest_sq = jnp.sum(rest * (2.0 * grid + rest), axis=0, keepdims=True)
            grid_1 = jnp.round(grid_sq * 16.0) * (1.0 / 16.0)
            grid_2 = grid_sq - grid_1
            rest_1 = narrow(rest_sq)
            rest_2 = narrow(rest_sq - rest_1)
            rest_3 = (rest_sq - rest_1) - rest_2
            heads = by_row([grid_1, grid_2, 1.0, 1.0, rest_1, rest_2, rest_3])
            tile = jnp.concatenate([grid, heads, ones3, mid, low, grid, grid, mid], axis=0)
            brhs[x, y, z] = tile.astype(jnp.bfloat16)
            kind = ext[x, y, z, 3:4, :]
            dext[x, y, z, 0:1, :] = lookup(kind, shield_root)
            dext[x, y, z, 1:2, :] = lookup(kind, negativity_table)
            if number is not None:
                heads = by_row([1.0, 1.0, grid_1, grid_2, 1.0, 1.0, 1.0])
                tails = by_row([rest_1, rest_2, rest_3])
                left = jnp.concatenate(
                    [
                        -2.0 * grid, heads, tails, -2.0 * grid,
                        -2.0 * grid, -2.0 * mid, -2.0 * low, -2.0 * mid,
                    ],
                    axis=0,
                )
                alhs[number] = jnp.transpose(left).astype(jnp.bfloat16)

        def derive_own(n, carry):
            x = n // cy
            y = lax.rem(n, cy)
            for z in range(cz):
                derive(x + 1, y + 1, z + 1, (x * cy + y) * cz + z)
            return carry

        lax.fori_loop(0, cx * cy, derive_own, 0)

        ycol[...] = jnp.zeros((ATOMS, ATOMS), jnp.float32)
        ycol[0:cells, :] = lookup(kind_own, shield_root)
        flipped = jnp.transpose(ycol[...])
        for number in range(cells):
            colg[number] = jnp.broadcast_to(flipped[:, number : number + 1], (ATOMS, ATOMS))
        ycol[...] = jnp.zeros((ATOMS, ATOMS), jnp.float32)

        def tiles_of(y):
            every = [
                (i, j, k) for j in (y, y + 1, y + 2) for i in (1, 2, None) for k in (1, 2, None)
            ]
            own = [t for t in every if t[0] and t[2] and 1 <= t[1] <= cy]
            far = [t for t in every if t[2] is None]
            return own, [t for t in every if t not in own + far], far

        row_of = lax.broadcasted_iota(jnp.int32, (ROWS, ATOMS), 0)
        lane_of = lax.broadcasted_iota(jnp.int32, (ROWS, ATOMS), 1)

        def keep_sums(at, c, first, second):
            one = jnp.sum(first, axis=1, keepdims=True)
            two = jnp.sum(second, axis=1, keepdims=True)
            ycol[pl.ds(at, ROWS), :] = ycol[pl.ds(at, ROWS), :] + jnp.where(
                lane_of == c, one, jnp.where(lane_of == c + 16, two, 0.0)
            )

        def coupling_part(y, tiles, base, last):
            def at_cell(xz):
                x, z = xz // cz, xz % cz
                return x, z, (x * cy + y) * cz + z

            def neighbour(x, z, tile):
                i, j, k = tile
                return ((cx + 1) * x if i is None else i, j, (cz + 1) * z if k is None else k)

            def squares(xz, target):
                x, z, c = at_cell(xz)
                for slot, tile in enumerate(tiles):
                    target[slot] = jnp.dot(
                        alhs[c], brhs[neighbour(x, z, tile)], preferred_element_type=jnp.float32
                    )

            def entries(xz, source):
                x, z, c = at_cell(xz)
                own_g = colg[c]
                if last:
                    sum_one, sum_chi = part_sum[0, c], part_sum[1, c]
                else:
                    sum_one = jnp.zeros((ROWS, ATOMS), jnp.float32)
                    sum_chi = jnp.zeros((ROWS, ATOMS), jnp.float32)
                for slot, tile in enumerate(tiles):
                    i, j, k = tile
                    near = neighbour(x, z, tile)
                    near_g = dext[(*near, slice(0, 1), slice(None))]
                    near_chi = dext[(*near, slice(1, 2), slice(None))]
                    q = jnp.minimum(jnp.maximum(source[slot], 1e-30), 1.0)
                    u = q * lax.rsqrt(q)
                    inv = jnp.exp2(lax.log2(u * q + own_g * near_g) * (-1.0 / 3.0))
                    inner_part = (u - 3.5) * q + (u * TAPER[0] - TAPER[1])
                    value = (inner_part * (q * q) + TAPER[2]) * inv
                    if near == (x + 1, y + 1, z + 1):
                        value = jnp.where(row_of == lane_of, 0.0, value)
                    kbuf[c, 0, base + slot] = value
                    sum_one = sum_one + value
                    sum_chi = sum_chi + value * near_chi
                if last:
                    keep_sums(0, c, sum_chi, sum_one)
                else:
                    part_sum[0, c] = sum_one
                    part_sum[1, c] = sum_chi

            buffers = (square_a, square_b)
            squares(0, square_a)
            for xz in range(cx * cz):
                if xz + 1 < cx * cz:
                    squares(xz + 1, buffers[(xz + 1) % 2])
                entries(xz, buffers[xz % 2])

        tile_sets = [tiles_of(y) for y in range(cy)]
        coupling_part(0, tile_sets[0][0], 0, False)
        pl.semaphore_wait(barrier, len(greeted))
        pos_copies = halo(ext, pos_send, pos_recv)
        for y in range(1, cy):
            coupling_part(y, tile_sets[y][0], 0, False)

        for fetch in fetches[2:]:
            fetch.wait()
        for x in range(cx):
            for y in range(cy):
                at = (x * cy + y) * cz
                for s in range(NTOR):
                    torc[0, s, at : at + cz, :] = tb[0, s, x, y]
                    torc[1, s, at : at + cz, :] = tb[1, s, x, y]
        for number, (x, y, z) in enumerate(cell_list):
            for s in range(NBOND):
                idxb[number, s : s + 1, :] = bp[s, x, y, z : z + 1, :]
                idxb[number, NBOND + s : NBOND + s + 1, :] = tf[s, x, y, z : z + 1, :]

        landed(pos_copies)

        def derive_x(n, carry):
            x = (cx + 1) * (n // (cy + 2))
            for z in range(cz + 2):
                derive(x, lax.rem(n, cy + 2), z, None)
            return carry

        def derive_y(n, carry):
            for z in range(cz + 2):
                derive(n // 2 + 1, (cy + 1) * lax.rem(n, 2), z, None)
            return carry

        def derive_z(n, carry):
            for z in (0, cz + 1):
                derive(n // cy + 1, lax.rem(n, cy) + 1, z, None)
            return carry

        lax.fori_loop(0, 2 * (cy + 2), derive_x, 0)
        lax.fori_loop(0, 2 * cx, derive_y, 0)
        lax.fori_loop(0, cx * cy, derive_z, 0)
        for y in range(cy):
            coupling_part(y, tile_sets[y][1] + tile_sets[y][2], len(tile_sets[y][0]), True)

        def gather_cell(c, carry):
            x, y, z = cell_of(c)
            index = jnp.maximum(idxb[c], 0)
            offset = lax.shift_right_logical(index, 7)
            atom = jnp.bitwise_and(index, 127)
            picked = [jnp.zeros((8, ATOMS), jnp.float32) for _ in range(4)]
            around = ext.at[pl.ds(x, 3), pl.ds(y, 3), pl.ds(z, 3)]
            for k, (a, b, d) in enumerate(STEPS):
                here = offset == k
                for f in range(4):
                    row = jnp.broadcast_to(
                        around[1 + a, 1 + b, 1 + d, f : f + 1, :], (8, ATOMS)
                    )
                    got = jnp.take_along_axis(row, atom, axis=1, mode="promise_in_bounds")
                    picked[f] = jnp.where(here, got, picked[f])
            sx = (offset >= 9).astype(jnp.int32) + (offset >= 18).astype(jnp.int32)
            rest = offset - 9 * sx
            sy = (rest >= 3).astype(jnp.int32) + (rest >= 6).astype(jnp.int32)
            sz = rest - 3 * sy
            for f, step in enumerate((sx, sy, sz)):
                shift = (step - 1).astype(jnp.float32) * cutoff
                own = ext[x + 1, y + 1, z + 1, f : f + 1, :]
                vec = picked[f] + shift - own
                for s in range(8):
                    bv[f, s, pl.ds(c, 1), :] = vec[s : s + 1, :]
            radius = lookup(picked[3], radius_table)
            for s in range(8):
                bv[3, s, pl.ds(c, 1), :] = radius[s : s + 1, :]
                gb[s, pl.ds(c, 1), :] = jnp.where(idxb[c, s : s + 1, :] >= 0, 1.0, 0.0)
            return carry

        def excess_damping():
            radius_own = lookup(kind_own, radius_table)
            excess = -lookup(kind_own, valence_table)
            for s in range(NBOND):
                vec = [bv[f, s, 0:cells, :] for f in range(3)]
                span = radius_own + bv[3, s, 0:cells, :]
                raw = gb[s, 0:cells, :] * jnp.exp(order_rate * dot3(vec, vec) / (span * span))
                raws[s, 0:cells, :] = raw
                excess = excess + raw
            g_here = 2.0 / (1.0 + jnp.exp(excess))
            for number, (x, y, z) in enumerate(cell_list):
                gext[x + 1, y + 1, z + 1, 0:1, :] = g_here[number : number + 1, :]
            return g_here

        scale = 20.0 * coulomb / cutoff

        def products():
            turned = jnp.transpose(ycol[...])
            return (scale * turned[0:cells, :], scale * turned[16 : 16 + cells, :])

        def apply_part(number, side):
            for y in range(cy):
                tiles = tile_sets[y][side]
                base = sum(len(group) for group in tile_sets[y][:side])

                def cell(xz, carry):
                    x = xz // cz
                    z = lax.rem(xz, cz)
                    c = (x * cy + y) * cz + z

                    def rows(r, inner):
                        at = pl.multiple_of(r * ROWS, ROWS)
                        first = jnp.zeros((ROWS, ATOMS), jnp.float32)
                        second = jnp.zeros((ROWS, ATOMS), jnp.float32)
                        for slot, (i, j, k) in enumerate(tiles):
                            ex = (cx + 1) * x if i is None else i
                            ez = (cz + 1) * z if k is None else k
                            value = kbuf[c, r, base + slot]
                            first = first + value * vext[number, ex, j, ez, 0:1, :]
                            second = second + value * vext[number, ex, j, ez, 1:2, :]
                        keep_sums(at, c, first, second)
                        return inner

                    return lax.fori_loop(0, ATOMS // ROWS, rows, carry)

                lax.fori_loop(0, cx * cz, cell, 0)

        def apply_own(number):
            ycol[...] = jnp.zeros((ATOMS, ATOMS), jnp.float32)
            apply_part(number, 0)

        def apply_near(number, copies):
            landed([c for c, side in zip(copies, SIDES) if side[2] == 0])
            apply_part(number, 1)

        def apply_far(number, copies):
            landed([c for c, side in zip(copies, SIDES) if side[2] != 0])
            apply_part(number, 2)
            return products()

        def place(number, first, second):
            for at, (x, y, z) in enumerate(cell_list):
                vext[number, x + 1, y + 1, z + 1, 0:1, :] = first[at : at + 1, :]
                vext[number, x + 1, y + 1, z + 1, 1:2, :] = second[at : at + 1, :]
            return halo(vext.at[number], vec_send.at[number], vec_recv.at[number])

        row8_lane = row8 == lax.broadcasted_iota(jnp.int32, (8, ATOMS), 1)

        def reduce_start(number, values):
            rows = by_row([jnp.sum(value, axis=0, keepdims=True) for value in values])
            rows = jnp.sum(rows, axis=1, keepdims=True)
            ar_send[number] = jnp.sum(jnp.where(row8_lane, rows, 0.0), axis=0, keepdims=True)
            copies = []
            for slot, peer in enumerate(flat):
                copies.append(
                    pltpu.make_async_remote_copy(
                        src_ref=ar_send.at[number],
                        dst_ref=ar_flat.at[number, slot],
                        send_sem=flat_send.at[number, slot],
                        recv_sem=flat_recv.at[number, slot],
                        device_id=flat_device(*peer),
                        device_id_type=MESH,
                    )
                )
            for copy in copies:
                copy.start()
            return copies

        def reduce_next(number, copies):
            landed(copies)
            parts = [ar_send[number]] + [ar_flat[number, slot] for slot in range(len(flat))]
            while len(parts) > 1:
                parts = [sum(parts[at : at + 2]) for at in range(0, len(parts), 2)]
            ar_mid[number] = parts[0]
            after = []
            for slot, peer in enumerate(line):
                after.append(
                    pltpu.make_async_remote_copy(
                        src_ref=ar_mid.at[number],
                        dst_ref=ar_line.at[number, slot],
                        send_sem=line_send.at[number, slot],
                        recv_sem=line_recv.at[number, slot],
                        device_id=line_device(*peer),
                        device_id_type=MESH,
                    )
                )
            for copy in after:
                copy.start()
            return after

        def reduce_end(number, copies):
            landed(copies)
            parts = [ar_mid[number]] + [ar_line[number, slot] for slot in range(len(line))]
            while len(parts) > 1:
                parts = [sum(parts[at : at + 2]) for at in range(0, len(parts), 2)]
            total = parts[0]
            return [jnp.broadcast_to(total[:, at : at + 1], (1, ATOMS)) for at in range(8)]

        chi = lookup(kind_own, negativity_table)
        kchi, ksum = products()
        diagonal = lookup(kind_own, hardness_table) + ksum
        ws = -(diagonal * chi + kchi)
        wt = -(diagonal + ksum)
        vec0 = place(0, ws, wt)
        red0 = reduce_start(0, [chi * chi, -chi * ws, ws * ws, -wt, wt * wt, chi])
        apply_own(0)
        lax.fori_loop(0, 2, gather_cell, 0)
        red0b = reduce_next(0, red0)
        apply_near(0, vec0)
        lax.fori_loop(2, cells, gather_cell, 0)
        k2s, k2t = apply_far(0, vec0)
        hws = diagonal * ws + k2s
        hwt = diagonal * wt + k2t
        rr0s, pq0s, qq0s, pq0t, qq0t, chi_sum, _, _ = reduce_end(0, red0b)
        rr0t = jnp.full((1, ATOMS), float(total_atoms), jnp.float32)
        a0s, a0t = rr0s / pq0s, rr0t / pq0t
        b0s = a0s * a0s * qq0s / rr0s - 1.0
        b0t = a0t * a0t * qq0t / rr0t - 1.0
        r1s, r1t = -chi - a0s * ws, -1.0 - a0t * wt
        d1s, d1t = r1s - b0s * chi, r1t - b0t
        hr1s, hr1t = ws - a0s * hws, wt - a0t * hwt
        q1s, q1t = hr1s + b0s * ws, hr1t + b0t * wt
        vec1 = place(1, q1s, q1t)
        red1 = reduce_start(
            1, [r1s * r1s, d1s * q1s, q1s * q1s, d1s, r1t * r1t, d1t * q1t, q1t * q1t, d1t]
        )
        g_here = excess_damping()
        g_copies = halo(gext, g_send, g_recv)
        apply_own(1)
        red1b = reduce_next(1, red1)
        apply_near(1, vec1)
        k3s, k3t = apply_far(1, vec1)
        hq1s = diagonal * q1s + k3s
        hq1t = diagonal * q1t + k3t
        rr1s, pq1s, qq1s, d1s_sum, rr1t, pq1t, qq1t, d1t_sum = reduce_end(1, red1b)
        a1s, a1t = rr1s / pq1s, rr1t / pq1t
        b1s = a1s * a1s * qq1s / rr1s - 1.0
        b1t = a1t * a1t * qq1t / rr1t - 1.0
        r2s, r2t = r1s - a1s * q1s, r1t - a1t * q1t
        d2s, d2t = r2s + b1s * d1s, r2t + b1t * d1t
        q2s = hr1s - a1s * hq1s + b1s * q1s
        q2t = hr1t - a1t * hq1t + b1t * q1t
        red2 = reduce_start(2, [r2s * r2s, d2s * q2s, d2s, r2t * r2t, d2t * q2t, d2t])

        landed(g_copies)

        def gather_damping(c, carry):
            x, y, z = cell_of(c)
            index = jnp.maximum(idxb[c], 0)
            offset = lax.shift_right_logical(index, 7)
            atom = jnp.bitwise_and(index, 127)
            picked = jnp.zeros((8, ATOMS), jnp.float32)
            around = gext.at[pl.ds(x, 3), pl.ds(y, 3), pl.ds(z, 3)]
            for k, (a, b, d) in enumerate(STEPS):
                row = jnp.broadcast_to(around[1 + a, 1 + b, 1 + d, 0:1, :], (8, ATOMS))
                got = jnp.take_along_axis(row, atom, axis=1, mode="promise_in_bounds")
                picked = jnp.where(offset == k, got, picked)
            for s in range(NBOND):
                raws[s, pl.ds(c, 1), :] = raws[s, pl.ds(c, 1), :] * picked[s : s + 1, :]
            return carry

        lax.fori_loop(0, cells, gather_damping, 0)
        red2b = reduce_next(2, red2)

        def spread_out(ref, lead, value):
            for x in range(cx):
                for y in range(cy):
                    at = (x * cy + y) * cz
                    ref[(*lead, x, y)] = value[at : at + cz, :]

        order = []
        for s in range(NBOND):
            order.append(raws[s, 0:cells, :] * g_here)
            spread_out(orders_out, (s,), order[s])
        bend = lookup(kind_own, bend_table)
        rest = lookup(kind_own, cosine_table)
        twist = lookup(kind_own, twist_table)
        vecs = [[bv[f, s, 0:cells, :] for f in range(3)] for s in range(NBOND)]
        radii = [bv[3, s, 0:cells, :] for s in range(NBOND)]
        inv = [lax.rsqrt(dot3(vecs[s], vecs[s]) + 1.0) for s in range(NBOND)]
        force = [[jnp.zeros((cells, ATOMS), jnp.float32) for _ in range(3)] for _ in range(NBOND)]
        for a in range(NBOND):
            for b in range(a + 1, NBOND):
                both = inv[a] * inv[b]
                cosine = dot3(vecs[a], vecs[b]) * both
                pull = -2.0 * bend * (order[a] * order[b]) * (cosine - rest)
                cross_part = pull * both
                own_part = pull * cosine
                pa = own_part * (inv[a] * inv[a])
                pb = own_part * (inv[b] * inv[b])
                for f in range(3):
                    force[a][f] = force[a][f] + (cross_part * vecs[b][f] - pa * vecs[a][f])
                    force[b][f] = force[b][f] + (cross_part * vecs[a][f] - pb * vecs[b][f])

        def choose(options, slot):
            out = options[0]
            for s in range(1, NBOND):
                out = jnp.where(slot == s, options[s], out)
            return out

        for t in range(NTOR):
            first = torc[0, t, 0:cells, :]
            second = torc[1, t, 0:cells, :]
            vj = [choose([vecs[s][f] for s in range(NBOND)], first) for f in range(3)]
            vk = [choose([vecs[s][f] for s in range(NBOND)], second) for f in range(3)]
            weight = choose(order, first) * choose(order, second)
            span = choose(radii, second) + bv[3, NBOND + t, 0:cells, :]
            far = [bv[f, NBOND + t, 0:cells, :] for f in range(3)]
            u = [far[f] - vk[f] for f in range(3)]
            weight = weight * jnp.exp(order_rate * dot3(u, u) / (span * span))
            weight = weight * gb[NBOND + t, 0:cells, :]
            n1 = cross3(vj, vk)
            n2 = cross3(vk, u)
            i1 = lax.rsqrt(dot3(n1, n1) + 1.0)
            i2 = lax.rsqrt(dot3(n2, n2) + 1.0)
            both = i1 * i2
            cosine = dot3(n1, n2) * both
            pull = 2.0 * twist * weight * cosine
            cross_part = pull * both
            own1 = pull * cosine * (i1 * i1)
            own2 = pull * cosine * (i2 * i2)
            p1 = [cross_part * n2[f] - own1 * n1[f] for f in range(3)]
            p2 = [cross_part * n1[f] - own2 * n2[f] for f in range(3)]
            fj = cross3(vk, p1)
            fw = cross3(p2, vk)
            part1 = cross3(p1, vj)
            part2 = cross3(u, p2)
            fk = [part1[f] + part2[f] - fw[f] for f in range(3)]
            for s in range(NBOND):
                for f in range(3):
                    force[s][f] = (
                        force[s][f]
                        + jnp.where(first == s, fj[f], 0.0)
                        + jnp.where(second == s, fk[f], 0.0)
                    )
            for f in range(3):
                spread_out(fforce, (f, t), fw[f])
        for s in range(NBOND):
            for f in range(3):
                spread_out(bforce, (f, s), force[s][f])

        rr2s, pq2s, d2s_sum, rr2t, pq2t, d2t_sum, _, _ = reduce_end(2, red2b)
        a2s, a2t = rr2s / pq2s, rr2t / pq2t
        solve_s = -a0s * chi + a1s * d1s + a2s * d2s
        solve_t = -a0t + a1t * d1t + a2t * d2t
        sum_s = -a0s * chi_sum + a1s * d1s_sum + a2s * d2s_sum
        sum_t = -a0t * rr0t + a1t * d1t_sum + a2t * d2t_sum
        result = charge_unit * (solve_s - (sum_s / sum_t) * solve_t)
        spread_out(charges, (), result)

        for copies in (pos_copies, g_copies, vec0, vec1, red0, red0b, red1, red1b, red2, red2b):
            finish(copies)

    def scratch():
        big = (cx + 2, cy + 2, cz + 2)
        sides = len(SIDES)
        dma = pltpu.SemaphoreType.DMA
        f32 = jnp.float32
        return [
            pltpu.VMEM((3, *block, ATOMS), f32),
            pltpu.VMEM((*block, ATOMS), jnp.int32),
            pltpu.VMEM((NBOND, *block, ATOMS), jnp.int32),
            pltpu.VMEM((2, NTOR, *block, ATOMS), jnp.int32),
            pltpu.VMEM((NTOR, *block, ATOMS), jnp.int32),
            dma((5,)),
            pltpu.VMEM((*big, 4, ATOMS), f32),
            pltpu.VMEM((*big, 2, ATOMS), f32),
            pltpu.VMEM((*big, DEPTH, ATOMS), jnp.bfloat16),
            pltpu.VMEM((cells, ATOMS, DEPTH), jnp.bfloat16),
            pltpu.VMEM((cells, ATOMS, ATOMS), f32),
            pltpu.VMEM((19, ATOMS, ATOMS), f32),
            pltpu.VMEM((19, ATOMS, ATOMS), f32),
            pltpu.VMEM((2, cells, ATOMS, ATOMS), f32),
            pltpu.VMEM((cells, ATOMS // ROWS, 27, ROWS, ATOMS), f32),
            pltpu.VMEM((ATOMS, ATOMS), f32),
            pltpu.VMEM((2, *big, 2, ATOMS), f32),
            pltpu.VMEM((*big, 1, ATOMS), f32),
            pltpu.VMEM((cells, 8, ATOMS), jnp.int32),
            pltpu.VMEM((4, 8, 16, ATOMS), f32),
            pltpu.VMEM((8, 16, ATOMS), f32),
            pltpu.VMEM((16, ATOMS), jnp.int32),
            pltpu.VMEM((2, NTOR, 16, ATOMS), jnp.int32),
            pltpu.VMEM((NBOND, 16, ATOMS), f32),
            pltpu.VMEM((3, 1, ATOMS), f32),
            pltpu.VMEM((3, len(flat), 1, ATOMS), f32),
            pltpu.VMEM((3, 1, ATOMS), f32),
            pltpu.VMEM((3, len(line), 1, ATOMS), f32),
            dma((sides,)), dma((sides,)),
            dma((2, sides)), dma((2, sides)),
            dma((sides,)), dma((sides,)),
            dma((3, len(flat))), dma((3, len(flat))),
            dma((3, len(line))), dma((3, len(line))),
        ]

    return kernel, scratch()


def write_out(*refs):
    sources, targets, sems = refs[:4], refs[4:8], refs[8]
    copies = [
        pltpu.make_async_copy(source, target, sems.at[number])
        for number, (source, target) in enumerate(zip(sources, targets))
    ]
    for copy in copies:
        copy.start()
    for copy in copies:
        copy.wait()


def solution(mesh):
    sizes = (mesh.shape["gx"], mesh.shape["gy"], mesh.shape["gz"])

    def on_device(positions, atom_kinds, bond_partners, torsion_bonds, torsion_far):
        block = positions.shape[1:4]
        total = ATOMS
        for count, size in zip(block, sizes):
            total *= count * size
        kernel, scratch = make_kernel(sizes, block, total)
        f32 = jnp.float32
        whole = pl.BlockSpec(memory_space=pltpu.VMEM)
        shapes = (
                jax.ShapeDtypeStruct((*block, ATOMS), f32),
                jax.ShapeDtypeStruct((NBOND, *block, ATOMS), f32),
                jax.ShapeDtypeStruct((3, NBOND, *block, ATOMS), f32),
                jax.ShapeDtypeStruct((3, NTOR, *block, ATOMS), f32),
            )
        arrays = (positions, atom_kinds, bond_partners, torsion_bonds, torsion_far)
        hbm = pl.BlockSpec(memory_space=pltpu.MemorySpace.HBM)
        results = pl.pallas_call(
            kernel,
            out_shape=shapes,
            in_specs=[hbm] * 5,
            out_specs=(whole,) * 4,
            scratch_shapes=scratch,
            compiler_params=pltpu.CompilerParams(
                collective_id=0, has_side_effects=True, vmem_limit_bytes=48 * 1024 * 1024
            ),
            name="reax_step",
        )(*[pltpu.with_memory_space_constraint(a, pltpu.MemorySpace.HBM) for a in arrays])
        return pl.pallas_call(
            write_out,
            out_shape=shapes,
            in_specs=[whole] * 4,
            out_specs=(hbm,) * 4,
            scratch_shapes=[pltpu.SemaphoreType.DMA((4,))],
            name="write_out",
        )(*[pltpu.with_memory_space_constraint(r, pltpu.MemorySpace.VMEM) for r in results])

    placed = (
        P(None, "gx", "gy", "gz", None),
        P("gx", "gy", "gz", None),
        P(None, "gx", "gy", "gz", None),
        P(None, None, "gx", "gy", "gz", None),
        P(None, "gx", "gy", "gz", None),
    )
    return jax.shard_map(
        on_device,
        mesh=mesh,
        in_specs=placed,
        out_specs=(
            P("gx", "gy", "gz", None),
            P(None, "gx", "gy", "gz", None),
            P(None, None, "gx", "gy", "gz", None),
            P(None, None, "gx", "gy", "gz", None),
        ),
        check_vma=False,
    )
```

```python
import jax
import jax.numpy as jnp
from jax import lax
from jax.experimental import pallas as pl
from jax.experimental.pallas import tpu as pltpu
from jax.sharding import PartitionSpec as P

MESH = pl.DeviceIdType.MESH

ATOMS = 128
NBOND = 4
NTOR = 4
cutoff = 10.0
coulomb = 14.4
order_rate = -0.3
charge_unit = 100.0
shield_table = (0.82, 1.08, 0.75)
negativity_table = (4.7, 8.5, 5.3)
hardness_table = (6.0, 7.2, 7.4)
radius_table = (5.0, 4.0, 3.0)
valence_table = (4.0, 2.0, 1.0)
bend_table = (40.0, 30.0, 10.0)
cosine_table = (-0.3333, -0.25, -0.5)
twist_table = (20.0, 12.0, 6.0)

STEPS = [(a, b, c) for a in (-1, 0, 1) for b in (-1, 0, 1) for c in (-1, 0, 1)]
SIDES = [s for s in STEPS if s != (0, 0, 0)]
ROWS = 128
TAPER_GRID = 2.0**-22
TAPER_42 = round(4.2 / (2 * TAPER_GRID)) * (2 * TAPER_GRID)
TAPER_05 = round(0.05 / TAPER_GRID) * TAPER_GRID
TAPER = (TAPER_42, TAPER_42 - 2.5 + TAPER_05, TAPER_05)
DEPTH = 64


def lookup(kind, table):
    return jnp.where(kind == 0, table[0], jnp.where(kind == 1, table[1], table[2])).astype(jnp.float32)


def send_range(step, size):
    if step > 0:
        return (size, 1)
    if step < 0:
        return (1, 1)
    return (1, size)


def land_range(step, size):
    if step > 0:
        return (0, 1)
    if step < 0:
        return (size + 1, 1)
    return (1, size)


def add3(a, b):
    return [p + q for p, q in zip(a, b)]


def dot3(a, b):
    return a[0] * b[0] + a[1] * b[1] + a[2] * b[2]


def cross3(a, b):
    return [
        a[1] * b[2] - a[2] * b[1],
        a[2] * b[0] - a[0] * b[2],
        a[0] * b[1] - a[1] * b[0],
    ]


def make_kernel(sizes, block, total_atoms):
    nx, ny, nz = sizes
    cx, cy, cz = block
    cells = cx * cy * cz
    cell_list = [(x, y, z) for x in range(cx) for y in range(cy) for z in range(cz)]
    px, pz = 2, nz // 2
    flat = [(i, j) for i in range(px) for j in range(ny) if (i, j) != (0, 0)]
    line = [
        (i, j, k)
        for i in range(nx // px)
        for j in range(nz // pz)
        for k in range(pz)
        if (i, j, k) != (0, 0, 0)
    ]

    def kernel(
        pos_in, kinds_in, bp_in, tb_in, tf_in,
        charges, orders_out, bforce, fforce,
        pos, kinds, bp, tb, tf, in_sems,
        ext, dext, brhs, alhs, colg, square_a, square_b, part_sum, kbuf, ycol, vext, gext, idxb, bv, gb, kindc, torc, raws,
        ar_send, ar_flat, ar_mid, ar_line,
        pos_send, pos_recv, vec_send, vec_recv, g_send, g_recv,
        flat_send, flat_recv, line_send, line_recv,
    ):
        ix = lax.axis_index("gx")
        iy = lax.axis_index("gy")
        iz = lax.axis_index("gz")

        def device(a, b, c):
            return (lax.rem(ix + a + nx, nx), lax.rem(iy + b + ny, ny), lax.rem(iz + c + nz, nz))

        fetches = [
            pltpu.make_async_copy(source, target, in_sems.at[number])
            for number, (source, target) in enumerate(
                ((pos_in, pos), (kinds_in, kinds), (bp_in, bp), (tf_in, tf), (tb_in, tb))
            )
        ]
        for fetch in fetches:
            fetch.start()
        def flat_device(i, j):
            return ((ix // px) * px + lax.rem(lax.rem(ix, px) + i, px), lax.rem(iy + j, ny), iz)

        def line_device(i, j, k):
            return (
                lax.rem(ix // px + i, nx // px) * px + lax.rem(ix, px),
                iy,
                lax.rem(iz // pz + j, nz // pz) * pz + lax.rem(lax.rem(iz, pz) + k, pz),
            )

        greeted = [device(*side) for side in SIDES]
        greeted += [flat_device(*peer) for peer in flat] + [line_device(*peer) for peer in line]
        barrier = pltpu.get_barrier_semaphore()
        for peer in greeted:
            pl.semaphore_signal(barrier, inc=1, device_id=peer, device_id_type=MESH)

        def halo(ref, send, recv):
            copies = []
            for number, (a, b, c) in enumerate(SIDES):
                sx, sy, sz = send_range(a, cx), send_range(b, cy), send_range(c, cz)
                lx, ly, lz = land_range(a, cx), land_range(b, cy), land_range(c, cz)
                copies.append(
                    pltpu.make_async_remote_copy(
                        src_ref=ref.at[pl.ds(*sx), pl.ds(*sy), pl.ds(*sz)],
                        dst_ref=ref.at[pl.ds(*lx), pl.ds(*ly), pl.ds(*lz)],
                        send_sem=send.at[number],
                        recv_sem=recv.at[number],
                        device_id=device(a, b, c),
                        device_id_type=MESH,
                    )
                )
            for copy, side in zip(copies, SIDES):
                if side[2] != 0:
                    copy.start()
            for copy, side in zip(copies, SIDES):
                if side[2] == 0:
                    copy.start()
            return copies

        def landed(copies):
            for copy in copies:
                copy.wait_recv()

        def finish(copies):
            for copy in copies:
                copy.wait_send()

        fetches[0].wait()
        fetches[1].wait()
        for x, y, z in cell_list:
            for f in range(3):
                ext[x + 1, y + 1, z + 1, f : f + 1, :] = pos[f, x, y, z : z + 1, :]
            ext[x + 1, y + 1, z + 1, 3:4, :] = kinds[x, y, z : z + 1, :].astype(jnp.float32)
        for x in range(cx):
            for y in range(cy):
                at = (x * cy + y) * cz
                kindc[at : at + cz, :] = kinds[x, y]
        kind_own = kindc[0:cells, :]

        def cell_of(c):
            return (c // (cy * cz), lax.rem(c // cz, cy), lax.rem(c, cz))

        shield_root = [float((cutoff * g) ** -1.5) for g in shield_table]
        row8 = lax.broadcasted_iota(jnp.int32, (8, ATOMS), 0)
        ones3 = jnp.where(row8 < 3, 1.0, 0.0)

        def narrow(value):
            return value.astype(jnp.bfloat16).astype(jnp.float32)

        def by_row(values):
            out = jnp.zeros((8, ATOMS), jnp.float32)
            for at, value in enumerate(values):
                if value is not None:
                    out = jnp.where(row8 == at, value, out)
            return out

        def derive(x, y, z, number):
            middle = (x - 0.5 * (cx + 2), y - 0.5 * (cy + 2), z - 0.5 * (cz + 2))
            place_at = by_row(
                [
                    ext[x, y, z, f : f + 1, :] * (1.0 / cutoff) + jnp.float32(middle[f])
                    for f in range(3)
                ]
            )
            grid = jnp.round(place_at * 64.0) * (1.0 / 64.0)
            rest = place_at - grid
            mid = narrow(rest)
            low = rest - mid
            grid_sq = jnp.sum(grid * grid, axis=0, keepdims=True)
            rest_sq = jnp.sum(rest * (2.0 * grid + rest), axis=0, keepdims=True)
            grid_1 = jnp.round(grid_sq * 16.0) * (1.0 / 16.0)
            grid_2 = grid_sq - grid_1
            rest_1 = narrow(rest_sq)
            rest_2 = narrow(rest_sq - rest_1)
            rest_3 = (rest_sq - rest_1) - rest_2
            heads = by_row([grid_1, grid_2, 1.0, 1.0, rest_1, rest_2, rest_3])
            tile = jnp.concatenate([grid, heads, ones3, mid, low, grid, grid, mid], axis=0)
            brhs[x, y, z] = tile.astype(jnp.bfloat16)
            kind = ext[x, y, z, 3:4, :]
            dext[x, y, z, 0:1, :] = lookup(kind, shield_root)
            dext[x, y, z, 1:2, :] = lookup(kind, negativity_table)
            if number is not None:
                heads = by_row([1.0, 1.0, grid_1, grid_2, 1.0, 1.0, 1.0])
                tails = by_row([rest_1, rest_2, rest_3])
                left = jnp.concatenate(
                    [
                        -2.0 * grid, heads, tails, -2.0 * grid,
                        -2.0 * grid, -2.0 * mid, -2.0 * low, -2.0 * mid,
                    ],
                    axis=0,
                )
                alhs[number] = jnp.transpose(left).astype(jnp.bfloat16)

        def derive_own(n, carry):
            x = n // cy
            y = lax.rem(n, cy)
            for z in range(cz):
                derive(x + 1, y + 1, z + 1, (x * cy + y) * cz + z)
            return carry

        lax.fori_loop(0, cx * cy, derive_own, 0)

        ycol[...] = jnp.zeros((ATOMS, ATOMS), jnp.float32)
        ycol[0:cells, :] = lookup(kind_own, shield_root)
        flipped = jnp.transpose(ycol[...])
        for number in range(cells):
            colg[number] = jnp.broadcast_to(flipped[:, number : number + 1], (ATOMS, ATOMS))
        ycol[...] = jnp.zeros((ATOMS, ATOMS), jnp.float32)

        def tiles_of(y):
            every = [
                (i, j, k) for j in (y, y + 1, y + 2) for i in (1, 2, None) for k in (1, 2, None)
            ]
            own = [t for t in every if t[0] and t[2] and 1 <= t[1] <= cy]
            far = [t for t in every if t[2] is None]
            return own, [t for t in every if t not in own + far], far

        row_of = lax.broadcasted_iota(jnp.int32, (ROWS, ATOMS), 0)
        lane_of = lax.broadcasted_iota(jnp.int32, (ROWS, ATOMS), 1)

        def keep_sums(at, c, first, second):
            one = jnp.sum(first, axis=1, keepdims=True)
            two = jnp.sum(second, axis=1, keepdims=True)
            ycol[pl.ds(at, ROWS), :] = ycol[pl.ds(at, ROWS), :] + jnp.where(
                lane_of == c, one, jnp.where(lane_of == c + 16, two, 0.0)
            )

        def coupling_part(y, side):
            tiles = tile_sets[y][side]
            base = sum(len(group) for group in tile_sets[y][:side])

            def at_cell(xz):
                x, z = xz // cz, xz % cz
                return x, z, (x * cy + y) * cz + z

            def neighbour(x, z, tile):
                i, j, k = tile
                return ((cx + 1) * x if i is None else i, j, (cz + 1) * z if k is None else k)

            def squares(xz, target):
                x, z, c = at_cell(xz)
                for slot, tile in enumerate(tiles):
                    target[slot] = jnp.dot(
                        alhs[c], brhs[neighbour(x, z, tile)], preferred_element_type=jnp.float32
                    )

            def entries(xz, source):
                x, z, c = at_cell(xz)
                own_g = colg[c]
                if side > 0:
                    sum_one, sum_chi = part_sum[0, c], part_sum[1, c]
                else:
                    sum_one = jnp.zeros((ROWS, ATOMS), jnp.float32)
                    sum_chi = jnp.zeros((ROWS, ATOMS), jnp.float32)
                for slot, tile in enumerate(tiles):
                    i, j, k = tile
                    near = neighbour(x, z, tile)
                    near_g = dext[(*near, slice(0, 1), slice(None))]
                    near_chi = dext[(*near, slice(1, 2), slice(None))]
                    q = jnp.minimum(jnp.maximum(source[slot], 1e-30), 1.0)
                    u = q * lax.rsqrt(q)
                    inv = jnp.exp2(lax.log2(u * q + own_g * near_g) * (-1.0 / 3.0))
                    inner_part = (u - 3.5) * q + (u * TAPER[0] - TAPER[1])
                    value = (inner_part * (q * q) + TAPER[2]) * inv
                    if near == (x + 1, y + 1, z + 1):
                        value = jnp.where(row_of == lane_of, 0.0, value)
                    kbuf[c, 0, base + slot] = value
                    sum_one = sum_one + value
                    sum_chi = sum_chi + value * near_chi
                if side == 2:
                    keep_sums(0, c, sum_chi, sum_one)
                else:
                    part_sum[0, c] = sum_one
                    part_sum[1, c] = sum_chi

            buffers = (square_a, square_b)
            squares(0, square_a)
            for xz in range(cx * cz):
                if xz + 1 < cx * cz:
                    squares(xz + 1, buffers[(xz + 1) % 2])
                entries(xz, buffers[xz % 2])

        tile_sets = [tiles_of(y) for y in range(cy)]
        coupling_part(0, 0)
        pl.semaphore_wait(barrier, len(greeted))
        pos_copies = halo(ext, pos_send, pos_recv)
        for y in range(1, cy):
            coupling_part(y, 0)

        for fetch in fetches[2:]:
            fetch.wait()
        for x in range(cx):
            for y in range(cy):
                at = (x * cy + y) * cz
                for s in range(NTOR):
                    torc[0, s, at : at + cz, :] = tb[0, s, x, y]
                    torc[1, s, at : at + cz, :] = tb[1, s, x, y]
        for number, (x, y, z) in enumerate(cell_list):
            for s in range(NBOND):
                idxb[number, s : s + 1, :] = bp[s, x, y, z : z + 1, :]
                idxb[number, NBOND + s : NBOND + s + 1, :] = tf[s, x, y, z : z + 1, :]

        def derive_x(n, carry):
            for z in range(1, cz + 1):
                derive((cx + 1) * (n // (cy + 2)), lax.rem(n, cy + 2), z, None)
            return carry

        def derive_y(n, carry):
            for z in range(1, cz + 1):
                derive(n // 2 + 1, (cy + 1) * lax.rem(n, 2), z, None)
            return carry

        def derive_z(n, carry):
            for z in (0, cz + 1):
                derive(n // (cy + 2), lax.rem(n, cy + 2), z, None)
            return carry

        landed([c for c, side in zip(pos_copies, SIDES) if side[2] == 0])
        lax.fori_loop(0, 2 * (cy + 2), derive_x, 0)
        lax.fori_loop(0, 2 * cx, derive_y, 0)
        for y in range(cy):
            coupling_part(y, 1)
        landed([c for c, side in zip(pos_copies, SIDES) if side[2] != 0])
        lax.fori_loop(0, (cx + 2) * (cy + 2), derive_z, 0)
        for y in range(cy):
            coupling_part(y, 2)

        def gather_cell(c, carry):
            x, y, z = cell_of(c)
            index = jnp.maximum(idxb[c], 0)
            offset = lax.shift_right_logical(index, 7)
            atom = jnp.bitwise_and(index, 127)
            picked = [jnp.zeros((8, ATOMS), jnp.float32) for _ in range(4)]
            around = ext.at[pl.ds(x, 3), pl.ds(y, 3), pl.ds(z, 3)]
            for k, (a, b, d) in enumerate(STEPS):
                here = offset == k
                for f in range(4):
                    row = jnp.broadcast_to(
                        around[1 + a, 1 + b, 1 + d, f : f + 1, :], (8, ATOMS)
                    )
                    got = jnp.take_along_axis(row, atom, axis=1, mode="promise_in_bounds")
                    picked[f] = jnp.where(here, got, picked[f])
            sx = (offset >= 9).astype(jnp.int32) + (offset >= 18).astype(jnp.int32)
            rest = offset - 9 * sx
            sy = (rest >= 3).astype(jnp.int32) + (rest >= 6).astype(jnp.int32)
            sz = rest - 3 * sy
            for f, step in enumerate((sx, sy, sz)):
                shift = (step - 1).astype(jnp.float32) * cutoff
                own = ext[x + 1, y + 1, z + 1, f : f + 1, :]
                vec = picked[f] + shift - own
                for s in range(8):
                    bv[f, s, pl.ds(c, 1), :] = vec[s : s + 1, :]
            radius = lookup(picked[3], radius_table)
            for s in range(8):
                bv[3, s, pl.ds(c, 1), :] = radius[s : s + 1, :]
                gb[s, pl.ds(c, 1), :] = jnp.where(idxb[c, s : s + 1, :] >= 0, 1.0, 0.0)
            return carry

        def excess_damping():
            radius_own = lookup(kind_own, radius_table)
            excess = -lookup(kind_own, valence_table)
            for s in range(NBOND):
                vec = [bv[f, s, 0:cells, :] for f in range(3)]
                span = radius_own + bv[3, s, 0:cells, :]
                raw = gb[s, 0:cells, :] * jnp.exp(order_rate * dot3(vec, vec) / (span * span))
                raws[s, 0:cells, :] = raw
                excess = excess + raw
            g_here = 2.0 / (1.0 + jnp.exp(excess))
            for number, (x, y, z) in enumerate(cell_list):
                gext[x + 1, y + 1, z + 1, 0:1, :] = g_here[number : number + 1, :]
            return g_here

        scale = 20.0 * coulomb / cutoff

        def products():
            turned = jnp.transpose(ycol[...])
            return (scale * turned[0:cells, :], scale * turned[16 : 16 + cells, :])

        def apply_part(number, side):
            for y in range(cy):
                tiles = tile_sets[y][side]
                base = sum(len(group) for group in tile_sets[y][:side])

                def cell(xz, carry):
                    x = xz // cz
                    z = lax.rem(xz, cz)
                    c = (x * cy + y) * cz + z

                    def rows(r, inner):
                        at = pl.multiple_of(r * ROWS, ROWS)
                        first = jnp.zeros((ROWS, ATOMS), jnp.float32)
                        second = jnp.zeros((ROWS, ATOMS), jnp.float32)
                        for slot, (i, j, k) in enumerate(tiles):
                            ex = (cx + 1) * x if i is None else i
                            ez = (cz + 1) * z if k is None else k
                            value = kbuf[c, r, base + slot]
                            first = first + value * vext[number, ex, j, ez, 0:1, :]
                            second = second + value * vext[number, ex, j, ez, 1:2, :]
                        keep_sums(at, c, first, second)
                        return inner

                    return lax.fori_loop(0, ATOMS // ROWS, rows, carry)

                lax.fori_loop(0, cx * cz, cell, 0)

        def apply_own(number):
            ycol[...] = jnp.zeros((ATOMS, ATOMS), jnp.float32)
            apply_part(number, 0)

        def apply_near(number, copies):
            landed([c for c, side in zip(copies, SIDES) if side[2] == 0])
            apply_part(number, 1)

        def apply_far(number, copies):
            landed([c for c, side in zip(copies, SIDES) if side[2] != 0])
            apply_part(number, 2)
            return products()

        def place(number, first, second):
            for at, (x, y, z) in enumerate(cell_list):
                vext[number, x + 1, y + 1, z + 1, 0:1, :] = first[at : at + 1, :]
                vext[number, x + 1, y + 1, z + 1, 1:2, :] = second[at : at + 1, :]
            return halo(vext.at[number], vec_send.at[number], vec_recv.at[number])

        row8_lane = row8 == lax.broadcasted_iota(jnp.int32, (8, ATOMS), 1)

        def reduce_start(number, values):
            rows = by_row([jnp.sum(value, axis=0, keepdims=True) for value in values])
            rows = jnp.sum(rows, axis=1, keepdims=True)
            ar_send[number] = jnp.sum(jnp.where(row8_lane, rows, 0.0), axis=0, keepdims=True)
            copies = []
            for slot, peer in enumerate(flat):
                copies.append(
                    pltpu.make_async_remote_copy(
                        src_ref=ar_send.at[number],
                        dst_ref=ar_flat.at[number, slot],
                        send_sem=flat_send.at[number, slot],
                        recv_sem=flat_recv.at[number, slot],
                        device_id=flat_device(*peer),
                        device_id_type=MESH,
                    )
                )
            for copy in copies:
                copy.start()
            return copies

        def reduce_next(number, copies):
            landed(copies)
            parts = [ar_send[number]] + [ar_flat[number, slot] for slot in range(len(flat))]
            while len(parts) > 1:
                parts = [sum(parts[at : at + 2]) for at in range(0, len(parts), 2)]
            ar_mid[number] = parts[0]
            after = []
            for slot, peer in enumerate(line):
                after.append(
                    pltpu.make_async_remote_copy(
                        src_ref=ar_mid.at[number],
                        dst_ref=ar_line.at[number, slot],
                        send_sem=line_send.at[number, slot],
                        recv_sem=line_recv.at[number, slot],
                        device_id=line_device(*peer),
                        device_id_type=MESH,
                    )
                )
            for copy in after:
                copy.start()
            return after

        def reduce_end(number, copies):
            landed(copies)
            parts = [ar_mid[number]] + [ar_line[number, slot] for slot in range(len(line))]
            while len(parts) > 1:
                parts = [sum(parts[at : at + 2]) for at in range(0, len(parts), 2)]
            total = parts[0]
            return [jnp.broadcast_to(total[:, at : at + 1], (1, ATOMS)) for at in range(8)]

        chi = lookup(kind_own, negativity_table)
        kchi, ksum = products()
        diagonal = lookup(kind_own, hardness_table) + ksum
        ws = -(diagonal * chi + kchi)
        wt = -(diagonal + ksum)
        vec0 = place(0, ws, wt)
        red0 = reduce_start(0, [chi * chi, -chi * ws, ws * ws, -wt, wt * wt, chi])
        apply_own(0)
        lax.fori_loop(0, 2, gather_cell, 0)
        red0b = reduce_next(0, red0)
        apply_near(0, vec0)
        lax.fori_loop(2, cells, gather_cell, 0)
        k2s, k2t = apply_far(0, vec0)
        hws = diagonal * ws + k2s
        hwt = diagonal * wt + k2t
        rr0s, pq0s, qq0s, pq0t, qq0t, chi_sum, _, _ = reduce_end(0, red0b)
        rr0t = jnp.full((1, ATOMS), float(total_atoms), jnp.float32)
        a0s, a0t = rr0s / pq0s, rr0t / pq0t
        b0s = a0s * a0s * qq0s / rr0s - 1.0
        b0t = a0t * a0t * qq0t / rr0t - 1.0
        r1s, r1t = -chi - a0s * ws, -1.0 - a0t * wt
        d1s, d1t = r1s - b0s * chi, r1t - b0t
        hr1s, hr1t = ws - a0s * hws, wt - a0t * hwt
        q1s, q1t = hr1s + b0s * ws, hr1t + b0t * wt
        vec1 = place(1, q1s, q1t)
        red1 = reduce_start(
            1, [r1s * r1s, d1s * q1s, q1s * q1s, d1s, r1t * r1t, d1t * q1t, q1t * q1t, d1t]
        )
        g_here = excess_damping()
        g_copies = halo(gext, g_send, g_recv)
        apply_own(1)
        red1b = reduce_next(1, red1)
        apply_near(1, vec1)
        k3s, k3t = apply_far(1, vec1)
        hq1s = diagonal * q1s + k3s
        hq1t = diagonal * q1t + k3t
        rr1s, pq1s, qq1s, d1s_sum, rr1t, pq1t, qq1t, d1t_sum = reduce_end(1, red1b)
        a1s, a1t = rr1s / pq1s, rr1t / pq1t
        b1s = a1s * a1s * qq1s / rr1s - 1.0
        b1t = a1t * a1t * qq1t / rr1t - 1.0
        r2s, r2t = r1s - a1s * q1s, r1t - a1t * q1t
        d2s, d2t = r2s + b1s * d1s, r2t + b1t * d1t
        q2s = hr1s - a1s * hq1s + b1s * q1s
        q2t = hr1t - a1t * hq1t + b1t * q1t
        red2 = reduce_start(2, [r2s * r2s, d2s * q2s, d2s, r2t * r2t, d2t * q2t, d2t])

        landed(g_copies)

        def gather_damping(c, carry):
            x, y, z = cell_of(c)
            index = jnp.maximum(idxb[c], 0)
            offset = lax.shift_right_logical(index, 7)
            atom = jnp.bitwise_and(index, 127)
            picked = jnp.zeros((8, ATOMS), jnp.float32)
            around = gext.at[pl.ds(x, 3), pl.ds(y, 3), pl.ds(z, 3)]
            for k, (a, b, d) in enumerate(STEPS):
                row = jnp.broadcast_to(around[1 + a, 1 + b, 1 + d, 0:1, :], (8, ATOMS))
                got = jnp.take_along_axis(row, atom, axis=1, mode="promise_in_bounds")
                picked = jnp.where(offset == k, got, picked)
            for s in range(NBOND):
                raws[s, pl.ds(c, 1), :] = raws[s, pl.ds(c, 1), :] * picked[s : s + 1, :]
            return carry

        lax.fori_loop(0, cells, gather_damping, 0)
        red2b = reduce_next(2, red2)

        def spread_out(ref, lead, value):
            for x in range(cx):
                for y in range(cy):
                    at = (x * cy + y) * cz
                    ref[(*lead, x, y)] = value[at : at + cz, :]

        order = []
        for s in range(NBOND):
            order.append(raws[s, 0:cells, :] * g_here)
            spread_out(orders_out, (s,), order[s])
        bend = lookup(kind_own, bend_table)
        rest = lookup(kind_own, cosine_table)
        twist = lookup(kind_own, twist_table)
        vecs = [[bv[f, s, 0:cells, :] for f in range(3)] for s in range(NBOND)]
        radii = [bv[3, s, 0:cells, :] for s in range(NBOND)]
        inv = [lax.rsqrt(dot3(vecs[s], vecs[s]) + 1.0) for s in range(NBOND)]
        force = [[jnp.zeros((cells, ATOMS), jnp.float32) for _ in range(3)] for _ in range(NBOND)]
        for a in range(NBOND):
            for b in range(a + 1, NBOND):
                both = inv[a] * inv[b]
                cosine = dot3(vecs[a], vecs[b]) * both
                pull = -2.0 * bend * (order[a] * order[b]) * (cosine - rest)
                cross_part = pull * both
                own_part = pull * cosine
                pa = own_part * (inv[a] * inv[a])
                pb = own_part * (inv[b] * inv[b])
                for f in range(3):
                    force[a][f] = force[a][f] + (cross_part * vecs[b][f] - pa * vecs[a][f])
                    force[b][f] = force[b][f] + (cross_part * vecs[a][f] - pb * vecs[b][f])

        def choose(options, slot):
            out = options[0]
            for s in range(1, NBOND):
                out = jnp.where(slot == s, options[s], out)
            return out

        for t in range(NTOR):
            first = torc[0, t, 0:cells, :]
            second = torc[1, t, 0:cells, :]
            vj = [choose([vecs[s][f] for s in range(NBOND)], first) for f in range(3)]
            vk = [choose([vecs[s][f] for s in range(NBOND)], second) for f in range(3)]
            weight = choose(order, first) * choose(order, second)
            span = choose(radii, second) + bv[3, NBOND + t, 0:cells, :]
            far = [bv[f, NBOND + t, 0:cells, :] for f in range(3)]
            u = [far[f] - vk[f] for f in range(3)]
            weight = weight * jnp.exp(order_rate * dot3(u, u) / (span * span))
            weight = weight * gb[NBOND + t, 0:cells, :]
            n1 = cross3(vj, vk)
            n2 = cross3(vk, u)
            i1 = lax.rsqrt(dot3(n1, n1) + 1.0)
            i2 = lax.rsqrt(dot3(n2, n2) + 1.0)
            both = i1 * i2
            cosine = dot3(n1, n2) * both
            pull = 2.0 * twist * weight * cosine
            cross_part = pull * both
            own1 = pull * cosine * (i1 * i1)
            own2 = pull * cosine * (i2 * i2)
            p1 = [cross_part * n2[f] - own1 * n1[f] for f in range(3)]
            p2 = [cross_part * n1[f] - own2 * n2[f] for f in range(3)]
            fj = cross3(vk, p1)
            fw = cross3(p2, vk)
            part1 = cross3(p1, vj)
            part2 = cross3(u, p2)
            fk = [part1[f] + part2[f] - fw[f] for f in range(3)]
            for s in range(NBOND):
                for f in range(3):
                    force[s][f] = (
                        force[s][f]
                        + jnp.where(first == s, fj[f], 0.0)
                        + jnp.where(second == s, fk[f], 0.0)
                    )
            for f in range(3):
                spread_out(fforce, (f, t), fw[f])
        for s in range(NBOND):
            for f in range(3):
                spread_out(bforce, (f, s), force[s][f])

        rr2s, pq2s, d2s_sum, rr2t, pq2t, d2t_sum, _, _ = reduce_end(2, red2b)
        a2s, a2t = rr2s / pq2s, rr2t / pq2t
        solve_s = -a0s * chi + a1s * d1s + a2s * d2s
        solve_t = -a0t + a1t * d1t + a2t * d2t
        sum_s = -a0s * chi_sum + a1s * d1s_sum + a2s * d2s_sum
        sum_t = -a0t * rr0t + a1t * d1t_sum + a2t * d2t_sum
        result = charge_unit * (solve_s - (sum_s / sum_t) * solve_t)
        spread_out(charges, (), result)

        for copies in (pos_copies, g_copies, vec0, vec1, red0, red0b, red1, red1b, red2, red2b):
            finish(copies)

    def scratch():
        big = (cx + 2, cy + 2, cz + 2)
        sides = len(SIDES)
        dma = pltpu.SemaphoreType.DMA
        f32 = jnp.float32
        return [
            pltpu.VMEM((3, *block, ATOMS), f32),
            pltpu.VMEM((*block, ATOMS), jnp.int32),
            pltpu.VMEM((NBOND, *block, ATOMS), jnp.int32),
            pltpu.VMEM((2, NTOR, *block, ATOMS), jnp.int32),
            pltpu.VMEM((NTOR, *block, ATOMS), jnp.int32),
            dma((5,)),
            pltpu.VMEM((*big, 4, ATOMS), f32),
            pltpu.VMEM((*big, 2, ATOMS), f32),
            pltpu.VMEM((*big, DEPTH, ATOMS), jnp.bfloat16),
            pltpu.VMEM((cells, ATOMS, DEPTH), jnp.bfloat16),
            pltpu.VMEM((cells, ATOMS, ATOMS), f32),
            pltpu.VMEM((19, ATOMS, ATOMS), f32),
            pltpu.VMEM((19, ATOMS, ATOMS), f32),
            pltpu.VMEM((2, cells, ATOMS, ATOMS), f32),
            pltpu.VMEM((cells, ATOMS // ROWS, 27, ROWS, ATOMS), f32),
            pltpu.VMEM((ATOMS, ATOMS), f32),
            pltpu.VMEM((2, *big, 2, ATOMS), f32),
            pltpu.VMEM((*big, 1, ATOMS), f32),
            pltpu.VMEM((cells, 8, ATOMS), jnp.int32),
            pltpu.VMEM((4, 8, 16, ATOMS), f32),
            pltpu.VMEM((8, 16, ATOMS), f32),
            pltpu.VMEM((16, ATOMS), jnp.int32),
            pltpu.VMEM((2, NTOR, 16, ATOMS), jnp.int32),
            pltpu.VMEM((NBOND, 16, ATOMS), f32),
            pltpu.VMEM((3, 1, ATOMS), f32),
            pltpu.VMEM((3, len(flat), 1, ATOMS), f32),
            pltpu.VMEM((3, 1, ATOMS), f32),
            pltpu.VMEM((3, len(line), 1, ATOMS), f32),
            dma((sides,)), dma((sides,)),
            dma((2, sides)), dma((2, sides)),
            dma((sides,)), dma((sides,)),
            dma((3, len(flat))), dma((3, len(flat))),
            dma((3, len(line))), dma((3, len(line))),
        ]

    return kernel, scratch()


def write_out(*refs):
    sources, targets, sems = refs[:4], refs[4:8], refs[8]
    copies = [
        pltpu.make_async_copy(source, target, sems.at[number])
        for number, (source, target) in enumerate(zip(sources, targets))
    ]
    for copy in copies:
        copy.start()
    for copy in copies:
        copy.wait()


def solution(mesh):
    sizes = (mesh.shape["gx"], mesh.shape["gy"], mesh.shape["gz"])

    def on_device(positions, atom_kinds, bond_partners, torsion_bonds, torsion_far):
        block = positions.shape[1:4]
        total = ATOMS
        for count, size in zip(block, sizes):
            total *= count * size
        kernel, scratch = make_kernel(sizes, block, total)
        f32 = jnp.float32
        whole = pl.BlockSpec(memory_space=pltpu.VMEM)
        shapes = (
                jax.ShapeDtypeStruct((*block, ATOMS), f32),
                jax.ShapeDtypeStruct((NBOND, *block, ATOMS), f32),
                jax.ShapeDtypeStruct((3, NBOND, *block, ATOMS), f32),
                jax.ShapeDtypeStruct((3, NTOR, *block, ATOMS), f32),
            )
        arrays = (positions, atom_kinds, bond_partners, torsion_bonds, torsion_far)
        hbm = pl.BlockSpec(memory_space=pltpu.MemorySpace.HBM)
        results = pl.pallas_call(
            kernel,
            out_shape=shapes,
            in_specs=[hbm] * 5,
            out_specs=(whole,) * 4,
            scratch_shapes=scratch,
            compiler_params=pltpu.CompilerParams(
                collective_id=0, has_side_effects=True, vmem_limit_bytes=48 * 1024 * 1024
            ),
            name="reax_step",
        )(*[pltpu.with_memory_space_constraint(a, pltpu.MemorySpace.HBM) for a in arrays])
        return pl.pallas_call(
            write_out,
            out_shape=shapes,
            in_specs=[whole] * 4,
            out_specs=(hbm,) * 4,
            scratch_shapes=[pltpu.SemaphoreType.DMA((4,))],
            name="write_out",
        )(*[pltpu.with_memory_space_constraint(r, pltpu.MemorySpace.VMEM) for r in results])

    placed = (
        P(None, "gx", "gy", "gz", None),
        P("gx", "gy", "gz", None),
        P(None, "gx", "gy", "gz", None),
        P(None, None, "gx", "gy", "gz", None),
        P(None, "gx", "gy", "gz", None),
    )
    return jax.shard_map(
        on_device,
        mesh=mesh,
        in_specs=placed,
        out_specs=(
            P("gx", "gy", "gz", None),
            P(None, "gx", "gy", "gz", None),
            P(None, None, "gx", "gy", "gz", None),
            P(None, None, "gx", "gy", "gz", None),
        ),
        check_vma=False,
    )
```
